128 devices in a mesh: space: 16 (over z, x), bins: 8 (over y, core).
Axes of the slice: x: 4, y: 4, z: 4, core: 2. Of those that a mesh axis runs over, the one named last changes fastest.
Arguments:
- spectrum: bfloat16 [1152, 384, 256], P('bins', 'space'), may hold values from 0.099609375 to 2
- group_speed: float32 [2, 1152], P(None, 'bins'), may hold values from -0.3 to 0.3
- stokes_kernel: bfloat16 [1152, 128], P('bins'), may hold values from -0.1875 to 0.1875
- pair_bins: int32 [3, 4608], replicated, may hold values from 0 to 1151
- pair_coef: float32 [4608], replicated, may hold values from -3 to 3
- currents: float32 [256, 384, 128], P(('space', 'bins')), may hold values from -6 to 6
- col_map: int32 [128], replicated, may hold values from 0 to 127, each once
- wave_wet: int32 [384, 256], P('space'), may hold values 0 or 1
- ocean_wet: int32 [256, 384], P(('space', 'bins')), may hold values 0 or 1
Outputs:
- new_spectrum: bfloat16 [1152, 384, 256], P(None, ('space', 'bins'))
- new_currents: float32 [256, 384, 128], P(('space', 'bins'))
The draws below stay inside these ranges and needn't reach their ends.
All inputs are finite; a program needn't handle non-finite values. No bound on the sum of `wave_wet` or of `ocean_wet` on one device may be relied on, other than what follows from the above.
Results may differ from the reference program's by a relative error of at most 0.0052.
Values may be sent and summed in bfloat16 or wider, within the bound.
No kernel may reach another device: no remote copies, remote signals or barrier semaphores. Data moves between devices by JAX's collectives and lax.ppermute only.
A program may use at most 64 MiB of HBM per device.

```python
import math
import jax
import jax.numpy as jnp
from jax import lax

NBINS = 1152
LEV = 64
NPAIRS = 4608
OCOLS = 2
NX = 384
GY = 256
OGROUPS = 128


def plant(array, stream_key, low, largest):
    index_at = [jax.random.randint(jax.random.fold_in(stream_key, axis), (), 0, length) for axis, length in enumerate(array.shape)]
    main_axis = array.shape.index(max(array.shape))
    neighbour = index_at[:main_axis] + [(index_at[main_axis] + 1) % array.shape[main_axis]] + index_at[main_axis + 1:]
    return array.at[tuple(index_at)].set(low).at[tuple(neighbour)].set(largest)


def levels(rng, extent, cuts, least, high):
    factor_of = 1.0
    for dim, shards_of in cuts:
        steps = jax.random.uniform(jax.random.fold_in(jax.random.fold_in(rng, 6), dim), (shards_of,), jnp.float32, least / len(cuts), high / len(cuts))
        factor_of = factor_of * jnp.repeat(jnp.exp(steps), extent[dim] // shards_of).reshape((-1,) + (1,) * (len(extent) - 1 - dim))
    return factor_of


def noise(rng, extent, width, bound, cuts=(), kind=jnp.bfloat16):
    gain = levels(rng, extent, cuts, -0.22, 0.18) if cuts else 1.0
    values = jax.random.normal(rng, extent, jnp.float32) * width * gain
    return jnp.minimum(jnp.maximum(values, -bound), bound).astype(kind)


def setup_inputs(seed: int = 0) -> dict:
    key_list = jax.random.split(jax.random.key(seed), 10)
    return {
        "spectrum": jnp.clip(jnp.exp(math.log(2.0) - 2.9996462 * jax.random.uniform(key_list[0], (NBINS, NX, GY), jnp.float32) ** levels(key_list[0], (NBINS, NX, GY), ((0, 8), (1, 16)), -0.2, 0.2)), 0.099609375, 2.0).astype(jnp.bfloat16),
        "group_speed": jnp.clip(jax.random.uniform(key_list[1], (2, NBINS), jnp.float32, -0.3, 0.3) * levels(key_list[1], (2, NBINS), ((1, 8),), -0.4, 0.0), -0.3, 0.3),
        "stokes_kernel": noise(key_list[2], (NBINS, 2 * LEV), NBINS ** -0.5, 0.1875, ((0, 8),)),
        "pair_bins": plant(jax.random.randint(key_list[3], (3, NPAIRS), 0, NBINS), jax.random.fold_in(key_list[3], 1), 0, NBINS - 1).astype(jnp.int32),
        "pair_coef": noise(key_list[4], (NPAIRS,), 0.5, 3.0, (), jnp.float32),
        "currents": noise(key_list[5], (GY, NX, 2 * LEV), 1.0, 6.0, ((0, 128),), jnp.float32),
        "col_map": jax.random.permutation(key_list[6], OGROUPS).astype(jnp.int32),
        "wave_wet": plant((jax.random.randint(key_list[7], (NX, GY), 0, 5) < 4).astype(jnp.int32), jax.random.fold_in(key_list[7], 1), 0, 1),
        "ocean_wet": plant((jax.random.randint(key_list[8], (GY, NX), 0, 5) < 4).astype(jnp.int32), jax.random.fold_in(key_list[8], 1), 0, 1),
    }


DT_OCEAN = 0.5
CORIOLIS = 0.8
MIXING = 0.4
CURRENT_SCALE = 0.15
DT_SOURCE = 0.5


def levels_laplacian(field):
    upper = jnp.concatenate([field[..., :1], field[..., :-1]], axis=-1)
    lower = jnp.concatenate([field[..., 1:], field[..., -1:]], axis=-1)
    return upper + lower - 2.0 * field


def ocean_step(currents, drift, wet):
    east = currents[..., :LEV]
    north = currents[..., LEV:]
    east_drift = drift[..., :LEV]
    north_drift = drift[..., LEV:]
    new_east = east + DT_OCEAN * (CORIOLIS * (north + north_drift) + MIXING * levels_laplacian(east))
    new_north = north + DT_OCEAN * (-CORIOLIS * (east + east_drift) + MIXING * levels_laplacian(north))
    return wet[..., None].astype(jnp.float32) * jnp.concatenate([new_east, new_north], axis=-1)


def advect_bin(energy, speed_x, speed_y, cur, wet):
    energy = energy.astype(jnp.float32)
    cx = speed_x + cur[0]
    cy = speed_y + cur[1]
    plus_x = jnp.maximum(cx, 0.0) * energy
    minus_x = jnp.minimum(cx, 0.0) * energy
    plus_y = jnp.maximum(cy, 0.0) * energy
    minus_y = jnp.minimum(cy, 0.0) * energy
    plus_x_prev = jnp.pad(plus_x[:-1, :], ((1, 0), (0, 0)))
    minus_x_next = jnp.pad(minus_x[1:, :], ((0, 1), (0, 0)))
    plus_y_prev = jnp.pad(plus_y[:, :-1], ((0, 0), (1, 0)))
    minus_y_next = jnp.pad(minus_y[:, 1:], ((0, 0), (0, 1)))
    result = energy - plus_x + plus_x_prev - minus_x_next + minus_x - plus_y + plus_y_prev - minus_y_next + minus_y
    return (wet.astype(jnp.float32) * result).astype(jnp.bfloat16)


def reference(spectrum, group_speed, stokes_kernel, pair_bins, pair_coef, currents, col_map, wave_wet, ocean_wet):
    slot_col = (col_map[:, None] * OCOLS + jnp.arange(OCOLS, dtype=jnp.int32)[None, :]).reshape(-1).astype(jnp.int32)
    drift_cols = jnp.einsum('kxc,kl->cxl', spectrum.astype(jnp.float32), stokes_kernel.astype(jnp.float32))
    drift = jnp.take(drift_cols, slot_col, axis=0)
    new_currents = ocean_step(currents, drift, ocean_wet)
    surface = jnp.stack([new_currents[:, :, 0], new_currents[:, :, LEV]])
    inverse = jnp.argsort(slot_col).astype(jnp.int32)
    cur = CURRENT_SCALE * jnp.tanh(jnp.transpose(jnp.take(surface, inverse, axis=1), (0, 2, 1)))

    def one_bin(item):
        energy, speeds = item
        return advect_bin(energy, speeds[0], speeds[1], cur, wave_wet)

    advected = lax.map(one_bin, (spectrum, jnp.transpose(group_speed)))

    def one_row(row):
        first = jnp.take(row, pair_bins[0], axis=0).astype(jnp.float32)
        second = jnp.take(row, pair_bins[1], axis=0).astype(jnp.float32)
        products = (pair_coef[:, None] * first * second).astype(jnp.bfloat16)
        source = jax.ops.segment_sum(products.astype(jnp.float32), pair_bins[2], num_segments=NBINS)
        return (row.astype(jnp.float32) + DT_SOURCE * source).astype(jnp.bfloat16)

    rows_first = jnp.transpose(advected, (1, 0, 2))
    new_rows = lax.map(one_row, rows_first)
    new_spectrum = jnp.transpose(new_rows, (1, 0, 2))
    return new_spectrum, new_currents
```

```python
import functools

import jax
import jax.numpy as jnp
from jax import lax
from jax.experimental import pallas as pl
from jax.experimental.pallas import tpu as pltpu
from jax.sharding import PartitionSpec as P

DT_OCEAN = 0.5
CORIOLIS = 0.8
MIXING = 0.4
CURRENT_SCALE = 0.15
DT_SOURCE = 0.5

LANES = 128
ACCS = 4
UNROLL = 32
BLOCK = 16
ROW_GAP = 400
SPEED_LANE = 32
HIGHEST = lax.Precision.HIGHEST
VMEM = pltpu.VMEM
SMEM = pltpu.SMEM


def in_vmem():
    return pl.BlockSpec(memory_space=VMEM)


def in_smem():
    return pl.BlockSpec(memory_space=SMEM)


def call(body, out_shape, ins, outs, scratch, flops, moved, args, name):
    return pl.pallas_call(
        body,
        out_shape=out_shape,
        in_specs=ins,
        out_specs=outs,
        scratch_shapes=scratch,
        name=name,
        compiler_params=pltpu.CompilerParams(vmem_limit_bytes=58 * 2**20),
        cost_estimate=pl.CostEstimate(flops=flops, bytes_accessed=moved, transcendentals=0),
    )(*args)


def wet_columns(wet_ref):
    wet = wet_ref[...].astype(jnp.float32)
    rows = wet.shape[1]
    return jnp.concatenate([wet, jnp.zeros((6, rows), jnp.float32)], axis=0).T


def surface_kernel(currents_ref, wet_ref, speed_ref, out_ref, rows_ref):
    rows = currents_ref.shape[1]
    half = LANES // 2
    lane = lax.broadcasted_iota(jnp.int32, (rows, LANES), 1)
    wet = wet_columns(wet_ref)
    sign = jnp.where(lane < half, CORIOLIS, -CORIOLIS)
    kept = (lane == 0) | (lane == 1) | (lane == half)
    rows_ref[...] = jnp.zeros_like(rows_ref)
    for slot in range(2):
        x = currents_ref[slot]
        cross = sign * pltpu.roll(x, half, 1)
        below = pltpu.roll(x, LANES - 1, 1)
        column = wet[:, slot : slot + 1]
        value = column * (x + DT_OCEAN * (cross + MIXING * (below - x)))
        value = jnp.where(lane == 1, column, value)
        rows_ref[pl.ds(slot * ROW_GAP + 8, rows), :] = jnp.where(kept, value, 0.0)
    total = jnp.broadcast_to(speed_ref[...], (LANES, LANES))
    for slot in range(2):
        for row in range(5):
            part = rows_ref[pl.ds(slot * ROW_GAP + 7 + row, LANES, stride=3), :]
            shift = 2 * (slot * 5 + row)
            total = total + (pltpu.roll(part, shift, 1) if shift else part)
    out_ref[...] = total


def columns_of(map_ref):
    row = jnp.broadcast_to(map_ref[...].astype(jnp.float32), (LANES, LANES))
    column = row.T
    return jnp.concatenate([column, column], axis=1)


def chosen(column, slot):
    index = lax.broadcasted_iota(jnp.int32, column.shape, 1).astype(jnp.float32)
    return (2.0 * column + float(slot)) == index


def tables_kernel(recv_ref, map_ref, surface_ref, speeds_ref):
    recv = recv_ref[...]
    turned = recv.T
    column = columns_of(map_ref)
    parts = []
    for slot in range(2):
        pick = chosen(column, slot).astype(jnp.float32)
        parts.append(jnp.dot(turned, pick, precision=HIGHEST, preferred_element_type=jnp.float32))
    surface_ref[...] = jnp.zeros_like(surface_ref)
    surface_ref[0:10, :] = parts[0][0:10] + parts[1][10:20]
    surface_ref[16:26, :] = parts[0][64:74] + parts[1][74:84]
    bins = speeds_ref.shape[1]
    lane = lax.broadcasted_iota(jnp.int32, (bins, LANES), 1)
    index = lax.broadcasted_iota(jnp.int32, (bins, LANES), 0)
    first = ((lane & 7) * 16 + (lane >> 3)) * 9
    own = (index >= first) & (index < first + 9)
    rows = jnp.dot(
        own.astype(jnp.float32), recv, precision=HIGHEST, preferred_element_type=jnp.float32
    )
    place = index - ((index * 7282) >> 16) * 9
    ones = jnp.ones((LANES, LANES), jnp.float32)
    for part in range(2):
        value = jnp.where(lane == place + (SPEED_LANE + 9 * part), rows, 0.0)
        speeds_ref[part] = jnp.dot(
            value, ones, precision=HIGHEST, preferred_element_type=jnp.float32
        )


def drift_kernel(whole_ref, map_ref, routed_ref, near_ref, weights_ref, rows_ref):
    sources, _, local_bins, _ = whole_ref.shape
    bins = sources * local_bins
    turned = whole_ref[:, 6].reshape(bins, LANES).T
    weights_ref[0:16, :] = turned[0:16]
    weights_ref[16:32, :] = turned[64:80]
    column = columns_of(map_ref)
    picks = [chosen(column, slot).astype(jnp.float32).astype(jnp.bfloat16) for slot in range(2)]
    rows_ref[...] = jnp.zeros_like(rows_ref)
    near_ref[...] = jnp.zeros_like(near_ref)
    for row in range(3):
        parts = [jnp.zeros((LANES, LANES), jnp.float32) for _ in range(2)]
        for half in range(2):
            cells = whole_ref[:, 2 * row + half].reshape(bins, LANES)
            drift = jnp.dot(turned, cells, preferred_element_type=jnp.float32)
            lanes = slice(half * LANES, (half + 1) * LANES)
            near_ref[row : row + 1, lanes] = drift[0:1]
            near_ref[8 + row : 9 + row, lanes] = drift[64:65]
            narrow = drift.astype(jnp.bfloat16)
            for slot in range(2):
                parts[slot] = parts[slot] + lax.dot_general(
                    picks[slot][:, lanes],
                    narrow,
                    (((1,), (1,)), ((), ())),
                    preferred_element_type=jnp.float32,
                )
        for slot in range(2):
            rows_ref[pl.ds(slot * 3 + row, LANES, stride=8), :] = parts[slot]
    routed_ref[...] = rows_ref[...].astype(jnp.bfloat16)


def wave_kernel(
    pair_ref,
    coef_ref,
    whole_ref,
    below_ref,
    above_ref,
    speeds_ref,
    surface_ref,
    near_ref,
    weights_ref,
    wet_ref,
    out_ref,
    field_ref,
    cur_ref,
    *acc_refs,
):
    sources, _, local_bins, _ = whole_ref.shape
    bins = sources * local_bins
    pairs = coef_ref.shape[0]
    steps = local_bins // BLOCK

    weights = weights_ref[...]
    for side, ref in enumerate((below_ref, above_ref)):
        for half in range(2):
            cells = ref[:, half].reshape(bins, LANES)
            drift = jnp.dot(weights, cells, preferred_element_type=jnp.float32)
            lanes = slice(half * LANES, (half + 1) * LANES)
            cur_ref[24 + side : 25 + side, lanes] = drift[0:1]
            cur_ref[32 + side : 33 + side, lanes] = drift[16:17]
    for row in range(5):
        if row in (0, 4):
            side = 0 if row == 0 else 1
            east = cur_ref[24 + side : 25 + side, :]
            north = cur_ref[32 + side : 33 + side, :]
        else:
            east = near_ref[row - 1 : row, :]
            north = near_ref[8 + row - 1 : 8 + row, :]
        fixed_east = surface_ref[2 * row : 2 * row + 1, :]
        wet = surface_ref[2 * row + 1 : 2 * row + 2, :]
        fixed_north = surface_ref[16 + 2 * row : 17 + 2 * row, :]
        factor = (DT_OCEAN * CORIOLIS) * wet
        cur_ref[row : row + 1, :] = CURRENT_SCALE * jnp.tanh(fixed_east + factor * north)
        cur_ref[8 + row : 9 + row, :] = CURRENT_SCALE * jnp.tanh(fixed_north - factor * east)
    for row in range(3):
        cur_ref[16 + row : 17 + row, :] = wet_ref[row : row + 1, :].astype(jnp.float32)

    lane = lax.broadcasted_iota(jnp.int32, (BLOCK, LANES), 1)
    at_first = lane == 0
    at_last = lane == LANES - 1

    def advect(step, carry):
        source = step // steps
        start = pl.multiple_of((step - source * steps) * BLOCK, BLOCK)
        first = source * local_bins + start
        span = pl.ds(start, BLOCK)
        speed_x = speeds_ref[0, pl.ds(pl.multiple_of(first, BLOCK), BLOCK), :]
        speed_y = speeds_ref[1, pl.ds(pl.multiple_of(first, BLOCK), BLOCK), :]

        def cells(ref, chunk):
            return ref[source, chunk, span, :].astype(jnp.float32)

        def row_flux(energy, row, half):
            current = cur_ref[row : row + 1, half * LANES : (half + 1) * LANES]
            return (speed_x + current) * energy

        energy = [[cells(whole_ref, 2 * row + half) for half in range(2)] for row in range(3)]
        for half in range(2):
            flux = [row_flux(cells(below_ref, half), 0, half)]
            flux += [row_flux(energy[row][half], row + 1, half) for row in range(3)]
            flux += [row_flux(cells(above_ref, half), 4, half)]
            for row in range(3):
                energy[row][half] = (
                    energy[row][half],
                    energy[row][half]
                    - jnp.abs(flux[row + 1])
                    + jnp.maximum(flux[row], 0.0)
                    - jnp.minimum(flux[row + 2], 0.0),
                )
        for row in range(3):
            forward = []
            backward = []
            moved = []
            for half in range(2):
                old, value = energy[row][half]
                current = cur_ref[9 + row : 10 + row, half * LANES : (half + 1) * LANES]
                side = (speed_y + current) * old
                moved.append(value - jnp.abs(side))
                forward.append(pltpu.roll(jnp.maximum(side, 0.0), 1, 1))
                backward.append(pltpu.roll(jnp.minimum(side, 0.0), LANES - 1, 1))
            left = [
                jnp.where(at_first, 0.0, forward[0]),
                jnp.where(at_first, forward[0], forward[1]),
            ]
            right = [
                jnp.where(at_last, backward[1], backward[0]),
                jnp.where(at_last, 0.0, backward[1]),
            ]
            for half in range(2):
                wet = cur_ref[16 + row : 17 + row, half * LANES : (half + 1) * LANES]
                result = wet * (moved[half] + left[half] - right[half])
                rows = pl.ds(first * 8 + (2 * row + half), BLOCK, stride=8)
                field_ref[rows, :] = result
                acc_refs[0][rows, :] = result
        zeros = jnp.zeros((BLOCK * 8, LANES), jnp.float32)
        for ref in acc_refs[1:]:
            ref[pl.ds(pl.multiple_of(first * 8, BLOCK * 8), BLOCK * 8), :] = zeros
        return carry

    lax.fori_loop(0, sources * steps, advect, 0)

    def interact(step, carry):
        start = pl.multiple_of(step * UNROLL, UNROLL)
        firsts = pair_ref.at[pl.ds(start, UNROLL)]
        seconds = pair_ref.at[pl.ds(pairs + start, UNROLL)]
        targets = pair_ref.at[pl.ds(2 * pairs + start, UNROLL)]
        coefs = coef_ref.at[pl.ds(start, UNROLL)]
        for item in range(UNROLL):
            first = pl.ds(pl.multiple_of(firsts[item], 8), 8)
            second = pl.ds(pl.multiple_of(seconds[item], 8), 8)
            target = pl.ds(pl.multiple_of(targets[item], 8), 8)
            ref = acc_refs[item % ACCS]
            product = coefs[item] * (field_ref[first, :] * field_ref[second, :])
            ref[target, :] = ref[target, :] + product
        return carry

    lax.fori_loop(0, pairs // UNROLL, interact, 0)

    def finish(step, carry):
        first = pl.multiple_of(step * BLOCK, BLOCK)
        for row in range(3):
            for half in range(2):
                rows = pl.ds(first * 8 + (2 * row + half), BLOCK, stride=8)
                total = acc_refs[0][rows, :]
                for ref in acc_refs[1:]:
                    total = total + ref[rows, :]
                out_ref[row, pl.ds(first, BLOCK), half * LANES : (half + 1) * LANES] = (
                    total.astype(jnp.bfloat16)
                )
        return carry

    lax.fori_loop(0, bins // BLOCK, finish, 0)


def ocean_kernel(currents_ref, recv_ref, wet_ref, out_ref, wide_ref, rows_ref):
    rows = currents_ref.shape[1]
    half = LANES // 2
    lane = lax.broadcasted_iota(jnp.int32, (rows, LANES), 1)
    place = lane & (half - 1)
    sign = jnp.where(lane < half, CORIOLIS, -CORIOLIS)
    wet = wet_columns(wet_ref)
    wide_ref[...] = recv_ref[...].astype(jnp.float32)
    for slot in range(2):
        for row in range(3):
            rows_ref[pl.ds(row, LANES, stride=3), :] = wide_ref[
                pl.ds(slot * 3 + row, LANES, stride=8), :
            ]
        x = currents_ref[slot]
        upper = jnp.where(place == 0, x, pltpu.roll(x, 1, 1))
        lower = jnp.where(place == half - 1, x, pltpu.roll(x, LANES - 1, 1))
        cross = sign * pltpu.roll(x + rows_ref[...], half, 1)
        mixed = upper + lower - 2.0 * x
        out_ref[slot] = wet[:, slot : slot + 1] * (x + DT_OCEAN * (cross + MIXING * mixed))


def per_device(
    spectrum,
    group_speed,
    stokes_kernel,
    pair_bins,
    pair_coef,
    currents,
    col_map,
    wave_wet,
    ocean_wet,
):
    local_bins, tile_rows, columns = spectrum.shape
    space_count = lax.axis_size("space")
    bins_count = lax.axis_size("bins")
    devices = space_count * bins_count
    rows = tile_rows // bins_count
    bins = local_bins * bins_count
    pairs = pair_bins.shape[1]
    both = ("space", "bins")
    f32 = jnp.float32
    bf16 = jnp.bfloat16
    space_at = lax.axis_index("space")
    bins_at = lax.axis_index("bins")

    cells = spectrum.reshape(local_bins, bins_count, rows, 2, LANES)
    cells = jnp.transpose(cells, (1, 2, 3, 0, 4)).reshape(bins_count, 6, local_bins, LANES)
    kernel_copies = jnp.broadcast_to(
        stokes_kernel[None, None], (bins_count, 1, local_bins, LANES)
    )
    whole = lax.all_to_all(
        jnp.concatenate([cells, kernel_copies], axis=1),
        "bins",
        split_axis=0,
        concat_axis=0,
        tiled=True,
    )

    piece = local_bins // space_count
    speeds = lax.dynamic_slice(group_speed, (0, space_at * piece), (2, piece)).reshape(1, -1)
    speeds = jnp.pad(speeds, ((0, 0), (SPEED_LANE, LANES - SPEED_LANE - 2 * piece)))
    surface = call(
        surface_kernel,
        jax.ShapeDtypeStruct((devices, LANES), f32),
        [in_vmem()] * 3,
        in_vmem(),
        [VMEM((2 * ROW_GAP, LANES), f32)],
        4_000_000,
        500_000,
        (currents, ocean_wet, speeds),
        "surface",
    )
    arrived = lax.all_to_all(surface, both, split_axis=0, concat_axis=0, tiled=True)
    map_row = col_map.reshape(1, -1)
    surface_rows, speed_rows = call(
        tables_kernel,
        (
            jax.ShapeDtypeStruct((32, columns), f32),
            jax.ShapeDtypeStruct((2, bins, LANES), f32),
        ),
        [in_vmem()] * 2,
        (in_vmem(), in_vmem()),
        [],
        600_000_000,
        1_300_000,
        (arrived, map_row),
        "tables",
    )

    ahead = [(at, at + 1) for at in range(devices - 1)]
    back = [(at + 1, at) for at in range(devices - 1)]
    below = lax.ppermute(whole[:, 4:6], both, ahead)
    above = lax.ppermute(whole[:, 0:2], both, back)

    routed, near, weights = call(
        drift_kernel,
        (
            jax.ShapeDtypeStruct((devices * 8, LANES), bf16),
            jax.ShapeDtypeStruct((16, columns), f32),
            jax.ShapeDtypeStruct((32, bins), bf16),
        ),
        [in_vmem()] * 2,
        (in_vmem(),) * 3,
        [VMEM((devices * 8, LANES), f32)],
        300_000_000,
        2_500_000,
        (whole, map_row),
        "drift",
    )
    routed = lax.all_to_all(
        routed.reshape(devices, 8, LANES), both, split_axis=0, concat_axis=0, tiled=True
    ).reshape(devices * 8, LANES)

    own_wet = lax.dynamic_slice(wave_wet, (bins_at * rows, 0), (rows, columns))
    new_spectrum = call(
        wave_kernel,
        jax.ShapeDtypeStruct((rows, bins, columns), bf16),
        [in_smem()] * 2 + [in_vmem()] * 8,
        in_vmem(),
        [VMEM((bins * 8, LANES), f32), VMEM((40, columns), f32)]
        + [VMEM((bins * 8, LANES), f32)] * ACCS,
        40_000_000,
        8_000_000,
        (
            pair_bins.reshape(-1) * 8,
            pair_coef * DT_SOURCE,
            whole,
            below,
            above,
            speed_rows,
            surface_rows,
            near,
            weights,
            own_wet,
        ),
        "waves",
    )
    new_currents = call(
        ocean_kernel,
        jax.ShapeDtypeStruct(currents.shape, f32),
        [in_vmem()] * 3,
        in_vmem(),
        [VMEM((devices * 8, LANES), f32), VMEM((currents.shape[1], LANES), f32)],
        4_000_000,
        1_500_000,
        (currents, routed, ocean_wet),
        "ocean",
    )
    return (jnp.transpose(new_spectrum, (1, 0, 2)), new_currents)


def solution(mesh):
    placed = (
        P("bins", "space", None),
        P(None, "bins"),
        P("bins", None),
        P(),
        P(),
        P(("space", "bins"), None, None),
        P(),
        P("space", None),
        P(("space", "bins"), None),
    )
    return jax.shard_map(
        per_device,
        mesh=mesh,
        in_specs=placed,
        out_specs=(P(None, ("space", "bins"), None), P(("space", "bins"), None, None)),
        check_vma=False,
    )
```

```python
import functools

import jax
import jax.numpy as jnp
from jax import lax
from jax.experimental import pallas as pl
from jax.experimental.pallas import tpu as pltpu
from jax.sharding import PartitionSpec as P


DT_OCEAN = 0.5
CORIOLIS = 0.8
MIXING = 0.4
CURRENT_SCALE = 0.15
DT_SOURCE = 0.5

LANES = 128
ACCS = 2
CHUNKS = 7
UNROLL = 32
BLOCK = 16
ROW_GAP = 400
SPEED_LANE = 32
HIGHEST = lax.Precision.HIGHEST
VMEM = pltpu.VMEM
SMEM = pltpu.SMEM


def in_vmem():
    return pl.BlockSpec(memory_space=VMEM)


def in_smem():
    return pl.BlockSpec(memory_space=SMEM)


def anywhere():
    return pl.BlockSpec(memory_space=pl.ANY)


def call(body, out_shape, ins, outs, scratch, flops, moved, args, limit=16):
    return pl.pallas_call(
        body,
        out_shape=out_shape,
        in_specs=ins,
        out_specs=outs,
        scratch_shapes=scratch,
        compiler_params=pltpu.CompilerParams(vmem_limit_bytes=limit * 2**20),
        cost_estimate=pl.CostEstimate(flops=flops, bytes_accessed=moved, transcendentals=0),
    )(*args)


def pack_kernel(order, ids_ref, spectrum_ref, stokes_ref, *refs):
    count = len(order)
    out_refs, (wide_ref, piece_ref, sems) = refs[:count], refs[count:]
    local_bins, tile_rows, _ = spectrum_ref.shape
    rows = tile_rows // count
    for half in range(2):
        lanes = slice(half * LANES, (half + 1) * LANES)
        value = spectrum_ref[:, :, lanes].astype(jnp.float32)
        wide_ref[half] = value.reshape(local_bins * tile_rows, LANES)
    copies = []
    for turn in order:
        base = (ids_ref[0] ^ turn) * rows
        for row in range(rows):
            for half in range(2):
                value = wide_ref[half, pl.ds(base + row, local_bins, stride=tile_rows), :]
                piece_ref[turn, 2 * row + half] = value.astype(jnp.bfloat16)
        piece_ref[turn, 6] = stokes_ref[...]
        copies.append(
            pltpu.make_async_copy(piece_ref.at[turn], out_refs[turn], sems.at[turn])
        )
        copies[-1].start()
    for copy in copies:
        copy.wait()


def piece_copies(piece_refs, whole_ref, sems, own):
    return [
        pltpu.make_async_copy(ref, whole_ref.at[own ^ turn], sems.at[turn])
        for turn, ref in enumerate(piece_refs)
    ]


def wet_columns(wet_ref):
    wet = wet_ref[...].astype(jnp.float32)
    rows = wet.shape[1]
    return jnp.concatenate([wet, jnp.zeros((6, rows), jnp.float32)], axis=0).T


def surface_kernel(currents_ref, wet_ref, speed_ref, out_ref, rows_ref):
    rows = currents_ref.shape[1]
    half = LANES // 2
    lane = lax.broadcasted_iota(jnp.int32, (rows, LANES), 1)
    wet = wet_columns(wet_ref)
    sign = jnp.where(lane < half, CORIOLIS, -CORIOLIS)
    kept = (lane == 0) | (lane == 1) | (lane == half)
    rows_ref[...] = jnp.zeros_like(rows_ref)
    for slot in range(2):
        x = currents_ref[slot]
        cross = sign * pltpu.roll(x, half, 1)
        below = pltpu.roll(x, LANES - 1, 1)
        column = wet[:, slot : slot + 1]
        value = column * (x + DT_OCEAN * (cross + MIXING * (below - x)))
        value = jnp.where(lane == 1, column, value)
        rows_ref[pl.ds(slot * ROW_GAP + 8, rows), :] = jnp.where(kept, value, 0.0)
    total = jnp.broadcast_to(speed_ref[...], (LANES, LANES))
    for slot in range(2):
        for row in range(5):
            part = rows_ref[pl.ds(slot * ROW_GAP + 7 + row, LANES, stride=3), :]
            shift = 2 * (slot * 5 + row)
            total = total + (pltpu.roll(part, shift, 1) if shift else part)
    out_ref[...] = total


def columns_of(map_ref):
    row = jnp.broadcast_to(map_ref[...].astype(jnp.float32), (LANES, LANES))
    column = row.T
    return jnp.concatenate([column, column], axis=1)


def chosen(column, slot):
    index = lax.broadcasted_iota(jnp.int32, column.shape, 1).astype(jnp.float32)
    return (2.0 * column + float(slot)) == index


def tables_kernel(recv_ref, map_ref, surface_ref, speeds_ref):
    recv = recv_ref[...]
    turned = recv.T
    column = columns_of(map_ref)
    parts = []
    for slot in range(2):
        pick = chosen(column, slot).astype(jnp.float32)
        parts.append(jnp.dot(turned, pick, precision=HIGHEST, preferred_element_type=jnp.float32))
    surface_ref[...] = jnp.zeros_like(surface_ref)
    surface_ref[0:10, :] = parts[0][0:10] + parts[1][10:20]
    surface_ref[16:26, :] = parts[0][64:74] + parts[1][74:84]
    bins = speeds_ref.shape[1]
    lane = lax.broadcasted_iota(jnp.int32, (bins, LANES), 1)
    index = lax.broadcasted_iota(jnp.int32, (bins, LANES), 0)
    first = ((lane & 7) * 16 + (lane >> 3)) * 9
    own = (index >= first) & (index < first + 9)
    rows = jnp.dot(
        own.astype(jnp.float32), recv, precision=HIGHEST, preferred_element_type=jnp.float32
    )
    place = index - ((index * 7282) >> 16) * 9
    ones = jnp.ones((LANES, LANES), jnp.float32)
    for part in range(2):
        value = jnp.where(lane == place + (SPEED_LANE + 9 * part), rows, 0.0)
        speeds_ref[part] = jnp.dot(
            value, ones, precision=HIGHEST, preferred_element_type=jnp.float32
        )


def drift_kernel(count, ids_ref, map_ref, *refs):
    piece_refs = refs[:count]
    routed_ref, near_ref, weights_ref, rows_ref, whole_ref, sems = refs[count:]
    copies = piece_copies(piece_refs, whole_ref, sems, ids_ref[0])
    for copy in copies:
        copy.start()
    sources, _, local_bins, _ = whole_ref.shape
    bins = sources * local_bins
    for copy in copies:
        copy.wait()
    turned = whole_ref[:, 6].reshape(bins, LANES).T
    weights_ref[0:16, :] = turned[0:16]
    weights_ref[16:32, :] = turned[64:80]
    column = columns_of(map_ref)
    picks = [chosen(column, slot).astype(jnp.float32).astype(jnp.bfloat16) for slot in range(2)]
    rows_ref[...] = jnp.zeros_like(rows_ref)
    near_ref[...] = jnp.zeros_like(near_ref)
    for row in range(3):
        parts = [jnp.zeros((LANES, LANES), jnp.float32) for _ in range(2)]
        for half in range(2):
            cells = whole_ref[:, 2 * row + half].reshape(bins, LANES)
            drift = jnp.dot(turned, cells, preferred_element_type=jnp.float32)
            lanes = slice(half * LANES, (half + 1) * LANES)
            near_ref[row : row + 1, lanes] = drift[0:1]
            near_ref[8 + row : 9 + row, lanes] = drift[64:65]
            narrow = drift.astype(jnp.bfloat16)
            for slot in range(2):
                parts[slot] = parts[slot] + lax.dot_general(
                    picks[slot][:, lanes],
                    narrow,
                    (((1,), (1,)), ((), ())),
                    preferred_element_type=jnp.float32,
                )
        for slot in range(2):
            rows_ref[pl.ds(slot * 3 + row, LANES, stride=8), :] = parts[slot]
    routed_ref[...] = rows_ref[...].astype(jnp.bfloat16)


def wave_kernel(
    count,
    ids_ref,
    speeds_hbm,
    pair_hbm,
    coef_hbm,
    below_hbm,
    above_hbm,
    surface_ref,
    near_ref,
    weights_ref,
    wet_ref,
    *refs,
):
    piece_refs = refs[:count]
    (
        out_hbm,
        whole_ref,
        below_ref,
        above_ref,
        speeds_ref,
        pair_ref,
        coef_ref,
        out_ref,
        field_ref,
        cur_ref,
        piece_sems,
        halo_sems,
        table_sems,
        out_sems,
        *acc_refs,
    ) = refs[count:]
    sources, _, local_bins, _ = whole_ref.shape
    bins = sources * local_bins
    pairs = coef_ref.shape[0]
    steps = local_bins // BLOCK

    halo_copies = []
    for source in range(sources):
        for side, (src, dst) in enumerate(((below_hbm, below_ref), (above_hbm, above_ref))):
            halo_copies.append(
                pltpu.make_async_copy(
                    src.at[ids_ref[1 + side] ^ source],
                    dst.at[source],
                    halo_sems.at[2 * source + side],
                )
            )
    bulk_copies = piece_copies(piece_refs, whole_ref, piece_sems, ids_ref[0])
    bulk_copies.append(pltpu.make_async_copy(speeds_hbm, speeds_ref, table_sems.at[0]))
    pair_copies = [
        pltpu.make_async_copy(pair_hbm, pair_ref, table_sems.at[1]),
        pltpu.make_async_copy(coef_hbm, coef_ref, table_sems.at[2]),
    ]
    for copy in halo_copies + bulk_copies + pair_copies:
        copy.start()
    for ref in acc_refs[1:]:
        ref[...] = jnp.zeros_like(ref)
    for copy in halo_copies:
        copy.wait()

    weights = weights_ref[...]
    for side, ref in enumerate((below_ref, above_ref)):
        for half in range(2):
            cells = ref[:, half].reshape(bins, LANES)
            drift = jnp.dot(weights, cells, preferred_element_type=jnp.float32)
            lanes = slice(half * LANES, (half + 1) * LANES)
            cur_ref[24 + side : 25 + side, lanes] = drift[0:1]
            cur_ref[32 + side : 33 + side, lanes] = drift[16:17]
    for row in range(5):
        if row in (0, 4):
            side = 0 if row == 0 else 1
            east = cur_ref[24 + side : 25 + side, :]
            north = cur_ref[32 + side : 33 + side, :]
        else:
            east = near_ref[row - 1 : row, :]
            north = near_ref[8 + row - 1 : 8 + row, :]
        fixed_east = surface_ref[2 * row : 2 * row + 1, :]
        wet = surface_ref[2 * row + 1 : 2 * row + 2, :]
        fixed_north = surface_ref[16 + 2 * row : 17 + 2 * row, :]
        factor = (DT_OCEAN * CORIOLIS) * wet
        cur_ref[row : row + 1, :] = CURRENT_SCALE * jnp.tanh(fixed_east + factor * north)
        cur_ref[8 + row : 9 + row, :] = CURRENT_SCALE * jnp.tanh(fixed_north - factor * east)
    for row in range(3):
        cur_ref[16 + row : 17 + row, :] = wet_ref[row : row + 1, :].astype(jnp.float32)

    lane = lax.broadcasted_iota(jnp.int32, (BLOCK, LANES), 1)
    at_first = lane == 0
    at_last = lane == LANES - 1

    def advect(step, carry):
        source = step // steps
        start = pl.multiple_of((step - source * steps) * BLOCK, BLOCK)
        first = source * local_bins + start
        span = pl.ds(start, BLOCK)
        speed_x = speeds_ref[0, pl.ds(pl.multiple_of(first, BLOCK), BLOCK), :]
        speed_y = speeds_ref[1, pl.ds(pl.multiple_of(first, BLOCK), BLOCK), :]

        def cells(ref, chunk):
            return ref[source, chunk, span, :].astype(jnp.float32)

        def row_flux(energy, row, half):
            current = cur_ref[row : row + 1, half * LANES : (half + 1) * LANES]
            return (speed_x + current) * energy

        energy = [[cells(whole_ref, 2 * row + half) for half in range(2)] for row in range(3)]
        for half in range(2):
            flux = [row_flux(cells(below_ref, half), 0, half)]
            flux += [row_flux(energy[row][half], row + 1, half) for row in range(3)]
            flux += [row_flux(cells(above_ref, half), 4, half)]
            for row in range(3):
                energy[row][half] = (
                    energy[row][half],
                    energy[row][half]
                    - jnp.abs(flux[row + 1])
                    + jnp.maximum(flux[row], 0.0)
                    - jnp.minimum(flux[row + 2], 0.0),
                )
        for row in range(3):
            forward = []
            backward = []
            moved = []
            for half in range(2):
                old, value = energy[row][half]
                current = cur_ref[9 + row : 10 + row, half * LANES : (half + 1) * LANES]
                side = (speed_y + current) * old
                moved.append(value - jnp.abs(side))
                forward.append(pltpu.roll(jnp.maximum(side, 0.0), 1, 1))
                backward.append(pltpu.roll(jnp.minimum(side, 0.0), LANES - 1, 1))
            left = [
                jnp.where(at_first, 0.0, forward[0]),
                jnp.where(at_first, forward[0], forward[1]),
            ]
            right = [
                jnp.where(at_last, backward[1], backward[0]),
                jnp.where(at_last, 0.0, backward[1]),
            ]
            for half in range(2):
                wet = cur_ref[16 + row : 17 + row, half * LANES : (half + 1) * LANES]
                result = wet * (moved[half] + left[half] - right[half])
                rows = pl.ds(first * 8 + (2 * row + half), BLOCK, stride=8)
                field_ref[rows, :] = result
                acc_refs[0][rows, :] = result
        return carry

    for copy in bulk_copies:
        copy.wait()
    lax.fori_loop(0, sources * steps, advect, 0)
    for copy in pair_copies:
        copy.wait()

    def interact(step, carry):
        start = pl.multiple_of(step * UNROLL, UNROLL)
        firsts = pair_ref.at[pl.ds(start, UNROLL)]
        seconds = pair_ref.at[pl.ds(pairs + start, UNROLL)]
        targets = pair_ref.at[pl.ds(2 * pairs + start, UNROLL)]
        coefs = coef_ref.at[pl.ds(start, UNROLL)]
        for item in range(UNROLL):
            first = pl.ds(pl.multiple_of(firsts[item], 8), 8)
            second = pl.ds(pl.multiple_of(seconds[item], 8), 8)
            target = pl.ds(pl.multiple_of(targets[item], 8), 8)
            ref = acc_refs[item % ACCS]
            product = coefs[item] * (field_ref[first, :] * field_ref[second, :])
            ref[target, :] = ref[target, :] + product
        return carry

    lax.fori_loop(0, pairs // UNROLL, interact, 0)

    def finish(step, carry):
        first = pl.multiple_of(step * BLOCK, BLOCK)
        for row in range(3):
            for half in range(2):
                rows = pl.ds(first * 8 + (2 * row + half), BLOCK, stride=8)
                total = acc_refs[0][rows, :]
                for ref in acc_refs[1:]:
                    total = total + ref[rows, :]
                out_ref[row, pl.ds(first, BLOCK), half * LANES : (half + 1) * LANES] = (
                    total.astype(jnp.bfloat16)
                )
        return carry

    parts = 4
    out_copies = []
    for part in range(parts):
        span = pl.ds(part * (bins // parts), bins // parts)
        each = bins // BLOCK // parts
        lax.fori_loop(part * each, (part + 1) * each, finish, 0)
        for row in range(3):
            out_copies.append(
                pltpu.make_async_copy(
                    out_ref.at[row, span], out_hbm.at[row, span], out_sems.at[3 * part + row]
                )
            )
            out_copies[-1].start()
    for copy in out_copies:
        copy.wait()


def ocean_kernel(currents_ref, recv_ref, wet_ref, out_ref, wide_ref, rows_ref):
    rows = currents_ref.shape[1]
    half = LANES // 2
    lane = lax.broadcasted_iota(jnp.int32, (rows, LANES), 1)
    place = lane & (half - 1)
    sign = jnp.where(lane < half, CORIOLIS, -CORIOLIS)
    wet = wet_columns(wet_ref)
    wide_ref[...] = recv_ref[...].astype(jnp.float32)
    for slot in range(2):
        for row in range(3):
            rows_ref[pl.ds(row, LANES, stride=3), :] = wide_ref[
                pl.ds(slot * 3 + row, LANES, stride=8), :
            ]
        x = currents_ref[slot]
        upper = jnp.where(place == 0, x, pltpu.roll(x, 1, 1))
        lower = jnp.where(place == half - 1, x, pltpu.roll(x, LANES - 1, 1))
        cross = sign * pltpu.roll(x + rows_ref[...], half, 1)
        mixed = upper + lower - 2.0 * x
        out_ref[slot] = wet[:, slot : slot + 1] * (x + DT_OCEAN * (cross + MIXING * mixed))


def per_device(
    spectrum,
    group_speed,
    stokes_kernel,
    pair_bins,
    pair_coef,
    currents,
    col_map,
    wave_wet,
    ocean_wet,
):
    local_bins, tile_rows, columns = spectrum.shape
    space_count = lax.axis_size("space")
    bins_count = lax.axis_size("bins")
    devices = space_count * bins_count
    rows = tile_rows // bins_count
    bins = local_bins * bins_count
    pairs = pair_bins.shape[1]
    both = ("space", "bins")
    f32 = jnp.float32
    bf16 = jnp.bfloat16
    space_at = lax.axis_index("space")
    bins_at = lax.axis_index("bins")

    ids = jnp.stack(
        [bins_at, (bins_at + bins_count - 1) % bins_count, (bins_at + 1) % bins_count]
    ).astype(jnp.int32)

    order = (4, 5, 2, 3, 6, 7, 1, 0)
    piece_shape = (CHUNKS, local_bins, LANES)
    sent = call(
        functools.partial(pack_kernel, order),
        [jax.ShapeDtypeStruct(piece_shape, bf16)] * bins_count,
        [in_smem(), in_vmem(), in_vmem()],
        [anywhere()] * bins_count,
        [
            VMEM((2, local_bins * tile_rows, LANES), f32),
            VMEM((bins_count, *piece_shape), bf16),
            pltpu.SemaphoreType.DMA((bins_count,)),
        ],
        2_000_000,
        4_000_000,
        (ids, spectrum, stokes_kernel),
    )
    pieces = [sent[0]] * bins_count
    for turn in order[:-1]:
        partners = [(at, at ^ turn) for at in range(bins_count)]
        pieces[turn] = lax.ppermute(sent[turn], "bins", partners)

    piece = local_bins // space_count
    speeds = lax.dynamic_slice(group_speed, (0, space_at * piece), (2, piece)).reshape(1, -1)
    speeds = jnp.pad(speeds, ((0, 0), (SPEED_LANE, LANES - SPEED_LANE - 2 * piece)))
    surface = call(
        surface_kernel,
        jax.ShapeDtypeStruct((devices, LANES), f32),
        [in_vmem()] * 3,
        in_vmem(),
        [VMEM((2 * ROW_GAP, LANES), f32)],
        4_000_000,
        500_000,
        (currents, ocean_wet, speeds),
    )
    arrived = lax.all_to_all(surface, both, split_axis=0, concat_axis=0, tiled=True)
    map_row = col_map.reshape(1, -1)
    surface_rows, speed_rows = call(
        tables_kernel,
        (
            jax.ShapeDtypeStruct((32, columns), f32),
            jax.ShapeDtypeStruct((2, bins, LANES), f32),
        ),
        [in_vmem()] * 2,
        (in_vmem(), in_vmem()),
        [],
        600_000_000,
        1_300_000,
        (arrived, map_row),
    )

    ahead = [(at, at + 1) for at in range(devices - 1)]
    back = [(at + 1, at) for at in range(devices - 1)]
    below = lax.ppermute(jnp.stack([piece[4:6] for piece in pieces]), both, ahead)
    above = lax.ppermute(jnp.stack([piece[0:2] for piece in pieces]), both, back)

    whole_shape = (bins_count, *piece_shape)
    routed, near, weights = call(
        functools.partial(drift_kernel, bins_count),
        (
            jax.ShapeDtypeStruct((devices * 8, LANES), bf16),
            jax.ShapeDtypeStruct((16, columns), f32),
            jax.ShapeDtypeStruct((32, bins), bf16),
        ),
        [in_smem(), in_vmem()] + [anywhere()] * bins_count,
        (in_vmem(),) * 3,
        [
            VMEM((devices * 8, LANES), f32),
            VMEM(whole_shape, bf16),
            pltpu.SemaphoreType.DMA((bins_count,)),
        ],
        300_000_000,
        2_500_000,
        (ids, map_row, *pieces),
    )
    routed = lax.all_to_all(
        routed.reshape(devices, 8, LANES), both, split_axis=0, concat_axis=0, tiled=True
    )
    routed = routed.reshape(devices * 8, LANES)

    own_wet = lax.dynamic_slice(wave_wet, (bins_at * rows, 0), (rows, columns))
    halo_shape = (bins_count, 2, local_bins, LANES)
    new_spectrum = call(
        functools.partial(wave_kernel, bins_count),
        jax.ShapeDtypeStruct((rows, bins, columns), bf16),
        [in_smem()] + [anywhere()] * 5 + [in_vmem()] * 4 + [anywhere()] * bins_count,
        anywhere(),
        [
            VMEM(whole_shape, bf16),
            VMEM(halo_shape, bf16),
            VMEM(halo_shape, bf16),
            VMEM((2, bins, LANES), f32),
            SMEM((3 * pairs,), jnp.int32),
            SMEM((pairs,), f32),
            VMEM((rows, bins, columns), bf16),
            VMEM((bins * 8, LANES), f32),
            VMEM((40, columns), f32),
            pltpu.SemaphoreType.DMA((bins_count,)),
            pltpu.SemaphoreType.DMA((2 * bins_count,)),
            pltpu.SemaphoreType.DMA((3,)),
            pltpu.SemaphoreType.DMA((12,)),
        ]
        + [VMEM((bins * 8, LANES), f32)] * ACCS,
        40_000_000,
        8_000_000,
        (
            ids,
            speed_rows,
            pair_bins.reshape(-1) * 8,
            pair_coef * DT_SOURCE,
            below,
            above,
            surface_rows,
            near,
            weights,
            own_wet,
            *pieces,
        ),
        26,
    )
    new_currents = call(
        ocean_kernel,
        jax.ShapeDtypeStruct(currents.shape, f32),
        [in_vmem()] * 3,
        in_vmem(),
        [VMEM((devices * 8, LANES), f32), VMEM((currents.shape[1], LANES), f32)],
        4_000_000,
        1_500_000,
        (currents, routed, ocean_wet),
    )
    return (jnp.transpose(new_spectrum, (1, 0, 2)), new_currents)


def solution(mesh):
    placed = (
        P("bins", "space", None),
        P(None, "bins"),
        P("bins", None),
        P(),
        P(),
        P(("space", "bins"), None, None),
        P(),
        P("space", None),
        P(("space", "bins"), None),
    )

    return jax.shard_map(
        per_device,
        mesh=mesh,
        in_specs=placed,
        out_specs=(P(None, ("space", "bins"), None), P(("space", "bins"), None, None)),
        check_vma=False,
    )
```

```python
import functools

import jax
import jax.numpy as jnp
from jax import lax
from jax.experimental import pallas as pl
from jax.experimental.pallas import tpu as pltpu
from jax.sharding import PartitionSpec as P


DT_OCEAN = 0.5
CORIOLIS = 0.8
MIXING = 0.4
CURRENT_SCALE = 0.15
DT_SOURCE = 0.5

LANES = 128
ACCS = 3
WAVE_LIMIT = 24
CHUNKS = 7
UNROLL = 48
BLOCK = 16
ROW_GAP = 400
SPEED_LANE = 32
HIGHEST = lax.Precision.HIGHEST
VMEM = pltpu.VMEM
SMEM = pltpu.SMEM


def in_vmem():
    return pl.BlockSpec(memory_space=VMEM)


def in_smem():
    return pl.BlockSpec(memory_space=SMEM)


def in_hbm():
    return pl.BlockSpec(memory_space=pltpu.HBM)


def call(body, out_shape, ins, outs, scratch, flops, moved, args, limit=16):
    return pl.pallas_call(
        body,
        out_shape=out_shape,
        in_specs=ins,
        out_specs=outs,
        scratch_shapes=scratch,
        compiler_params=pltpu.CompilerParams(vmem_limit_bytes=limit * 2**20),
        cost_estimate=pl.CostEstimate(flops=flops, bytes_accessed=moved, transcendentals=0),
    )(*args)


def pack_kernel(order, ids_ref, spectrum_hbm, stokes_hbm, *refs):
    count = len(order)
    out_refs = refs[:count]
    narrow_ref, wide_ref, in_sems, stokes_sems = refs[count:]
    local_bins, tile_rows, _ = spectrum_hbm.shape
    rows = tile_rows // count
    chunks = in_sems.shape[0]
    part = local_bins // chunks
    loads = []
    for chunk in range(chunks):
        span = pl.ds(chunk * part, part)
        loads.append(
            pltpu.make_async_copy(spectrum_hbm.at[span], narrow_ref.at[span], in_sems.at[chunk])
        )
        loads[-1].start()
    stokes = [
        pltpu.make_async_copy(stokes_hbm, out_refs[turn].at[6], stokes_sems.at[turn])
        for turn in range(count)
    ]
    for copy in stokes:
        copy.start()
    own = ids_ref[0]
    for chunk in range(chunks):
        loads[chunk].wait()
        first = chunk * part
        for half in range(2):
            lanes = slice(half * LANES, (half + 1) * LANES)
            value = narrow_ref[first : first + part, :, lanes].astype(jnp.float32)
            wide_ref[half, first * tile_rows : (first + part) * tile_rows] = value.reshape(
                part * tile_rows, LANES
            )
        for turn in order:
            base = (own ^ turn) * rows + first * tile_rows
            for row in range(rows):
                for half in range(2):
                    value = wide_ref[half, pl.ds(base + row, part, stride=tile_rows), :]
                    out_refs[turn][2 * row + half, first : first + part, :] = value.astype(
                        jnp.bfloat16
                    )
    for copy in stokes:
        copy.wait()


def joined(refs, chunk):
    return jnp.concatenate([ref[chunk] for ref in refs], axis=0)


def edges_kernel(*refs):
    last_ref, first_ref = refs[-2:]
    for turn, ref in enumerate(refs[:-2]):
        last_ref[turn] = ref[4:6]
        first_ref[turn] = ref[0:2]


def wet_columns(wet_ref):
    wet = wet_ref[...].astype(jnp.float32)
    rows = wet.shape[1]
    return jnp.concatenate([wet, jnp.zeros((6, rows), jnp.float32)], axis=0).T


def surface_kernel(currents_ref, wet_ref, speed_ref, out_ref, rows_ref):
    rows = currents_ref.shape[1]
    half = LANES // 2
    lane = lax.broadcasted_iota(jnp.int32, (rows, LANES), 1)
    wet = wet_columns(wet_ref)
    sign = jnp.where(lane < half, CORIOLIS, -CORIOLIS)
    kept = (lane == 0) | (lane == 1) | (lane == half)
    rows_ref[...] = jnp.zeros_like(rows_ref)
    for slot in range(2):
        x = currents_ref[slot]
        cross = sign * pltpu.roll(x, half, 1)
        below = pltpu.roll(x, LANES - 1, 1)
        column = wet[:, slot : slot + 1]
        value = column * (x + DT_OCEAN * (cross + MIXING * (below - x)))
        value = jnp.where(lane == 1, column, value)
        rows_ref[pl.ds(slot * ROW_GAP + 8, rows), :] = jnp.where(kept, value, 0.0)
    total = jnp.broadcast_to(speed_ref[...], (LANES, LANES))
    for slot in range(2):
        for row in range(5):
            part = rows_ref[pl.ds(slot * ROW_GAP + 7 + row, LANES, stride=3), :]
            shift = 2 * (slot * 5 + row)
            total = total + (pltpu.roll(part, shift, 1) if shift else part)
    out_ref[...] = total


def columns_of(map_ref):
    row = jnp.broadcast_to(map_ref[...].astype(jnp.float32), (LANES, LANES))
    column = row.T
    return jnp.concatenate([column, column], axis=1)


def chosen(column, slot):
    index = lax.broadcasted_iota(jnp.int32, column.shape, 1).astype(jnp.float32)
    return (2.0 * column + float(slot)) == index


def tables_kernel(recv_ref, map_ref, coef_ref, surface_ref, speeds_ref, coefs_ref):
    for block in range(coef_ref.shape[0]):
        row = DT_SOURCE * coef_ref[block : block + 1, :]
        coefs_ref[block * LANES : (block + 1) * LANES, :] = jnp.broadcast_to(
            row, (LANES, LANES)
        ).T
    recv = recv_ref[...]
    turned = recv.T
    column = columns_of(map_ref)
    parts = []
    for slot in range(2):
        pick = chosen(column, slot).astype(jnp.float32)
        parts.append(jnp.dot(turned, pick, precision=HIGHEST, preferred_element_type=jnp.float32))
    surface_ref[...] = jnp.zeros_like(surface_ref)
    surface_ref[0:10, :] = parts[0][0:10] + parts[1][10:20]
    surface_ref[16:26, :] = parts[0][64:74] + parts[1][74:84]
    bins = speeds_ref.shape[1]
    lane = lax.broadcasted_iota(jnp.int32, (bins, LANES), 1)
    index = lax.broadcasted_iota(jnp.int32, (bins, LANES), 0)
    first = ((lane & 7) * 16 + (lane >> 3)) * 9
    own = (index >= first) & (index < first + 9)
    rows = jnp.dot(
        own.astype(jnp.float32), recv, precision=HIGHEST, preferred_element_type=jnp.float32
    )
    place = index - ((index * 7282) >> 16) * 9
    ones = jnp.ones((LANES, LANES), jnp.float32)
    for part in range(2):
        value = jnp.where(lane == place + (SPEED_LANE + 9 * part), rows, 0.0)
        speeds_ref[part] = jnp.dot(
            value, ones, precision=HIGHEST, preferred_element_type=jnp.float32
        )


def drift_kernel(count, ids_ref, map_ref, *refs):
    piece_refs = refs[:count]
    routed_ref, near_ref, weights_ref, rows_ref, stokes_ref = refs[count:]
    own = ids_ref[0]
    for turn, ref in enumerate(piece_refs):
        stokes_ref[own ^ turn] = ref[6]
    in_order = stokes_ref[...].reshape(-1, LANES).T
    weights_ref[0:16, :] = in_order[0:16]
    weights_ref[16:32, :] = in_order[64:80]
    turned = joined(piece_refs, 6).T
    column = columns_of(map_ref)
    picks = [chosen(column, slot).astype(jnp.float32).astype(jnp.bfloat16) for slot in range(2)]
    rows_ref[...] = jnp.zeros_like(rows_ref)
    near_ref[...] = jnp.zeros_like(near_ref)
    for row in range(3):
        parts = [jnp.zeros((LANES, LANES), jnp.float32) for _ in range(2)]
        for half in range(2):
            cells = joined(piece_refs, 2 * row + half)
            drift = jnp.dot(turned, cells, preferred_element_type=jnp.float32)
            lanes = slice(half * LANES, (half + 1) * LANES)
            near_ref[row : row + 1, lanes] = drift[0:1]
            near_ref[8 + row : 9 + row, lanes] = drift[64:65]
            narrow = drift.astype(jnp.bfloat16)
            for slot in range(2):
                parts[slot] = parts[slot] + lax.dot_general(
                    picks[slot][:, lanes],
                    narrow,
                    (((1,), (1,)), ((), ())),
                    preferred_element_type=jnp.float32,
                )
        for slot in range(2):
            rows_ref[pl.ds(slot * 3 + row, LANES, stride=8), :] = parts[slot]
    routed_ref[...] = rows_ref[...].astype(jnp.bfloat16)


def wave_kernel(
    count,
    ids_ref,
    pair_hbm,
    coef_ref,
    speeds_ref,
    below_ref,
    above_ref,
    surface_ref,
    near_ref,
    weights_ref,
    wet_ref,
    *refs,
):
    piece_refs = refs[:count]
    out_hbm, pair_ref, out_ref, field_ref, cur_ref, pair_sem, out_sems, *acc_refs = refs[count:]
    local_bins = piece_refs[0].shape[1]
    bins = count * local_bins
    pairs = coef_ref.shape[0]

    pair_copy = pltpu.make_async_copy(pair_hbm, pair_ref, pair_sem)
    pair_copy.start()
    own = ids_ref[0]
    for ref in acc_refs:
        ref[...] = jnp.zeros_like(ref)

    weights = weights_ref[...]
    for side, ref in enumerate((below_ref, above_ref)):
        for half in range(2):
            blocks = [ref[ids_ref[1 + side] ^ block, half] for block in range(count)]
            cells = jnp.concatenate(blocks, axis=0)
            drift = jnp.dot(weights, cells, preferred_element_type=jnp.float32)
            lanes = slice(half * LANES, (half + 1) * LANES)
            cur_ref[24 + side : 25 + side, lanes] = drift[0:1]
            cur_ref[32 + side : 33 + side, lanes] = drift[16:17]
    for row in range(5):
        if row in (0, 4):
            side = 0 if row == 0 else 1
            east = cur_ref[24 + side : 25 + side, :]
            north = cur_ref[32 + side : 33 + side, :]
        else:
            east = near_ref[row - 1 : row, :]
            north = near_ref[8 + row - 1 : 8 + row, :]
        fixed_east = surface_ref[2 * row : 2 * row + 1, :]
        wet = surface_ref[2 * row + 1 : 2 * row + 2, :]
        fixed_north = surface_ref[16 + 2 * row : 17 + 2 * row, :]
        factor = (DT_OCEAN * CORIOLIS) * wet
        cur_ref[row : row + 1, :] = CURRENT_SCALE * jnp.tanh(fixed_east + factor * north)
        cur_ref[8 + row : 9 + row, :] = CURRENT_SCALE * jnp.tanh(fixed_north - factor * east)
    for row in range(3):
        cur_ref[16 + row : 17 + row, :] = wet_ref[row : row + 1, :].astype(jnp.float32)

    lane = lax.broadcasted_iota(jnp.int32, (BLOCK, LANES), 1)
    at_first = lane == 0
    at_last = lane == LANES - 1

    def advect(piece_ref, block, step):
        start = pl.multiple_of(step * BLOCK, BLOCK)
        first = block * local_bins + start
        span = pl.ds(start, BLOCK)
        below_at = ids_ref[1] ^ block
        above_at = ids_ref[2] ^ block
        speed_x = speeds_ref[0, pl.ds(pl.multiple_of(first, BLOCK), BLOCK), :]
        speed_y = speeds_ref[1, pl.ds(pl.multiple_of(first, BLOCK), BLOCK), :]

        def row_flux(energy, row, half):
            current = cur_ref[row : row + 1, half * LANES : (half + 1) * LANES]
            return (speed_x + current) * energy

        energy = [
            [piece_ref[2 * row + half, span, :].astype(jnp.float32) for half in range(2)]
            for row in range(3)
        ]
        for half in range(2):
            flux = [row_flux(below_ref[below_at, half, span, :].astype(jnp.float32), 0, half)]
            flux += [row_flux(energy[row][half], row + 1, half) for row in range(3)]
            flux += [row_flux(above_ref[above_at, half, span, :].astype(jnp.float32), 4, half)]
            for row in range(3):
                energy[row][half] = (
                    energy[row][half],
                    energy[row][half]
                    - jnp.abs(flux[row + 1])
                    + jnp.maximum(flux[row], 0.0)
                    - jnp.minimum(flux[row + 2], 0.0),
                )
        for row in range(3):
            forward = []
            backward = []
            moved = []
            for half in range(2):
                old, value = energy[row][half]
                current = cur_ref[9 + row : 10 + row, half * LANES : (half + 1) * LANES]
                side = (speed_y + current) * old
                moved.append(value - jnp.abs(side))
                forward.append(pltpu.roll(jnp.maximum(side, 0.0), 1, 1))
                backward.append(pltpu.roll(jnp.minimum(side, 0.0), LANES - 1, 1))
            left = [
                jnp.where(at_first, 0.0, forward[0]),
                jnp.where(at_first, forward[0], forward[1]),
            ]
            right = [
                jnp.where(at_last, backward[1], backward[0]),
                jnp.where(at_last, 0.0, backward[1]),
            ]
            for half in range(2):
                wet = cur_ref[16 + row : 17 + row, half * LANES : (half + 1) * LANES]
                result = wet * (moved[half] + left[half] - right[half])
                rows = pl.ds(first * 8 + (2 * row + half), BLOCK, stride=8)
                field_ref[rows, :] = result

    for turn, piece_ref in enumerate(piece_refs):
        block = own ^ turn

        def one(step, carry, piece_ref=piece_ref, block=block):
            advect(piece_ref, block, step)
            return carry

        lax.fori_loop(0, local_bins // BLOCK, one, 0)
    pair_copy.wait()

    def interact(step, carry):
        start = pl.multiple_of(step * UNROLL, UNROLL)
        firsts = pair_ref.at[pl.ds(start, UNROLL)]
        seconds = pair_ref.at[pl.ds(pairs + start, UNROLL)]
        targets = pair_ref.at[pl.ds(2 * pairs + start, UNROLL)]
        coefs = coef_ref.at[pl.ds(start, UNROLL)]
        for item in range(UNROLL):
            first = pl.ds(pl.multiple_of(firsts[item], 8), 8)
            second = pl.ds(pl.multiple_of(seconds[item], 8), 8)
            target = pl.ds(pl.multiple_of(targets[item], 8), 8)
            ref = acc_refs[item % ACCS]
            product = coefs[item : item + 1, :] * (field_ref[first, :] * field_ref[second, :])
            ref[target, :] = ref[target, :] + product
        return carry

    lax.fori_loop(0, pairs // UNROLL, interact, 0)

    def finish(step, carry):
        first = pl.multiple_of(step * BLOCK, BLOCK)
        for row in range(3):
            for half in range(2):
                rows = pl.ds(first * 8 + (2 * row + half), BLOCK, stride=8)
                total = field_ref[rows, :]
                for ref in acc_refs:
                    total = total + ref[rows, :]
                out_ref[row, pl.ds(first, BLOCK), half * LANES : (half + 1) * LANES] = (
                    total.astype(jnp.bfloat16)
                )
        return carry

    parts = 4
    out_copies = []
    for part in range(parts):
        span = pl.ds(part * (bins // parts), bins // parts)
        each = bins // BLOCK // parts
        lax.fori_loop(part * each, (part + 1) * each, finish, 0)
        for row in range(3):
            out_copies.append(
                pltpu.make_async_copy(
                    out_ref.at[row, span], out_hbm.at[row, span], out_sems.at[3 * part + row]
                )
            )
            out_copies[-1].start()
    for copy in out_copies:
        copy.wait()


def ocean_kernel(currents_ref, recv_ref, wet_ref, out_ref, wide_ref, rows_ref):
    rows = currents_ref.shape[1]
    half = LANES // 2
    lane = lax.broadcasted_iota(jnp.int32, (rows, LANES), 1)
    place = lane & (half - 1)
    sign = jnp.where(lane < half, CORIOLIS, -CORIOLIS)
    wet = wet_columns(wet_ref)
    wide_ref[...] = recv_ref[...].astype(jnp.float32)
    for slot in range(2):
        for row in range(3):
            rows_ref[pl.ds(row, LANES, stride=3), :] = wide_ref[
                pl.ds(slot * 3 + row, LANES, stride=8), :
            ]
        x = currents_ref[slot]
        upper = jnp.where(place == 0, x, pltpu.roll(x, 1, 1))
        lower = jnp.where(place == half - 1, x, pltpu.roll(x, LANES - 1, 1))
        cross = sign * pltpu.roll(x + rows_ref[...], half, 1)
        mixed = upper + lower - 2.0 * x
        out_ref[slot] = wet[:, slot : slot + 1] * (x + DT_OCEAN * (cross + MIXING * mixed))


def wave_program(ids, pair_rows, coefs, speeds, below, above, surface, near, weights, wet, *pieces):
    f32 = jnp.float32
    count = len(pieces)
    rows, columns = wet.shape
    bins = speeds.shape[1]
    return call(
        functools.partial(wave_kernel, count),
        jax.ShapeDtypeStruct((rows, bins, columns), jnp.bfloat16),
        [in_smem(), in_hbm()] + [in_vmem()] * (8 + count),
        in_hbm(),
        [
            SMEM(pair_rows.shape, jnp.int32),
            VMEM((rows, bins, columns), jnp.bfloat16),
            VMEM((bins * 8, LANES), f32),
            VMEM((40, columns), f32),
            pltpu.SemaphoreType.DMA,
            pltpu.SemaphoreType.DMA((12,)),
        ]
        + [VMEM((bins * 8, LANES), f32)] * ACCS,
        40_000_000,
        8_000_000,
        (ids, pair_rows, coefs, speeds, below, above, surface, near, weights, wet, *pieces),
        WAVE_LIMIT,
    )


def per_device(
    spectrum,
    group_speed,
    stokes_kernel,
    pair_bins,
    pair_coef,
    currents,
    col_map,
    wave_wet,
    ocean_wet,
):
    local_bins, tile_rows, columns = spectrum.shape
    space_count = lax.axis_size("space")
    bins_count = lax.axis_size("bins")
    devices = space_count * bins_count
    rows = tile_rows // bins_count
    bins = local_bins * bins_count
    pairs = pair_bins.shape[1]
    both = ("space", "bins")
    f32 = jnp.float32
    bf16 = jnp.bfloat16
    space_at = lax.axis_index("space")
    bins_at = lax.axis_index("bins")

    near_ids = [lax.rem(bins_at + step, bins_count) for step in (bins_count - 1, 1)]
    ids = jnp.stack([bins_at, *near_ids]).astype(jnp.int32)

    order = (4, 5, 2, 3, 6, 7, 1, 0)
    piece_shape = (CHUNKS, local_bins, LANES)
    sent = call(
        functools.partial(pack_kernel, order),
        [jax.ShapeDtypeStruct(piece_shape, bf16)] * bins_count,
        [in_smem(), in_hbm(), in_hbm()],
        [in_vmem()] * bins_count,
        [
            VMEM(spectrum.shape, bf16),
            VMEM((2, local_bins * tile_rows, LANES), f32),
            pltpu.SemaphoreType.DMA((3,)),
            pltpu.SemaphoreType.DMA((bins_count,)),
        ],
        2_000_000,
        4_000_000,
        (
            ids,
            pltpu.with_memory_space_constraint(spectrum, pltpu.HBM),
            pltpu.with_memory_space_constraint(stokes_kernel, pltpu.HBM),
        ),
    )
    pieces = [sent[0]] * bins_count
    for turn in order[:-1]:
        partners = [(at, at ^ turn) for at in range(bins_count)]
        pieces[turn] = lax.ppermute(sent[turn], "bins", partners)

    piece = local_bins // space_count
    speeds = lax.dynamic_slice(group_speed, (0, space_at * piece), (2, piece)).reshape(1, -1)
    speeds = jnp.pad(speeds, ((0, 0), (SPEED_LANE, LANES - SPEED_LANE - 2 * piece)))
    surface = call(
        surface_kernel,
        jax.ShapeDtypeStruct((devices, LANES), f32),
        [in_vmem()] * 3,
        in_vmem(),
        [VMEM((2 * ROW_GAP, LANES), f32)],
        4_000_000,
        500_000,
        (currents, ocean_wet, speeds),
    )
    arrived = lax.all_to_all(surface, both, split_axis=0, concat_axis=0, tiled=True)
    map_row = col_map.reshape(1, -1)
    surface_rows, speed_rows, coefs = call(
        tables_kernel,
        (
            jax.ShapeDtypeStruct((32, columns), f32),
            jax.ShapeDtypeStruct((2, bins, LANES), f32),
            jax.ShapeDtypeStruct((pairs, LANES), f32),
        ),
        [in_vmem()] * 3,
        (in_vmem(),) * 3,
        [],
        600_000_000,
        1_300_000,
        (arrived.reshape(devices, LANES), map_row, pair_coef.reshape(-1, LANES)),
    )

    pair_rows = pair_bins.reshape(-1) * 8

    ahead = [(at, at + 1) for at in range(devices - 1)]
    back = [(at + 1, at) for at in range(devices - 1)]
    halo_shape = (bins_count, 2, local_bins, LANES)
    last_rows, first_rows = call(
        edges_kernel,
        [jax.ShapeDtypeStruct(halo_shape, bf16)] * 2,
        [in_vmem()] * bins_count,
        [in_vmem()] * 2,
        [],
        1_000_000,
        2_400_000,
        tuple(pieces),
    )
    below = lax.ppermute(last_rows, both, ahead)
    above = lax.ppermute(first_rows, both, back)

    routed, near, weights = call(
        functools.partial(drift_kernel, bins_count),
        (
            jax.ShapeDtypeStruct((devices * 8, LANES), bf16),
            jax.ShapeDtypeStruct((16, columns), f32),
            jax.ShapeDtypeStruct((32, bins), bf16),
        ),
        [in_smem(), in_vmem()] + [in_vmem()] * bins_count,
        (in_vmem(),) * 3,
        [VMEM((devices * 8, LANES), f32), VMEM((bins_count, local_bins, LANES), bf16)],
        300_000_000,
        2_500_000,
        (ids, map_row, *pieces),
    )
    routed = lax.all_to_all(
        routed.reshape(devices, 8, LANES), both, split_axis=0, concat_axis=0, tiled=True
    )
    routed = routed.reshape(devices * 8, LANES)

    own_wet = lax.dynamic_slice(wave_wet, (bins_at * rows, 0), (rows, columns))
    new_spectrum = wave_program(
        ids,
        pair_rows,
        coefs,
        speed_rows,
        below,
        above,
        surface_rows,
        near,
        weights,
        own_wet,
        *pieces,
    )
    new_currents = call(
        ocean_kernel,
        jax.ShapeDtypeStruct(currents.shape, f32),
        [in_vmem()] * 3,
        in_vmem(),
        [VMEM((devices * 8, LANES), f32), VMEM((currents.shape[1], LANES), f32)],
        4_000_000,
        1_500_000,
        (currents, routed, ocean_wet),
    )
    return (jnp.transpose(new_spectrum, (1, 0, 2)), new_currents)


def solution(mesh):
    placed = (
        P("bins", "space", None),
        P(None, "bins"),
        P("bins", None),
        P(),
        P(),
        P(("space", "bins"), None, None),
        P(),
        P("space", None),
        P(("space", "bins"), None),
    )

    return jax.shard_map(
        per_device,
        mesh=mesh,
        in_specs=placed,
        out_specs=(P(None, ("space", "bins"), None), P(("space", "bins"), None, None)),
        check_vma=False,
    )
```

```python
import functools

import jax
import jax.numpy as jnp
from jax import lax
from jax.experimental import pallas as pl
from jax.experimental.pallas import tpu as pltpu
from jax.sharding import PartitionSpec as P


DT_OCEAN = 0.5
CORIOLIS = 0.8
MIXING = 0.4
CURRENT_SCALE = 0.15
DT_SOURCE = 0.5

LANES = 128
ACCS = 3
WAVE_LIMIT = 36
CHUNKS = 7
UNROLL = 48
BLOCK = 16
PITCH = 24
ROW_GAP = 400
SPEED_LANE = 32
PIECES = 16
HIGHEST = lax.Precision.HIGHEST
VMEM = pltpu.VMEM
SMEM = pltpu.SMEM


def in_vmem():
    return pl.BlockSpec(memory_space=VMEM)


def in_smem():
    return pl.BlockSpec(memory_space=SMEM)


def in_hbm():
    return pl.BlockSpec(memory_space=pltpu.HBM)


def kept_in(space, *values):
    return [pltpu.with_memory_space_constraint(value, space) for value in values]


def call(body, out_shape, ins, outs, scratch, flops, moved, args, limit=16):
    return pl.pallas_call(
        body,
        out_shape=out_shape,
        in_specs=ins,
        out_specs=outs,
        scratch_shapes=scratch,
        compiler_params=pltpu.CompilerParams(vmem_limit_bytes=limit * 2**20),
        cost_estimate=pl.CostEstimate(flops=flops, bytes_accessed=moved, transcendentals=0),
    )(*args)


def pack_kernel(order, ids_ref, spectrum_hbm, stokes_hbm, *refs):
    count = len(order)
    out_refs = refs[:count]
    narrow_ref, wide_ref, in_sems, stokes_sems = refs[count:]
    local_bins, tile_rows, _ = spectrum_hbm.shape
    rows = tile_rows // count
    chunks = in_sems.shape[0]
    part = local_bins // chunks
    loads = []
    for chunk in range(chunks):
        span = pl.ds(chunk * part, part)
        loads.append(
            pltpu.make_async_copy(spectrum_hbm.at[span], narrow_ref.at[span], in_sems.at[chunk])
        )
        loads[-1].start()
    stokes = [
        pltpu.make_async_copy(stokes_hbm, out_refs[turn].at[6], stokes_sems.at[turn])
        for turn in range(count)
    ]
    for copy in stokes:
        copy.start()
    own = ids_ref[0]
    for chunk in range(chunks):
        loads[chunk].wait()
        first = chunk * part
        for half in range(2):
            lanes = slice(half * LANES, (half + 1) * LANES)
            value = narrow_ref[first : first + part, :, lanes].astype(jnp.float32)
            wide_ref[half, first * tile_rows : (first + part) * tile_rows] = value.reshape(
                part * tile_rows, LANES
            )
        for turn in order:
            base = (own ^ turn) * rows + first * tile_rows
            for row in range(rows):
                for half in range(2):
                    value = wide_ref[half, pl.ds(base + row, part, stride=tile_rows), :]
                    out_refs[turn][2 * row + half, first : first + part, :] = value.astype(
                        jnp.bfloat16
                    )
    for copy in stokes:
        copy.wait()


def joined(refs, chunk):
    return jnp.concatenate([ref[chunk] for ref in refs], axis=0)


def edges_kernel(*refs):
    last_ref, first_ref = refs[-2:]
    for turn, ref in enumerate(refs[:-2]):
        last_ref[turn] = ref[4:6]
        first_ref[turn] = ref[0:2]


def wet_columns(wet_ref):
    wet = wet_ref[...].astype(jnp.float32)
    rows = wet.shape[1]
    return jnp.concatenate([wet, jnp.zeros((6, rows), jnp.float32)], axis=0).T


def surface_kernel(ids_ref, currents_ref, wet_ref, speed_ref, out_ref, rows_ref):
    rows = currents_ref.shape[1]
    half = LANES // 2
    lane = lax.broadcasted_iota(jnp.int32, (rows, LANES), 1)
    wet = wet_columns(wet_ref)
    sign = jnp.where(lane < half, CORIOLIS, -CORIOLIS)
    kept = (lane == 0) | (lane == 1) | (lane == half)
    rows_ref[...] = jnp.zeros_like(rows_ref)
    for slot in range(2):
        x = currents_ref[slot]
        cross = sign * pltpu.roll(x, half, 1)
        below = pltpu.roll(x, LANES - 1, 1)
        column = wet[:, slot : slot + 1]
        value = column * (x + DT_OCEAN * (cross + MIXING * (below - x)))
        value = jnp.where(lane == 1, column, value)
        rows_ref[pl.ds(slot * ROW_GAP + 8, rows), :] = jnp.where(kept, value, 0.0)
    local_bins = speed_ref.shape[1]
    piece = local_bins // PIECES
    index = lax.broadcasted_iota(jnp.int32, (local_bins, LANES), 0) - ids_ref[3] * piece
    place = lax.broadcasted_iota(jnp.int32, (local_bins, LANES), 1) - SPEED_LANE
    inside = (index >= 0) & (index < piece)
    speeds = jnp.zeros((1, LANES), jnp.float32)
    for part in range(2):
        pick = (inside & (place == index + part * piece)).astype(jnp.float32)
        speeds = speeds + jnp.dot(
            speed_ref[part : part + 1, :],
            pick,
            precision=HIGHEST,
            preferred_element_type=jnp.float32,
        )
    total = jnp.broadcast_to(speeds, (LANES, LANES))
    for slot in range(2):
        for row in range(5):
            part = rows_ref[pl.ds(slot * ROW_GAP + 7 + row, LANES, stride=3), :]
            shift = 2 * (slot * 5 + row)
            total = total + (pltpu.roll(part, shift, 1) if shift else part)
    out_ref[...] = total


def columns_of(map_ref):
    row = jnp.broadcast_to(map_ref[...].astype(jnp.float32), (LANES, LANES))
    column = row.T
    return jnp.concatenate([column, column], axis=1)


def chosen(column, slot):
    index = lax.broadcasted_iota(jnp.int32, column.shape, 1).astype(jnp.float32)
    return (2.0 * column + float(slot)) == index


def tables_kernel(
    recv_ref, map_ref, coef_ref, pair_ref, surface_ref, speeds_ref, coefs_ref, rows_ref
):
    for block in range(coef_ref.shape[0]):
        lanes = slice(block * LANES, (block + 1) * LANES)
        for side in range(3):
            at = side * coef_ref.shape[0] + block
            rows_ref[at : at + 1, :] = pair_ref[side : side + 1, lanes] * 8
        row = DT_SOURCE * coef_ref[block : block + 1, :]
        coefs_ref[block * LANES : (block + 1) * LANES, :] = jnp.broadcast_to(
            row, (LANES, LANES)
        ).T
    recv = recv_ref[...]
    turned = recv.T
    column = columns_of(map_ref)
    parts = []
    for slot in range(2):
        pick = chosen(column, slot).astype(jnp.float32)
        parts.append(jnp.dot(turned, pick, precision=HIGHEST, preferred_element_type=jnp.float32))
    surface_ref[...] = jnp.zeros_like(surface_ref)
    surface_ref[0:10, :] = parts[0][0:10] + parts[1][10:20]
    surface_ref[16:26, :] = parts[0][64:74] + parts[1][74:84]
    bins = speeds_ref.shape[1]
    lane = lax.broadcasted_iota(jnp.int32, (bins, LANES), 1)
    index = lax.broadcasted_iota(jnp.int32, (bins, LANES), 0)
    first = ((lane & 7) * 16 + (lane >> 3)) * 9
    own = (index >= first) & (index < first + 9)
    rows = jnp.dot(
        own.astype(jnp.float32), recv, precision=HIGHEST, preferred_element_type=jnp.float32
    )
    place = index - ((index * 7282) >> 16) * 9
    ones = jnp.ones((LANES, LANES), jnp.float32)
    for part in range(2):
        value = jnp.where(lane == place + (SPEED_LANE + 9 * part), rows, 0.0)
        speeds_ref[part] = jnp.dot(
            value, ones, precision=HIGHEST, preferred_element_type=jnp.float32
        )


def drift_kernel(count, ids_ref, map_ref, *refs):
    piece_refs = refs[:count]
    routed_ref, near_ref, weights_ref, rows_ref, stokes_ref = refs[count:]
    own = ids_ref[0]
    for turn, ref in enumerate(piece_refs):
        stokes_ref[own ^ turn] = ref[6]
    in_order = stokes_ref[...].reshape(-1, LANES).T
    weights_ref[0:16, :] = in_order[0:16]
    weights_ref[16:32, :] = in_order[64:80]
    turned = joined(piece_refs, 6).T
    column = columns_of(map_ref)
    picks = [chosen(column, slot).astype(jnp.float32).astype(jnp.bfloat16) for slot in range(2)]
    rows_ref[...] = jnp.zeros_like(rows_ref)
    near_ref[...] = jnp.zeros_like(near_ref)
    for row in range(3):
        parts = [jnp.zeros((LANES, LANES), jnp.float32) for _ in range(2)]
        for half in range(2):
            cells = joined(piece_refs, 2 * row + half)
            drift = jnp.dot(turned, cells, preferred_element_type=jnp.float32)
            lanes = slice(half * LANES, (half + 1) * LANES)
            near_ref[row : row + 1, lanes] = drift[0:1]
            near_ref[8 + row : 9 + row, lanes] = drift[64:65]
            narrow = drift.astype(jnp.bfloat16)
            for slot in range(2):
                parts[slot] = parts[slot] + lax.dot_general(
                    picks[slot][:, lanes],
                    narrow,
                    (((1,), (1,)), ((), ())),
                    preferred_element_type=jnp.float32,
                )
        for slot in range(2):
            rows_ref[pl.ds(slot * 3 + row, LANES, stride=8), :] = parts[slot]
    routed_ref[...] = rows_ref[...].astype(jnp.bfloat16)


def wave_kernel(
    count,
    ids_ref,
    pair_hbm,
    coef_hbm,
    speeds_hbm,
    below_hbm,
    above_hbm,
    surface_ref,
    near_ref,
    weights_ref,
    wet_ref,
    *refs,
):
    piece_refs = refs[:count]
    (
        out_hbm,
        pair_ref,
        coef_ref,
        speeds_ref,
        below_ref,
        above_ref,
        out_ref,
        field_ref,
        cur_ref,
        turn_ref,
        beside_ref,
        in_sems,
        out_sems,
        *acc_refs,
    ) = refs[count:]
    local_bins = piece_refs[0].shape[1]
    bins = count * local_bins
    pairs = coef_ref.shape[0]

    moves = (
        (below_hbm, below_ref),
        (above_hbm, above_ref),
        (speeds_hbm, speeds_ref),
        (pair_hbm, pair_ref),
        (coef_hbm, coef_ref),
    )
    loads = [
        pltpu.make_async_copy(src, dst, in_sems.at[at]) for at, (src, dst) in enumerate(moves)
    ]
    for copy in loads:
        copy.start()
    own = ids_ref[0]
    turn_ref[...] = jnp.zeros_like(turn_ref)

    columns = 2 * LANES
    given = lax.broadcasted_iota(jnp.int32, (columns, 2 * columns), 0)
    taken = lax.broadcasted_iota(jnp.int32, (columns, 2 * columns), 1)
    pick = given == jnp.where(taken < columns, taken - 1, taken - columns + 1)
    pick = pick.astype(jnp.float32)
    narrow_pick = pick.astype(jnp.bfloat16)
    for row in range(3):
        cells = jnp.concatenate(
            [joined(piece_refs, 2 * row), joined(piece_refs, 2 * row + 1)], axis=1
        )
        beside = jnp.dot(cells, narrow_pick, preferred_element_type=jnp.float32)
        for part in range(4):
            beside_ref[row, part] = beside[:, part * LANES : (part + 1) * LANES].astype(
                jnp.bfloat16
            )

    loads[0].wait()
    loads[1].wait()
    weights = weights_ref[...]
    for side, ref in enumerate((below_ref, above_ref)):
        for half in range(2):
            blocks = [ref[ids_ref[1 + side] ^ block, half] for block in range(count)]
            cells = jnp.concatenate(blocks, axis=0)
            drift = jnp.dot(weights, cells, preferred_element_type=jnp.float32)
            lanes = slice(half * LANES, (half + 1) * LANES)
            cur_ref[24 + side : 25 + side, lanes] = drift[0:1]
            cur_ref[32 + side : 33 + side, lanes] = drift[16:17]
    for row in range(5):
        if row in (0, 4):
            side = 0 if row == 0 else 1
            east = cur_ref[24 + side : 25 + side, :]
            north = cur_ref[32 + side : 33 + side, :]
        else:
            east = near_ref[row - 1 : row, :]
            north = near_ref[8 + row - 1 : 8 + row, :]
        fixed_east = surface_ref[2 * row : 2 * row + 1, :]
        wet = surface_ref[2 * row + 1 : 2 * row + 2, :]
        fixed_north = surface_ref[16 + 2 * row : 17 + 2 * row, :]
        factor = (DT_OCEAN * CORIOLIS) * wet
        cur_ref[row : row + 1, :] = CURRENT_SCALE * jnp.tanh(fixed_east + factor * north)
        cur_ref[8 + row : 9 + row, :] = CURRENT_SCALE * jnp.tanh(fixed_north - factor * east)
    for row in range(3):
        wet = wet_ref[pl.ds(own * 3 + row, 1), :]
        cur_ref[16 + row : 17 + row, :] = wet.astype(jnp.float32)

    near_cur = jnp.dot(
        cur_ref[8:16, :], pick, precision=HIGHEST, preferred_element_type=jnp.float32
    )
    cur_ref[40:48, :] = near_cur[:, :columns]
    cur_ref[48:56, :] = near_cur[:, columns:]
    loads[2].wait()

    def advect(piece_ref, turn, block, step):
        start = pl.multiple_of(step * BLOCK, BLOCK)
        first = block * local_bins + start
        span = pl.ds(start, BLOCK)
        below_at = ids_ref[1] ^ block
        above_at = ids_ref[2] ^ block
        speed_x = speeds_ref[0, pl.ds(pl.multiple_of(first, BLOCK), BLOCK), :]
        speed_y = speeds_ref[1, pl.ds(pl.multiple_of(first, BLOCK), BLOCK), :]

        def row_flux(energy, row, half):
            current = cur_ref[row : row + 1, half * LANES : (half + 1) * LANES]
            return (speed_x + current) * energy

        energy = [
            [piece_ref[2 * row + half, span, :].astype(jnp.float32) for half in range(2)]
            for row in range(3)
        ]
        for half in range(2):
            flux = [row_flux(below_ref[below_at, half, span, :].astype(jnp.float32), 0, half)]
            flux += [row_flux(energy[row][half], row + 1, half) for row in range(3)]
            flux += [row_flux(above_ref[above_at, half, span, :].astype(jnp.float32), 4, half)]
            for row in range(3):
                energy[row][half] = (
                    energy[row][half],
                    energy[row][half]
                    - jnp.abs(flux[row + 1])
                    + jnp.maximum(flux[row], 0.0)
                    - jnp.minimum(flux[row + 2], 0.0),
                )
        for row in range(3):
            for half in range(2):
                old, value = energy[row][half]
                lanes = slice(half * LANES, (half + 1) * LANES)
                spot = pl.ds(pl.multiple_of(turn * local_bins + start, BLOCK), BLOCK)

                def side(at, cells, row=row, lanes=lanes):
                    return (speed_y + cur_ref[at + 1 + row : at + 2 + row, lanes]) * cells

                left = side(40, beside_ref[row, half, spot, :].astype(jnp.float32))
                right = side(48, beside_ref[row, 2 + half, spot, :].astype(jnp.float32))
                wet = cur_ref[16 + row : 17 + row, lanes]
                moved = value - jnp.abs(side(8, old))
                result = wet * (moved + jnp.maximum(left, 0.0) - jnp.minimum(right, 0.0))
                at = (2 * row + half) * PITCH
                turn_ref[at : at + BLOCK, :] = result
        zeros = jnp.zeros((8, LANES), jnp.float32)
        for item in range(BLOCK):
            rows = pl.ds(pl.multiple_of((first + item) * 8, 8), 8)
            tile = turn_ref[pl.ds(item, 8, stride=PITCH), :]
            field_ref[rows, :] = tile
            acc_refs[0][rows, :] = tile
            for ref in acc_refs[1:]:
                ref[rows, :] = zeros

    for turn, piece_ref in enumerate(piece_refs):
        block = own ^ turn

        def one(step, carry, piece_ref=piece_ref, turn=turn, block=block):
            advect(piece_ref, turn, block, step)
            return carry

        lax.fori_loop(0, local_bins // BLOCK, one, 0)
    loads[3].wait()
    loads[4].wait()

    def interact(step, carry):
        start = pl.multiple_of(step * UNROLL, UNROLL)
        firsts = pair_ref.at[pl.ds(start, UNROLL)]
        seconds = pair_ref.at[pl.ds(pairs + start, UNROLL)]
        targets = pair_ref.at[pl.ds(2 * pairs + start, UNROLL)]
        coefs = coef_ref.at[pl.ds(start, UNROLL)]
        for item in range(UNROLL):
            first = pl.ds(pl.multiple_of(firsts[item], 8), 8)
            second = pl.ds(pl.multiple_of(seconds[item], 8), 8)
            target = pl.ds(pl.multiple_of(targets[item], 8), 8)
            ref = acc_refs[item % ACCS]
            product = coefs[item : item + 1, :] * (field_ref[first, :] * field_ref[second, :])
            ref[target, :] = ref[target, :] + product
        return carry

    lax.fori_loop(0, pairs // UNROLL, interact, 0)

    def finish(step, carry):
        first = pl.multiple_of(step * BLOCK, BLOCK)
        for row in range(3):
            for half in range(2):
                rows = pl.ds(first * 8 + (2 * row + half), BLOCK, stride=8)
                total = acc_refs[0][rows, :]
                for ref in acc_refs[1:]:
                    total = total + ref[rows, :]
                out_ref[row, pl.ds(first, BLOCK), half * LANES : (half + 1) * LANES] = (
                    total.astype(jnp.bfloat16)
                )
        return carry

    parts = 4
    out_copies = []
    for part in range(parts):
        span = pl.ds(part * (bins // parts), bins // parts)
        each = bins // BLOCK // parts
        lax.fori_loop(part * each, (part + 1) * each, finish, 0)
        for row in range(3):
            out_copies.append(
                pltpu.make_async_copy(
                    out_ref.at[row, span], out_hbm.at[row, span], out_sems.at[3 * part + row]
                )
            )
            out_copies[-1].start()
    for copy in out_copies:
        copy.wait()


def ocean_kernel(currents_ref, recv_ref, wet_ref, out_ref, wide_ref, rows_ref):
    rows = currents_ref.shape[1]
    half = LANES // 2
    lane = lax.broadcasted_iota(jnp.int32, (rows, LANES), 1)
    place = lane & (half - 1)
    sign = jnp.where(lane < half, CORIOLIS, -CORIOLIS)
    wet = wet_columns(wet_ref)
    wide_ref[...] = recv_ref[...].astype(jnp.float32)
    for slot in range(2):
        for row in range(3):
            rows_ref[pl.ds(row, LANES, stride=3), :] = wide_ref[
                pl.ds(slot * 3 + row, LANES, stride=8), :
            ]
        x = currents_ref[slot]
        upper = jnp.where(place == 0, x, pltpu.roll(x, 1, 1))
        lower = jnp.where(place == half - 1, x, pltpu.roll(x, LANES - 1, 1))
        cross = sign * pltpu.roll(x + rows_ref[...], half, 1)
        mixed = upper + lower - 2.0 * x
        out_ref[slot] = wet[:, slot : slot + 1] * (x + DT_OCEAN * (cross + MIXING * mixed))


def wave_program(ids, pair_rows, coefs, speeds, below, above, surface, near, weights, wet, *pieces):
    f32 = jnp.float32
    count = len(pieces)
    columns = wet.shape[1]
    rows = wet.shape[0] // count
    bins = speeds.shape[1]
    return call(
        functools.partial(wave_kernel, count),
        jax.ShapeDtypeStruct((rows, bins, columns), jnp.bfloat16),
        [in_smem()] + [in_hbm()] * 5 + [in_vmem()] * (4 + count),
        in_hbm(),
        [
            SMEM(pair_rows.shape, jnp.int32),
            VMEM(coefs.shape, f32),
            VMEM(speeds.shape, f32),
            VMEM(below.shape, jnp.bfloat16),
            VMEM(above.shape, jnp.bfloat16),
            VMEM((rows, bins, columns), jnp.bfloat16),
            VMEM((bins * 8, LANES), f32),
            VMEM((56, columns), f32),
            VMEM((8 * PITCH, LANES), f32),
            VMEM((rows, 4, bins, LANES), jnp.bfloat16),
            pltpu.SemaphoreType.DMA((5,)),
            pltpu.SemaphoreType.DMA((12,)),
        ]
        + [VMEM((bins * 8, LANES), f32)] * ACCS,
        40_000_000,
        8_000_000,
        (
            ids,
            *kept_in(pltpu.HBM, pair_rows, coefs, speeds, below, above),
            surface,
            near,
            weights,
            wet,
            *kept_in(VMEM, *pieces),
        ),
        WAVE_LIMIT,
    )


def per_device(
    spectrum,
    group_speed,
    stokes_kernel,
    pair_bins,
    pair_coef,
    currents,
    col_map,
    wave_wet,
    ocean_wet,
):
    local_bins, tile_rows, columns = spectrum.shape
    space_count = lax.axis_size("space")
    bins_count = lax.axis_size("bins")
    devices = space_count * bins_count
    bins = local_bins * bins_count
    pairs = pair_bins.shape[1]
    both = ("space", "bins")
    f32 = jnp.float32
    bf16 = jnp.bfloat16
    space_at = lax.axis_index("space")
    bins_at = lax.axis_index("bins")

    near_ids = [lax.rem(bins_at + step, bins_count) for step in (bins_count - 1, 1)]
    ids = jnp.stack([bins_at, *near_ids, space_at]).astype(jnp.int32)

    order = (4, 5, 2, 6, 3, 7, 1, 0)
    piece_shape = (CHUNKS, local_bins, LANES)
    sent = call(
        functools.partial(pack_kernel, order),
        [jax.ShapeDtypeStruct(piece_shape, bf16)] * bins_count,
        [in_smem(), in_hbm(), in_hbm()],
        [in_vmem()] * bins_count,
        [
            VMEM(spectrum.shape, bf16),
            VMEM((2, local_bins * tile_rows, LANES), f32),
            pltpu.SemaphoreType.DMA((3,)),
            pltpu.SemaphoreType.DMA((bins_count,)),
        ],
        2_000_000,
        4_000_000,
        (
            ids,
            pltpu.with_memory_space_constraint(spectrum, pltpu.HBM),
            pltpu.with_memory_space_constraint(stokes_kernel, pltpu.HBM),
        ),
    )
    pieces = [sent[0]] * bins_count
    for turn in order[:-1]:
        partners = [(at, at ^ turn) for at in range(bins_count)]
        pieces[turn] = lax.ppermute(sent[turn], "bins", partners)

    surface = call(
        surface_kernel,
        jax.ShapeDtypeStruct((devices, LANES), f32),
        [in_smem()] + [in_vmem()] * 3,
        in_vmem(),
        [VMEM((2 * ROW_GAP, LANES), f32)],
        4_000_000,
        500_000,
        (ids, currents, ocean_wet, group_speed),
    )
    arrived = lax.all_to_all(surface, both, split_axis=0, concat_axis=0, tiled=True)
    map_row = col_map.reshape(1, -1)
    surface_rows, speed_rows, coefs, pair_rows = call(
        tables_kernel,
        (
            jax.ShapeDtypeStruct((32, columns), f32),
            jax.ShapeDtypeStruct((2, bins, LANES), f32),
            jax.ShapeDtypeStruct((pairs, LANES), f32),
            jax.ShapeDtypeStruct((3 * pairs // LANES, LANES), jnp.int32),
        ),
        [in_vmem()] * 4,
        (in_vmem(),) * 4,
        [],
        600_000_000,
        1_300_000,
        (arrived.reshape(devices, LANES), map_row, pair_coef.reshape(-1, LANES), pair_bins),
    )

    ahead = [(at, at + 1) for at in range(devices - 1)]
    back = [(at + 1, at) for at in range(devices - 1)]
    halo_shape = (bins_count, 2, local_bins, LANES)
    last_rows, first_rows = call(
        edges_kernel,
        [jax.ShapeDtypeStruct(halo_shape, bf16)] * 2,
        [in_vmem()] * bins_count,
        [in_vmem()] * 2,
        [],
        1_000_000,
        2_400_000,
        tuple(pieces),
    )
    below = lax.ppermute(last_rows, both, ahead)
    above = lax.ppermute(first_rows, both, back)

    routed, near, weights = call(
        functools.partial(drift_kernel, bins_count),
        (
            jax.ShapeDtypeStruct((devices * 8, LANES), bf16),
            jax.ShapeDtypeStruct((16, columns), f32),
            jax.ShapeDtypeStruct((32, bins), bf16),
        ),
        [in_smem(), in_vmem()] + [in_vmem()] * bins_count,
        (in_vmem(),) * 3,
        [VMEM((devices * 8, LANES), f32), VMEM((bins_count, local_bins, LANES), bf16)],
        300_000_000,
        2_500_000,
        (ids, map_row, *pieces),
    )
    routed = lax.all_to_all(
        routed.reshape(devices, 8, LANES), both, split_axis=0, concat_axis=0, tiled=True
    )
    routed = routed.reshape(devices * 8, LANES)

    new_spectrum = wave_program(
        ids,
        pair_rows.reshape(-1),
        coefs,
        speed_rows,
        below,
        above,
        surface_rows,
        near,
        weights,
        wave_wet,
        *pieces,
    )
    new_currents = call(
        ocean_kernel,
        jax.ShapeDtypeStruct(currents.shape, f32),
        [in_vmem()] * 3,
        in_vmem(),
        [VMEM((devices * 8, LANES), f32), VMEM((currents.shape[1], LANES), f32)],
        4_000_000,
        1_500_000,
        (currents, routed, ocean_wet),
    )
    return (jnp.transpose(new_spectrum, (1, 0, 2)), new_currents)


def solution(mesh):
    placed = (
        P("bins", "space", None),
        P(None, "bins"),
        P("bins", None),
        P(),
        P(),
        P(("space", "bins"), None, None),
        P(),
        P("space", None),
        P(("space", "bins"), None),
    )

    return jax.shard_map(
        per_device,
        mesh=mesh,
        in_specs=placed,
        out_specs=(P(None, ("space", "bins"), None), P(("space", "bins"), None, None)),
        check_vma=False,
    )
```

```python
import functools

import jax
import jax.numpy as jnp
from jax import lax
from jax.experimental import pallas as pl
from jax.experimental.pallas import tpu as pltpu
from jax.sharding import PartitionSpec as P


DT_OCEAN = 0.5
CORIOLIS = 0.8
MIXING = 0.4
CURRENT_SCALE = 0.15
DT_SOURCE = 0.5

LANES = 128
ACCS = 3
WAVE_LIMIT = 36
CHUNKS = 7
UNROLL = 48
BLOCK = 16
PITCH = 24
ROW_GAP = 400
SPEED_LANE = 32
PIECES = 16
HIGHEST = lax.Precision.HIGHEST
VMEM = pltpu.VMEM
SMEM = pltpu.SMEM


def in_vmem():
    return pl.BlockSpec(memory_space=VMEM)


def in_smem():
    return pl.BlockSpec(memory_space=SMEM)


def anywhere():
    return pl.BlockSpec(memory_space=pl.ANY)


def in_hbm():
    return pl.BlockSpec(memory_space=pltpu.HBM)


def kept_in(space, *values):
    return [pltpu.with_memory_space_constraint(value, space) for value in values]


def call(body, out_shape, ins, outs, scratch, flops, moved, args, limit=16):
    return pl.pallas_call(
        body,
        out_shape=out_shape,
        in_specs=ins,
        out_specs=outs,
        scratch_shapes=scratch,
        compiler_params=pltpu.CompilerParams(vmem_limit_bytes=limit * 2**20),
        cost_estimate=pl.CostEstimate(flops=flops, bytes_accessed=moved, transcendentals=0),
    )(*args)


def pack_kernel(order, ids_ref, spectrum_hbm, stokes_hbm, *refs):
    count = len(order)
    out_refs = refs[:count]
    narrow_ref, wide_ref, stokes_ref, piece_ref, in_sems, out_sems = refs[count:]
    local_bins, tile_rows, _ = spectrum_hbm.shape
    rows = tile_rows // count
    chunks = in_sems.shape[0] - 1
    part = local_bins // chunks
    loads = []
    for chunk in range(chunks):
        span = pl.ds(chunk * part, part)
        loads.append(
            pltpu.make_async_copy(spectrum_hbm.at[span], narrow_ref.at[span], in_sems.at[chunk])
        )
    loads.append(pltpu.make_async_copy(stokes_hbm, stokes_ref, in_sems.at[chunks]))
    for copy in loads:
        copy.start()
    own = ids_ref[0]
    stores = []
    for chunk in range(chunks):
        loads[chunk].wait()
        first = chunk * part
        span = pl.ds(first, part)
        for half in range(2):
            lanes = slice(half * LANES, (half + 1) * LANES)
            value = narrow_ref[first : first + part, :, lanes].astype(jnp.float32)
            wide_ref[half, first * tile_rows : (first + part) * tile_rows] = value.reshape(
                part * tile_rows, LANES
            )
        for turn in order:
            base = (own ^ turn) * rows + first * tile_rows
            ref = piece_ref.at[turn - 1] if turn else out_refs[0]
            for row in range(rows):
                for half in range(2):
                    value = wide_ref[half, pl.ds(base + row, part, stride=tile_rows), :]
                    ref[2 * row + half, first : first + part, :] = value.astype(jnp.bfloat16)
            if turn:
                stores.append(
                    pltpu.make_async_copy(
                        piece_ref.at[turn - 1, pl.ds(0, 6), span],
                        out_refs[turn].at[pl.ds(0, 6), span],
                        out_sems.at[turn, chunk],
                    )
                )
                stores[-1].start()
        if chunk == 0:
            loads[chunks].wait()
            out_refs[0][6] = stokes_ref[...]
            for turn in range(1, count):
                stores.append(
                    pltpu.make_async_copy(
                        stokes_ref, out_refs[turn].at[6], out_sems.at[turn, chunks]
                    )
                )
                stores[-1].start()
    for copy in stores:
        copy.wait()


def joined(refs, chunk):
    return jnp.concatenate([ref[chunk] for ref in refs], axis=0)


def edges_kernel(ids_ref, *refs):
    inner_ref, outer_ref = refs[-2:]
    core = ids_ref[0] & 1
    for turn, ref in enumerate(refs[:-2]):
        inner_ref[turn] = ref[pl.ds(4 - 4 * core, 2)]
        outer_ref[turn] = ref[pl.ds(4 * core, 2)]


def wet_columns(wet_ref):
    wet = wet_ref[...].astype(jnp.float32)
    rows = wet.shape[1]
    return jnp.concatenate([wet, jnp.zeros((6, rows), jnp.float32)], axis=0).T


def surface_kernel(ids_ref, currents_ref, wet_ref, speed_ref, out_ref, rows_ref):
    rows = currents_ref.shape[1]
    half = LANES // 2
    lane = lax.broadcasted_iota(jnp.int32, (rows, LANES), 1)
    wet = wet_columns(wet_ref)
    sign = jnp.where(lane < half, CORIOLIS, -CORIOLIS)
    kept = (lane == 0) | (lane == 1) | (lane == half)
    rows_ref[...] = jnp.zeros_like(rows_ref)
    for slot in range(2):
        x = currents_ref[slot]
        cross = sign * pltpu.roll(x, half, 1)
        below = pltpu.roll(x, LANES - 1, 1)
        column = wet[:, slot : slot + 1]
        value = column * (x + DT_OCEAN * (cross + MIXING * (below - x)))
        value = jnp.where(lane == 1, column, value)
        rows_ref[pl.ds(slot * ROW_GAP + 8, rows), :] = jnp.where(kept, value, 0.0)
    local_bins = speed_ref.shape[1]
    piece = local_bins // PIECES
    index = lax.broadcasted_iota(jnp.int32, (local_bins, LANES), 0) - ids_ref[3] * piece
    place = lax.broadcasted_iota(jnp.int32, (local_bins, LANES), 1) - SPEED_LANE
    inside = (index >= 0) & (index < piece)
    speeds = jnp.zeros((1, LANES), jnp.float32)
    for part in range(2):
        pick = (inside & (place == index + part * piece)).astype(jnp.float32)
        speeds = speeds + jnp.dot(
            speed_ref[part : part + 1, :],
            pick,
            precision=HIGHEST,
            preferred_element_type=jnp.float32,
        )
    total = jnp.broadcast_to(speeds, (LANES, LANES))
    for slot in range(2):
        for row in range(5):
            part = rows_ref[pl.ds(slot * ROW_GAP + 7 + row, LANES, stride=3), :]
            shift = 2 * (slot * 5 + row)
            total = total + (pltpu.roll(part, shift, 1) if shift else part)
    out_ref[...] = total


def columns_of(map_ref):
    row = jnp.broadcast_to(map_ref[...].astype(jnp.float32), (LANES, LANES))
    column = row.T
    return jnp.concatenate([column, column], axis=1)


def chosen(column, slot):
    index = lax.broadcasted_iota(jnp.int32, column.shape, 1).astype(jnp.float32)
    return (2.0 * column + float(slot)) == index


def tables_kernel(
    recv_ref,
    map_ref,
    coef_ref,
    pair_ref,
    surface_ref,
    speeds_hbm,
    coefs_hbm,
    rows_ref,
    speeds_ref,
    coefs_ref,
    sems,
):
    blocks = coef_ref.shape[0]
    copies = []
    for block in range(blocks):
        lanes = slice(block * LANES, (block + 1) * LANES)
        for side in range(3):
            at = side * blocks + block
            rows_ref[at : at + 1, :] = pair_ref[side : side + 1, lanes] * 8
        row = DT_SOURCE * coef_ref[block : block + 1, :]
        coefs_ref[lanes, :] = jnp.broadcast_to(row, (LANES, LANES)).T
        if (block + 1) % (blocks // 4) == 0:
            span = pl.ds((block + 1 - blocks // 4) * LANES, blocks // 4 * LANES)
            copies.append(
                pltpu.make_async_copy(
                    coefs_ref.at[span], coefs_hbm.at[span], sems.at[len(copies)]
                )
            )
            copies[-1].start()
    recv = recv_ref[...]
    turned = recv.T
    column = columns_of(map_ref)
    parts = []
    for slot in range(2):
        pick = chosen(column, slot).astype(jnp.float32)
        parts.append(jnp.dot(turned, pick, precision=HIGHEST, preferred_element_type=jnp.float32))
    surface_ref[...] = jnp.zeros_like(surface_ref)
    surface_ref[0:10, :] = parts[0][0:10] + parts[1][10:20]
    surface_ref[16:26, :] = parts[0][64:74] + parts[1][74:84]
    bins = speeds_ref.shape[1]
    lane = lax.broadcasted_iota(jnp.int32, (bins, LANES), 1)
    index = lax.broadcasted_iota(jnp.int32, (bins, LANES), 0)
    first = ((lane & 7) * 16 + (lane >> 3)) * 9
    own = (index >= first) & (index < first + 9)
    rows = jnp.dot(
        own.astype(jnp.float32), recv, precision=HIGHEST, preferred_element_type=jnp.float32
    )
    place = index - ((index * 7282) >> 16) * 9
    ones = jnp.ones((LANES, LANES), jnp.float32)
    for part in range(2):
        value = jnp.where(lane == place + (SPEED_LANE + 9 * part), rows, 0.0)
        speeds_ref[part] = jnp.dot(
            value, ones, precision=HIGHEST, preferred_element_type=jnp.float32
        )
        copies.append(
            pltpu.make_async_copy(
                speeds_ref.at[part], speeds_hbm.at[part], sems.at[len(copies)]
            )
        )
        copies[-1].start()
    for copy in copies:
        copy.wait()


def drift_kernel(count, ids_ref, map_ref, *refs):
    piece_refs = refs[:count]
    routed_hbm, near_ref, weights_ref, rows_ref, stokes_ref, routed_ref, sems = refs[count:]
    own = ids_ref[0]
    for turn, ref in enumerate(piece_refs):
        stokes_ref[own ^ turn] = ref[6]
    in_order = stokes_ref[...].reshape(-1, LANES).T
    weights_ref[0:16, :] = in_order[0:16]
    weights_ref[16:32, :] = in_order[64:80]
    turned = joined(piece_refs, 6).T
    column = columns_of(map_ref)
    picks = [chosen(column, slot).astype(jnp.float32).astype(jnp.bfloat16) for slot in range(2)]
    rows_ref[...] = jnp.zeros_like(rows_ref)
    near_ref[...] = jnp.zeros_like(near_ref)
    for row in range(3):
        parts = [jnp.zeros((LANES, LANES), jnp.float32) for _ in range(2)]
        for half in range(2):
            cells = joined(piece_refs, 2 * row + half)
            drift = jnp.dot(turned, cells, preferred_element_type=jnp.float32)
            lanes = slice(half * LANES, (half + 1) * LANES)
            near_ref[row : row + 1, lanes] = drift[0:1]
            near_ref[8 + row : 9 + row, lanes] = drift[64:65]
            narrow = drift.astype(jnp.bfloat16)
            for slot in range(2):
                parts[slot] = parts[slot] + lax.dot_general(
                    picks[slot][:, lanes],
                    narrow,
                    (((1,), (1,)), ((), ())),
                    preferred_element_type=jnp.float32,
                )
        for slot in range(2):
            rows_ref[pl.ds(slot * 3 + row, LANES, stride=8), :] = parts[slot]
    parts = sems.shape[0]
    size = rows_ref.shape[0] // parts
    copies = []
    for part in range(parts):
        span = pl.ds(part * size, size)
        routed_ref[span, :] = rows_ref[span, :].astype(jnp.bfloat16)
        copies.append(
            pltpu.make_async_copy(routed_ref.at[span], routed_hbm.at[span], sems.at[part])
        )
        copies[-1].start()
    for copy in copies:
        copy.wait()


def wave_kernel(
    count,
    ids_ref,
    pair_hbm,
    coef_hbm,
    speeds_hbm,
    inner_hbm,
    outer_hbm,
    surface_ref,
    near_ref,
    weights_ref,
    wet_ref,
    *refs,
):
    piece_refs = refs[:count]
    (
        out_hbm,
        pair_ref,
        coef_ref,
        speeds_ref,
        halo_ref,
        out_ref,
        field_ref,
        cur_ref,
        turn_ref,
        beside_ref,
        in_sems,
        out_sems,
        *acc_refs,
    ) = refs[count:]
    local_bins = piece_refs[0].shape[1]
    bins = count * local_bins
    pairs = coef_ref.shape[0]

    core = ids_ref[0] & 1
    moves = (
        (inner_hbm, halo_ref.at[1 - core]),
        (outer_hbm, halo_ref.at[core]),
        (speeds_hbm, speeds_ref),
        (pair_hbm, pair_ref),
        (coef_hbm, coef_ref),
    )
    loads = [
        pltpu.make_async_copy(src, dst, in_sems.at[at]) for at, (src, dst) in enumerate(moves)
    ]
    for copy in loads:
        copy.start()
    own = ids_ref[0]
    turn_ref[...] = jnp.zeros_like(turn_ref)

    columns = 2 * LANES
    given = lax.broadcasted_iota(jnp.int32, (columns, 2 * columns), 0)
    taken = lax.broadcasted_iota(jnp.int32, (columns, 2 * columns), 1)
    pick = given == jnp.where(taken < columns, taken - 1, taken - columns + 1)
    pick = pick.astype(jnp.float32)
    narrow_pick = pick.astype(jnp.bfloat16)
    for row in range(3):
        cells = jnp.concatenate(
            [joined(piece_refs, 2 * row), joined(piece_refs, 2 * row + 1)], axis=1
        )
        beside = jnp.dot(cells, narrow_pick, preferred_element_type=jnp.float32)
        for part in range(4):
            beside_ref[row, part] = beside[:, part * LANES : (part + 1) * LANES].astype(
                jnp.bfloat16
            )

    loads[0].wait()
    loads[1].wait()
    weights = weights_ref[...]
    for side in range(2):
        for half in range(2):
            blocks = [halo_ref[side, ids_ref[1 + side] ^ block, half] for block in range(count)]
            cells = jnp.concatenate(blocks, axis=0)
            drift = jnp.dot(weights, cells, preferred_element_type=jnp.float32)
            lanes = slice(half * LANES, (half + 1) * LANES)
            cur_ref[24 + side : 25 + side, lanes] = drift[0:1]
            cur_ref[32 + side : 33 + side, lanes] = drift[16:17]
    for row in range(5):
        if row in (0, 4):
            side = 0 if row == 0 else 1
            east = cur_ref[24 + side : 25 + side, :]
            north = cur_ref[32 + side : 33 + side, :]
        else:
            east = near_ref[row - 1 : row, :]
            north = near_ref[8 + row - 1 : 8 + row, :]
        fixed_east = surface_ref[2 * row : 2 * row + 1, :]
        wet = surface_ref[2 * row + 1 : 2 * row + 2, :]
        fixed_north = surface_ref[16 + 2 * row : 17 + 2 * row, :]
        factor = (DT_OCEAN * CORIOLIS) * wet
        cur_ref[row : row + 1, :] = CURRENT_SCALE * jnp.tanh(fixed_east + factor * north)
        cur_ref[8 + row : 9 + row, :] = CURRENT_SCALE * jnp.tanh(fixed_north - factor * east)
    for row in range(3):
        wet = wet_ref[pl.ds(own * 3 + row, 1), :]
        cur_ref[16 + row : 17 + row, :] = wet.astype(jnp.float32)

    near_cur = jnp.dot(
        cur_ref[8:16, :], pick, precision=HIGHEST, preferred_element_type=jnp.float32
    )
    cur_ref[40:48, :] = near_cur[:, :columns]
    cur_ref[48:56, :] = near_cur[:, columns:]
    loads[2].wait()

    def advect(piece_ref, turn, block, step):
        start = pl.multiple_of(step * BLOCK, BLOCK)
        first = block * local_bins + start
        span = pl.ds(start, BLOCK)
        below_at = ids_ref[1] ^ block
        above_at = ids_ref[2] ^ block
        speed_x = speeds_ref[0, pl.ds(pl.multiple_of(first, BLOCK), BLOCK), :]
        speed_y = speeds_ref[1, pl.ds(pl.multiple_of(first, BLOCK), BLOCK), :]

        def row_flux(energy, row, half):
            current = cur_ref[row : row + 1, half * LANES : (half + 1) * LANES]
            return (speed_x + current) * energy

        energy = [
            [piece_ref[2 * row + half, span, :].astype(jnp.float32) for half in range(2)]
            for row in range(3)
        ]
        for half in range(2):
            flux = [row_flux(halo_ref[0, below_at, half, span, :].astype(jnp.float32), 0, half)]
            flux += [row_flux(energy[row][half], row + 1, half) for row in range(3)]
            flux += [row_flux(halo_ref[1, above_at, half, span, :].astype(jnp.float32), 4, half)]
            for row in range(3):
                energy[row][half] = (
                    energy[row][half],
                    energy[row][half]
                    - jnp.abs(flux[row + 1])
                    + jnp.maximum(flux[row], 0.0)
                    - jnp.minimum(flux[row + 2], 0.0),
                )
        for row in range(3):
            for half in range(2):
                old, value = energy[row][half]
                lanes = slice(half * LANES, (half + 1) * LANES)
                spot = pl.ds(pl.multiple_of(turn * local_bins + start, BLOCK), BLOCK)

                def side(at, cells, row=row, lanes=lanes):
                    return (speed_y + cur_ref[at + 1 + row : at + 2 + row, lanes]) * cells

                left = side(40, beside_ref[row, half, spot, :].astype(jnp.float32))
                right = side(48, beside_ref[row, 2 + half, spot, :].astype(jnp.float32))
                wet = cur_ref[16 + row : 17 + row, lanes]
                moved = value - jnp.abs(side(8, old))
                result = wet * (moved + jnp.maximum(left, 0.0) - jnp.minimum(right, 0.0))
                at = (2 * row + half) * PITCH
                turn_ref[at : at + BLOCK, :] = result
        zeros = jnp.zeros((8, LANES), jnp.float32)
        for item in range(BLOCK):
            rows = pl.ds(pl.multiple_of((first + item) * 8, 8), 8)
            tile = turn_ref[pl.ds(item, 8, stride=PITCH), :]
            field_ref[rows, :] = tile
            acc_refs[0][rows, :] = tile
            for ref in acc_refs[1:]:
                ref[rows, :] = zeros

    for turn, piece_ref in enumerate(piece_refs):
        block = own ^ turn

        def one(step, carry, piece_ref=piece_ref, turn=turn, block=block):
            advect(piece_ref, turn, block, step)
            return carry

        lax.fori_loop(0, local_bins // BLOCK, one, 0)
    loads[3].wait()
    loads[4].wait()

    def interact(step, carry):
        start = pl.multiple_of(step * UNROLL, UNROLL)
        firsts = pair_ref.at[pl.ds(start, UNROLL)]
        seconds = pair_ref.at[pl.ds(pairs + start, UNROLL)]
        targets = pair_ref.at[pl.ds(2 * pairs + start, UNROLL)]
        coefs = coef_ref.at[pl.ds(start, UNROLL)]
        for item in range(UNROLL):
            first = pl.ds(pl.multiple_of(firsts[item], 8), 8)
            second = pl.ds(pl.multiple_of(seconds[item], 8), 8)
            target = pl.ds(pl.multiple_of(targets[item], 8), 8)
            ref = acc_refs[item % ACCS]
            product = coefs[item : item + 1, :] * (field_ref[first, :] * field_ref[second, :])
            ref[target, :] = ref[target, :] + product
        return carry

    lax.fori_loop(0, pairs // UNROLL, interact, 0)

    def finish(step, carry):
        first = pl.multiple_of(step * BLOCK, BLOCK)
        for row in range(3):
            for half in range(2):
                rows = pl.ds(first * 8 + (2 * row + half), BLOCK, stride=8)
                total = acc_refs[0][rows, :]
                for ref in acc_refs[1:]:
                    total = total + ref[rows, :]
                out_ref[row, pl.ds(first, BLOCK), half * LANES : (half + 1) * LANES] = (
                    total.astype(jnp.bfloat16)
                )
        return carry

    parts = 4
    out_copies = []
    for part in range(parts):
        span = pl.ds(part * (bins // parts), bins // parts)
        each = bins // BLOCK // parts
        lax.fori_loop(part * each, (part + 1) * each, finish, 0)
        for row in range(3):
            out_copies.append(
                pltpu.make_async_copy(
                    out_ref.at[row, span], out_hbm.at[row, span], out_sems.at[3 * part + row]
                )
            )
            out_copies[-1].start()
    for copy in out_copies:
        copy.wait()


def ocean_kernel(currents_ref, recv_ref, wet_ref, out_ref, wide_ref, rows_ref):
    rows = currents_ref.shape[1]
    half = LANES // 2
    lane = lax.broadcasted_iota(jnp.int32, (rows, LANES), 1)
    place = lane & (half - 1)
    sign = jnp.where(lane < half, CORIOLIS, -CORIOLIS)
    wet = wet_columns(wet_ref)
    wide_ref[...] = recv_ref[...].astype(jnp.float32)
    for slot in range(2):
        for row in range(3):
            rows_ref[pl.ds(row, LANES, stride=3), :] = wide_ref[
                pl.ds(slot * 3 + row, LANES, stride=8), :
            ]
        x = currents_ref[slot]
        upper = jnp.where(place == 0, x, pltpu.roll(x, 1, 1))
        lower = jnp.where(place == half - 1, x, pltpu.roll(x, LANES - 1, 1))
        cross = sign * pltpu.roll(x + rows_ref[...], half, 1)
        mixed = upper + lower - 2.0 * x
        out_ref[slot] = wet[:, slot : slot + 1] * (x + DT_OCEAN * (cross + MIXING * mixed))


def wave_program(ids, pair_rows, coefs, speeds, inner, outer, surface, near, weights, wet, *pieces):
    f32 = jnp.float32
    count = len(pieces)
    columns = wet.shape[1]
    rows = wet.shape[0] // count
    bins = speeds.shape[1]
    return call(
        functools.partial(wave_kernel, count),
        jax.ShapeDtypeStruct((rows, bins, columns), jnp.bfloat16),
        [in_smem(), anywhere()] + [in_hbm()] * 4 + [in_vmem()] * (4 + count),
        in_hbm(),
        [
            SMEM(pair_rows.shape, jnp.int32),
            VMEM(coefs.shape, f32),
            VMEM(speeds.shape, f32),
            VMEM((2, *inner.shape), jnp.bfloat16),
            VMEM((rows, bins, columns), jnp.bfloat16),
            VMEM((bins * 8, LANES), f32),
            VMEM((56, columns), f32),
            VMEM((8 * PITCH, LANES), f32),
            VMEM((rows, 4, bins, LANES), jnp.bfloat16),
            pltpu.SemaphoreType.DMA((5,)),
            pltpu.SemaphoreType.DMA((12,)),
        ]
        + [VMEM((bins * 8, LANES), f32)] * ACCS,
        40_000_000,
        8_000_000,
        (
            ids,
            pair_rows,
            *kept_in(pltpu.HBM, coefs, speeds, inner, outer),
            surface,
            near,
            weights,
            wet,
            *kept_in(VMEM, *pieces),
        ),
        WAVE_LIMIT,
    )


def per_device(
    spectrum,
    group_speed,
    stokes_kernel,
    pair_bins,
    pair_coef,
    currents,
    col_map,
    wave_wet,
    ocean_wet,
):
    local_bins, tile_rows, columns = spectrum.shape
    space_count = lax.axis_size("space")
    bins_count = lax.axis_size("bins")
    devices = space_count * bins_count
    bins = local_bins * bins_count
    pairs = pair_bins.shape[1]
    both = ("space", "bins")
    f32 = jnp.float32
    bf16 = jnp.bfloat16
    space_at = lax.axis_index("space")
    bins_at = lax.axis_index("bins")

    near_ids = [lax.rem(bins_at + step, bins_count) for step in (bins_count - 1, 1)]
    ids = jnp.stack([bins_at, *near_ids, space_at]).astype(jnp.int32)

    order = (4, 5, 2, 6, 3, 7, 1, 0)
    piece_shape = (CHUNKS, local_bins, LANES)
    sent = call(
        functools.partial(pack_kernel, order),
        [jax.ShapeDtypeStruct(piece_shape, bf16)]
        + [pltpu.HBM(piece_shape, bf16)] * (bins_count - 1),
        [in_smem(), in_hbm(), in_hbm()],
        [in_vmem()] + [in_hbm()] * (bins_count - 1),
        [
            VMEM(spectrum.shape, bf16),
            VMEM((2, local_bins * tile_rows, LANES), f32),
            VMEM(stokes_kernel.shape, bf16),
            VMEM((bins_count - 1, *piece_shape), bf16),
            pltpu.SemaphoreType.DMA((4,)),
            pltpu.SemaphoreType.DMA((bins_count, 4)),
        ],
        2_000_000,
        4_000_000,
        (
            ids,
            pltpu.with_memory_space_constraint(spectrum, pltpu.HBM),
            pltpu.with_memory_space_constraint(stokes_kernel, pltpu.HBM),
        ),
    )
    pieces = [sent[0]] * bins_count
    for turn in order[:-1]:
        partners = [(at, at ^ turn) for at in range(bins_count)]
        pieces[turn] = lax.ppermute(sent[turn], "bins", partners)

    surface = call(
        surface_kernel,
        jax.ShapeDtypeStruct((devices, LANES), f32),
        [in_smem()] + [in_vmem()] * 3,
        in_vmem(),
        [VMEM((2 * ROW_GAP, LANES), f32)],
        4_000_000,
        500_000,
        (ids, currents, ocean_wet, group_speed),
    )
    arrived = lax.all_to_all(surface, both, split_axis=0, concat_axis=0, tiled=True)
    map_row = col_map.reshape(1, -1)
    surface_rows, speed_rows, coefs, pair_rows = call(
        tables_kernel,
        (
            jax.ShapeDtypeStruct((32, columns), f32),
            pltpu.HBM((2, bins, LANES), f32),
            pltpu.HBM((pairs, LANES), f32),
            jax.ShapeDtypeStruct((3 * pairs // LANES, LANES), jnp.int32),
        ),
        [in_vmem()] * 4,
        (in_vmem(), in_hbm(), in_hbm(), in_vmem()),
        [
            VMEM((2, bins, LANES), f32),
            VMEM((pairs, LANES), f32),
            pltpu.SemaphoreType.DMA((6,)),
        ],
        600_000_000,
        1_300_000,
        (arrived.reshape(devices, LANES), map_row, pair_coef.reshape(-1, LANES), pair_bins),
    )

    halo_shape = (bins_count, 2, local_bins, LANES)
    inner, outer = call(
        edges_kernel,
        [jax.ShapeDtypeStruct(halo_shape, bf16)] * 2,
        [in_smem()] + [in_vmem()] * bins_count,
        [in_vmem()] * 2,
        [],
        1_000_000,
        2_400_000,
        (ids, *pieces),
    )
    outward = [(at, at + 1) for at in range(1, devices - 1, 2)]
    outward += [(at + 1, at) for at, _ in outward]
    outer = lax.ppermute(outer, both, outward)
    inner = lax.ppermute(inner, both, [(at, at ^ 1) for at in range(devices)])

    routed, near, weights = call(
        functools.partial(drift_kernel, bins_count),
        (
            pltpu.HBM((devices * 8, LANES), bf16),
            jax.ShapeDtypeStruct((16, columns), f32),
            jax.ShapeDtypeStruct((32, bins), bf16),
        ),
        [in_smem(), in_vmem()] + [in_vmem()] * bins_count,
        (in_hbm(), in_vmem(), in_vmem()),
        [
            VMEM((devices * 8, LANES), f32),
            VMEM((bins_count, local_bins, LANES), bf16),
            VMEM((devices * 8, LANES), bf16),
            pltpu.SemaphoreType.DMA((4,)),
        ],
        300_000_000,
        2_500_000,
        (ids, map_row, *pieces),
    )
    routed = lax.all_to_all(
        routed.reshape(devices, 8, LANES), both, split_axis=0, concat_axis=0, tiled=True
    )
    routed = routed.reshape(devices * 8, LANES)

    new_spectrum = wave_program(
        ids,
        pair_rows.reshape(-1),
        coefs,
        speed_rows,
        inner,
        outer,
        surface_rows,
        near,
        weights,
        wave_wet,
        *pieces,
    )
    new_currents = call(
        ocean_kernel,
        jax.ShapeDtypeStruct(currents.shape, f32),
        [in_vmem()] * 3,
        in_vmem(),
        [VMEM((devices * 8, LANES), f32), VMEM((currents.shape[1], LANES), f32)],
        4_000_000,
        1_500_000,
        (currents, routed, ocean_wet),
    )
    return (jnp.transpose(new_spectrum, (1, 0, 2)), new_currents)


def solution(mesh):
    placed = (
        P("bins", "space", None),
        P(None, "bins"),
        P("bins", None),
        P(),
        P(),
        P(("space", "bins"), None, None),
        P(),
        P("space", None),
        P(("space", "bins"), None),
    )

    return jax.shard_map(
        per_device,
        mesh=mesh,
        in_specs=placed,
        out_specs=(P(None, ("space", "bins"), None), P(("space", "bins"), None, None)),
        check_vma=False,
    )
```

```python
import functools

import jax
import jax.numpy as jnp
from jax import lax
from jax.experimental import pallas as pl
from jax.experimental.pallas import tpu as pltpu
from jax.sharding import PartitionSpec as P


DT_OCEAN = 0.5
CORIOLIS = 0.8
MIXING = 0.4
CURRENT_SCALE = 0.15
DT_SOURCE = 0.5

LANES = 128
ACCS = 3
WAVE_LIMIT = 36
CHUNKS = 7
UNROLL = 48
BLOCK = 16
PITCH = 24
ROW_GAP = 400
SPEED_LANE = 32
PIECES = 16
HIGHEST = lax.Precision.HIGHEST
VMEM = pltpu.VMEM
SMEM = pltpu.SMEM


def in_vmem():
    return pl.BlockSpec(memory_space=VMEM)


def in_smem():
    return pl.BlockSpec(memory_space=SMEM)


def anywhere():
    return pl.BlockSpec(memory_space=pl.ANY)


def in_hbm():
    return pl.BlockSpec(memory_space=pltpu.HBM)


def kept_in(space, *values):
    return [pltpu.with_memory_space_constraint(value, space) for value in values]


def call(body, out_shape, ins, outs, scratch, flops, moved, args, limit=16):
    return pl.pallas_call(
        body,
        out_shape=out_shape,
        in_specs=ins,
        out_specs=outs,
        scratch_shapes=scratch,
        compiler_params=pltpu.CompilerParams(vmem_limit_bytes=limit * 2**20),
        cost_estimate=pl.CostEstimate(flops=flops, bytes_accessed=moved, transcendentals=0),
    )(*args)


def placed(device, row):
    return row + (device & 1) * (2 - 2 * row)


def pack_kernel(order, ids_ref, spectrum_hbm, stokes_hbm, *refs):
    count = len(order)
    out_refs = refs[:count]
    narrow_ref, wide_ref, stokes_ref, piece_ref, in_sems, out_sems = refs[count:]
    local_bins, tile_rows, _ = spectrum_hbm.shape
    rows = tile_rows // count
    chunks = in_sems.shape[0] - 1
    part = local_bins // chunks
    loads = []
    for chunk in range(chunks):
        span = pl.ds(chunk * part, part)
        loads.append(
            pltpu.make_async_copy(spectrum_hbm.at[span], narrow_ref.at[span], in_sems.at[chunk])
        )
    loads.append(pltpu.make_async_copy(stokes_hbm, stokes_ref, in_sems.at[chunks]))
    for copy in loads:
        copy.start()
    own = ids_ref[0]
    stores = []
    for chunk in range(chunks):
        loads[chunk].wait()
        first = chunk * part
        span = pl.ds(first, part)
        for half in range(2):
            lanes = slice(half * LANES, (half + 1) * LANES)
            value = narrow_ref[first : first + part, :, lanes].astype(jnp.float32)
            wide_ref[half, first * tile_rows : (first + part) * tile_rows] = value.reshape(
                part * tile_rows, LANES
            )
        for turn in order:
            target = own ^ turn
            base = target * rows + first * tile_rows
            ref = piece_ref.at[turn - 1] if turn else out_refs[0]
            for row in range(rows):
                for half in range(2):
                    value = wide_ref[
                        half, pl.ds(base + placed(target, row), part, stride=tile_rows), :
                    ]
                    ref[2 * row + half, first : first + part, :] = value.astype(jnp.bfloat16)
            if turn:
                stores.append(
                    pltpu.make_async_copy(
                        piece_ref.at[turn - 1, pl.ds(0, 6), span],
                        out_refs[turn].at[pl.ds(0, 6), span],
                        out_sems.at[turn, chunk],
                    )
                )
                stores[-1].start()
        if chunk == 0:
            loads[chunks].wait()
            out_refs[0][6] = stokes_ref[...]
            for turn in range(2, count, 2):
                stores.append(
                    pltpu.make_async_copy(
                        stokes_ref, out_refs[turn].at[6], out_sems.at[turn, chunks]
                    )
                )
                stores[-1].start()
    for copy in stores:
        copy.wait()


def joined(refs, chunk):
    return jnp.concatenate([ref[chunk] for ref in refs], axis=0)


def edges_kernel(*refs):
    inner_ref, outer_ref, stokes_ref = refs[-3:]
    for turn, ref in enumerate(refs[:-3]):
        outer_ref[turn] = ref[0:2]
        inner_ref[turn] = ref[4:6]
        if turn % 2 == 0:
            stokes_ref[turn // 2] = ref[6]


def wet_columns(wet_ref):
    wet = wet_ref[...].astype(jnp.float32)
    rows = wet.shape[1]
    return jnp.concatenate([wet, jnp.zeros((6, rows), jnp.float32)], axis=0).T


def surface_kernel(ids_ref, currents_ref, wet_ref, speed_ref, out_ref, rows_ref):
    rows = currents_ref.shape[1]
    half = LANES // 2
    lane = lax.broadcasted_iota(jnp.int32, (rows, LANES), 1)
    wet = wet_columns(wet_ref)
    sign = jnp.where(lane < half, CORIOLIS, -CORIOLIS)
    kept = (lane == 0) | (lane == 1) | (lane == half)
    rows_ref[...] = jnp.zeros_like(rows_ref)
    for slot in range(2):
        x = currents_ref[slot]
        cross = sign * pltpu.roll(x, half, 1)
        below = pltpu.roll(x, LANES - 1, 1)
        column = wet[:, slot : slot + 1]
        value = column * (x + DT_OCEAN * (cross + MIXING * (below - x)))
        value = jnp.where(lane == 1, column, value)
        rows_ref[pl.ds(slot * ROW_GAP + 8, rows), :] = jnp.where(kept, value, 0.0)
    local_bins = speed_ref.shape[1]
    piece = local_bins // PIECES
    index = lax.broadcasted_iota(jnp.int32, (local_bins, LANES), 0) - ids_ref[3] * piece
    place = lax.broadcasted_iota(jnp.int32, (local_bins, LANES), 1) - SPEED_LANE
    inside = (index >= 0) & (index < piece)
    speeds = jnp.zeros((1, LANES), jnp.float32)
    for part in range(2):
        pick = (inside & (place == index + part * piece)).astype(jnp.float32)
        speeds = speeds + jnp.dot(
            speed_ref[part : part + 1, :],
            pick,
            precision=HIGHEST,
            preferred_element_type=jnp.float32,
        )
    total = jnp.broadcast_to(speeds, (LANES, LANES))
    for slot in range(2):
        for row in range(5):
            part = rows_ref[pl.ds(slot * ROW_GAP + 7 + row, LANES, stride=3), :]
            shift = 2 * (slot * 5 + row)
            total = total + (pltpu.roll(part, shift, 1) if shift else part)
    out_ref[...] = total


def columns_of(map_ref):
    row = jnp.broadcast_to(map_ref[...].astype(jnp.float32), (LANES, LANES))
    column = row.T
    return jnp.concatenate([column, column], axis=1)


def chosen(column, slot):
    index = lax.broadcasted_iota(jnp.int32, column.shape, 1).astype(jnp.float32)
    return (2.0 * column + float(slot)) == index


def thirds(value):
    high = value.astype(jnp.bfloat16)
    rest = value - high.astype(jnp.float32)
    middle = rest.astype(jnp.bfloat16)
    low = (rest - middle.astype(jnp.float32)).astype(jnp.bfloat16)
    return [high, middle, low]


def pairs_kernel(coef_ref, pair_ref, coefs_hbm, rows_ref, coefs_ref, sems):
    blocks = coef_ref.shape[0]
    copies = []
    for block in range(blocks):
        lanes = slice(block * LANES, (block + 1) * LANES)
        for side in range(3):
            at = side * blocks + block
            rows_ref[at : at + 1, :] = pair_ref[side : side + 1, lanes] * 8
        row = DT_SOURCE * coef_ref[block : block + 1, :]
        coefs_ref[lanes, :] = jnp.broadcast_to(row, (LANES, LANES)).T
        if (block + 1) % (blocks // 4) == 0:
            span = pl.ds((block + 1 - blocks // 4) * LANES, blocks // 4 * LANES)
            copies.append(
                pltpu.make_async_copy(
                    coefs_ref.at[span], coefs_hbm.at[span], sems.at[len(copies)]
                )
            )
            copies[-1].start()
    for copy in copies:
        copy.wait()


def tables_kernel(recv_ref, map_ref, surface_ref, speeds_hbm, speeds_ref, sems):
    bf16 = jnp.bfloat16
    parts = thirds(recv_ref[...])
    copies = []
    bins = speeds_ref.shape[1]
    lane = lax.broadcasted_iota(jnp.int32, (bins, LANES), 1)
    index = lax.broadcasted_iota(jnp.int32, (bins, LANES), 0)
    first = ((lane & 7) * 16 + (lane >> 3)) * 9
    own = ((index >= first) & (index < first + 9)).astype(jnp.float32).astype(bf16)
    rows = [jnp.dot(own, part, preferred_element_type=jnp.float32) for part in parts]
    place = index - ((index * 7282) >> 16) * 9
    ones = jnp.ones((LANES, LANES), bf16)
    for part in range(2):
        mine = lane == place + (SPEED_LANE + 9 * part)
        total = jnp.zeros((bins, LANES), jnp.float32)
        for value in rows:
            kept = jnp.where(mine, value, 0.0).astype(bf16)
            total = total + jnp.dot(kept, ones, preferred_element_type=jnp.float32)
        speeds_ref[part] = total
        copies.append(
            pltpu.make_async_copy(speeds_ref.at[part], speeds_hbm.at[part], sems.at[part])
        )
        copies[-1].start()
    turned = thirds(recv_ref[...].T)
    column = columns_of(map_ref)
    found = []
    for slot in range(2):
        pick = chosen(column, slot).astype(jnp.float32).astype(bf16)
        found.append(
            sum(jnp.dot(part, pick, preferred_element_type=jnp.float32) for part in turned)
        )
    surface_ref[...] = jnp.zeros_like(surface_ref)
    surface_ref[0:10, :] = found[0][0:10] + found[1][10:20]
    surface_ref[16:26, :] = found[0][64:74] + found[1][74:84]
    for copy in copies:
        copy.wait()


def drift_kernel(count, ids_ref, map_ref, other_ref, *refs):
    piece_refs = refs[:count]
    routed_hbm, near_ref, weights_ref, rows_ref, stokes_ref, routed_ref, sems = refs[count:]
    own = ids_ref[0]
    stokes = [
        other_ref[turn // 2] if turn % 2 else ref[6] for turn, ref in enumerate(piece_refs)
    ]
    for turn, value in enumerate(stokes):
        stokes_ref[own ^ turn] = value
    in_order = stokes_ref[...].reshape(-1, LANES).T
    weights_ref[0:16, :] = in_order[0:16]
    weights_ref[16:32, :] = in_order[64:80]
    turned = jnp.concatenate(stokes, axis=0).T
    column = columns_of(map_ref)
    picks = [chosen(column, slot).astype(jnp.float32).astype(jnp.bfloat16) for slot in range(2)]
    rows_ref[...] = jnp.zeros_like(rows_ref)
    near_ref[...] = jnp.zeros_like(near_ref)
    for row in range(3):
        parts = [jnp.zeros((LANES, LANES), jnp.float32) for _ in range(2)]
        for half in range(2):
            cells = joined(piece_refs, 2 * placed(own, row) + half)
            drift = jnp.dot(turned, cells, preferred_element_type=jnp.float32)
            lanes = slice(half * LANES, (half + 1) * LANES)
            near_ref[row : row + 1, lanes] = drift[0:1]
            near_ref[8 + row : 9 + row, lanes] = drift[64:65]
            narrow = drift.astype(jnp.bfloat16)
            for slot in range(2):
                parts[slot] = parts[slot] + lax.dot_general(
                    picks[slot][:, lanes],
                    narrow,
                    (((1,), (1,)), ((), ())),
                    preferred_element_type=jnp.float32,
                )
        for slot in range(2):
            rows_ref[pl.ds(slot * 3 + row, LANES, stride=8), :] = parts[slot]
    parts = sems.shape[0]
    size = rows_ref.shape[0] // parts
    copies = []
    for part in range(parts):
        span = pl.ds(part * size, size)
        routed_ref[span, :] = rows_ref[span, :].astype(jnp.bfloat16)
        copies.append(
            pltpu.make_async_copy(routed_ref.at[span], routed_hbm.at[span], sems.at[part])
        )
        copies[-1].start()
    for copy in copies:
        copy.wait()


def wave_kernel(
    count,
    ids_ref,
    pair_hbm,
    coef_hbm,
    speeds_hbm,
    inner_hbm,
    outer_hbm,
    surface_ref,
    near_ref,
    weights_ref,
    wet_ref,
    *refs,
):
    piece_refs = refs[:count]
    (
        out_hbm,
        pair_ref,
        coef_ref,
        speeds_ref,
        halo_ref,
        out_ref,
        field_ref,
        cur_ref,
        turn_ref,
        beside_ref,
        in_sems,
        out_sems,
        *acc_refs,
    ) = refs[count:]
    local_bins = piece_refs[0].shape[1]
    bins = count * local_bins
    pairs = coef_ref.shape[0]

    core = ids_ref[0] & 1
    moves = (
        (inner_hbm, halo_ref.at[1 - core]),
        (outer_hbm, halo_ref.at[core]),
        (speeds_hbm, speeds_ref),
        (pair_hbm, pair_ref),
        (coef_hbm, coef_ref),
    )
    loads = [
        pltpu.make_async_copy(src, dst, in_sems.at[at]) for at, (src, dst) in enumerate(moves)
    ]
    for copy in loads:
        copy.start()
    own = ids_ref[0]
    turn_ref[...] = jnp.zeros_like(turn_ref)

    columns = 2 * LANES
    given = lax.broadcasted_iota(jnp.int32, (columns, 2 * columns), 0)
    taken = lax.broadcasted_iota(jnp.int32, (columns, 2 * columns), 1)
    pick = given == jnp.where(taken < columns, taken - 1, taken - columns + 1)
    pick = pick.astype(jnp.float32)
    narrow_pick = pick.astype(jnp.bfloat16)
    for row in range(3):
        cells = jnp.concatenate(
            [joined(piece_refs, 2 * row + half) for half in range(2)], axis=1
        )
        beside = jnp.dot(cells, narrow_pick, preferred_element_type=jnp.float32)
        for part in range(4):
            beside_ref[row, part] = beside[:, part * LANES : (part + 1) * LANES].astype(
                jnp.bfloat16
            )

    loads[0].wait()
    loads[1].wait()
    weights = weights_ref[...]
    for side in range(2):
        for half in range(2):
            blocks = [halo_ref[side, ids_ref[1 + side] ^ block, half] for block in range(count)]
            cells = jnp.concatenate(blocks, axis=0)
            drift = jnp.dot(weights, cells, preferred_element_type=jnp.float32)
            lanes = slice(half * LANES, (half + 1) * LANES)
            cur_ref[24 + side : 25 + side, lanes] = drift[0:1]
            cur_ref[32 + side : 33 + side, lanes] = drift[16:17]
    for row in range(5):
        if row in (0, 4):
            side = 0 if row == 0 else 1
            east = cur_ref[24 + side : 25 + side, :]
            north = cur_ref[32 + side : 33 + side, :]
        else:
            east = near_ref[row - 1 : row, :]
            north = near_ref[8 + row - 1 : 8 + row, :]
        fixed_east = surface_ref[2 * row : 2 * row + 1, :]
        wet = surface_ref[2 * row + 1 : 2 * row + 2, :]
        fixed_north = surface_ref[16 + 2 * row : 17 + 2 * row, :]
        factor = (DT_OCEAN * CORIOLIS) * wet
        cur_ref[row : row + 1, :] = CURRENT_SCALE * jnp.tanh(fixed_east + factor * north)
        cur_ref[8 + row : 9 + row, :] = CURRENT_SCALE * jnp.tanh(fixed_north - factor * east)
    for row in range(3):
        wet = wet_ref[pl.ds(own * 3 + row, 1), :]
        cur_ref[16 + row : 17 + row, :] = wet.astype(jnp.float32)

    near_cur = jnp.dot(
        cur_ref[8:16, :], pick, precision=HIGHEST, preferred_element_type=jnp.float32
    )
    cur_ref[40:48, :] = near_cur[:, :columns]
    cur_ref[48:56, :] = near_cur[:, columns:]
    loads[2].wait()

    def advect(piece_ref, turn, block, step):
        start = pl.multiple_of(step * BLOCK, BLOCK)
        first = block * local_bins + start
        span = pl.ds(start, BLOCK)
        below_at = ids_ref[1] ^ block
        above_at = ids_ref[2] ^ block
        speed_x = speeds_ref[0, pl.ds(pl.multiple_of(first, BLOCK), BLOCK), :]
        speed_y = speeds_ref[1, pl.ds(pl.multiple_of(first, BLOCK), BLOCK), :]

        def row_flux(energy, row, half):
            current = cur_ref[row : row + 1, half * LANES : (half + 1) * LANES]
            return (speed_x + current) * energy

        energy = [
            [
                piece_ref[2 * placed(own, row) + half, span, :].astype(jnp.float32)
                for half in range(2)
            ]
            for row in range(3)
        ]
        for half in range(2):
            flux = [row_flux(halo_ref[0, below_at, half, span, :].astype(jnp.float32), 0, half)]
            flux += [row_flux(energy[row][half], row + 1, half) for row in range(3)]
            flux += [row_flux(halo_ref[1, above_at, half, span, :].astype(jnp.float32), 4, half)]
            for row in range(3):
                energy[row][half] = (
                    energy[row][half],
                    energy[row][half]
                    - jnp.abs(flux[row + 1])
                    + jnp.maximum(flux[row], 0.0)
                    - jnp.minimum(flux[row + 2], 0.0),
                )
        for row in range(3):
            for half in range(2):
                old, value = energy[row][half]
                lanes = slice(half * LANES, (half + 1) * LANES)
                at_row = placed(own, row)
                spot = pl.ds(pl.multiple_of(turn * local_bins + start, BLOCK), BLOCK)

                def side(at, cells, row=row, lanes=lanes):
                    return (speed_y + cur_ref[at + 1 + row : at + 2 + row, lanes]) * cells

                left = side(40, beside_ref[at_row, half, spot, :].astype(jnp.float32))
                right = side(48, beside_ref[at_row, 2 + half, spot, :].astype(jnp.float32))
                wet = cur_ref[16 + row : 17 + row, lanes]
                moved = value - jnp.abs(side(8, old))
                result = wet * (moved + jnp.maximum(left, 0.0) - jnp.minimum(right, 0.0))
                at = (2 * row + half) * PITCH
                turn_ref[at : at + BLOCK, :] = result
        zeros = jnp.zeros((8, LANES), jnp.float32)
        for item in range(BLOCK):
            rows = pl.ds(pl.multiple_of((first + item) * 8, 8), 8)
            tile = turn_ref[pl.ds(item, 8, stride=PITCH), :]
            field_ref[rows, :] = tile
            acc_refs[0][rows, :] = tile
            for ref in acc_refs[1:]:
                ref[rows, :] = zeros

    for turn, piece_ref in enumerate(piece_refs):
        block = own ^ turn

        def one(step, carry, piece_ref=piece_ref, turn=turn, block=block):
            advect(piece_ref, turn, block, step)
            return carry

        lax.fori_loop(0, local_bins // BLOCK, one, 0)
    loads[3].wait()
    loads[4].wait()

    def interact(step, carry):
        start = pl.multiple_of(step * UNROLL, UNROLL)
        firsts = pair_ref.at[pl.ds(start, UNROLL)]
        seconds = pair_ref.at[pl.ds(pairs + start, UNROLL)]
        targets = pair_ref.at[pl.ds(2 * pairs + start, UNROLL)]
        coefs = coef_ref.at[pl.ds(start, UNROLL)]
        for item in range(UNROLL):
            first = pl.ds(pl.multiple_of(firsts[item], 8), 8)
            second = pl.ds(pl.multiple_of(seconds[item], 8), 8)
            target = pl.ds(pl.multiple_of(targets[item], 8), 8)
            ref = acc_refs[item % ACCS]
            product = coefs[item : item + 1, :] * (field_ref[first, :] * field_ref[second, :])
            ref[target, :] = ref[target, :] + product
        return carry

    lax.fori_loop(0, pairs // UNROLL, interact, 0)

    def finish(step, carry):
        first = pl.multiple_of(step * BLOCK, BLOCK)
        for row in range(3):
            for half in range(2):
                rows = pl.ds(first * 8 + (2 * row + half), BLOCK, stride=8)
                total = acc_refs[0][rows, :]
                for ref in acc_refs[1:]:
                    total = total + ref[rows, :]
                out_ref[row, pl.ds(first, BLOCK), half * LANES : (half + 1) * LANES] = (
                    total.astype(jnp.bfloat16)
                )
        return carry

    parts = 4
    out_copies = []
    for part in range(parts):
        span = pl.ds(part * (bins // parts), bins // parts)
        each = bins // BLOCK // parts
        lax.fori_loop(part * each, (part + 1) * each, finish, 0)
        for row in range(3):
            out_copies.append(
                pltpu.make_async_copy(
                    out_ref.at[row, span], out_hbm.at[row, span], out_sems.at[3 * part + row]
                )
            )
            out_copies[-1].start()
    for copy in out_copies:
        copy.wait()


def ocean_kernel(currents_ref, recv_ref, wet_ref, out_ref, wide_ref, rows_ref):
    rows = currents_ref.shape[1]
    half = LANES // 2
    lane = lax.broadcasted_iota(jnp.int32, (rows, LANES), 1)
    place = lane & (half - 1)
    sign = jnp.where(lane < half, CORIOLIS, -CORIOLIS)
    wet = wet_columns(wet_ref)
    wide_ref[...] = recv_ref[...].astype(jnp.float32)
    for slot in range(2):
        for row in range(3):
            rows_ref[pl.ds(row, LANES, stride=3), :] = wide_ref[
                pl.ds(slot * 3 + row, LANES, stride=8), :
            ]
        x = currents_ref[slot]
        upper = jnp.where(place == 0, x, pltpu.roll(x, 1, 1))
        lower = jnp.where(place == half - 1, x, pltpu.roll(x, LANES - 1, 1))
        cross = sign * pltpu.roll(x + rows_ref[...], half, 1)
        mixed = upper + lower - 2.0 * x
        out_ref[slot] = wet[:, slot : slot + 1] * (x + DT_OCEAN * (cross + MIXING * mixed))


def wave_program(ids, pair_rows, coefs, speeds, inner, outer, surface, near, weights, wet, *pieces):
    f32 = jnp.float32
    count = len(pieces)
    columns = wet.shape[1]
    rows = wet.shape[0] // count
    bins = speeds.shape[1]
    return call(
        functools.partial(wave_kernel, count),
        jax.ShapeDtypeStruct((rows, bins, columns), jnp.bfloat16),
        [in_smem(), anywhere()] + [in_hbm()] * 4 + [in_vmem()] * (4 + count),
        in_hbm(),
        [
            SMEM(pair_rows.shape, jnp.int32),
            VMEM(coefs.shape, f32),
            VMEM(speeds.shape, f32),
            VMEM((2, *inner.shape), jnp.bfloat16),
            VMEM((rows, bins, columns), jnp.bfloat16),
            VMEM((bins * 8, LANES), f32),
            VMEM((56, columns), f32),
            VMEM((8 * PITCH, LANES), f32),
            VMEM((rows, 4, bins, LANES), jnp.bfloat16),
            pltpu.SemaphoreType.DMA((5,)),
            pltpu.SemaphoreType.DMA((12,)),
        ]
        + [VMEM((bins * 8, LANES), f32)] * ACCS,
        40_000_000,
        8_000_000,
        (
            ids,
            pair_rows,
            *kept_in(pltpu.HBM, coefs, speeds, inner, outer),
            surface,
            near,
            weights,
            wet,
            *kept_in(VMEM, *pieces),
        ),
        WAVE_LIMIT,
    )


def per_device(
    spectrum,
    group_speed,
    stokes_kernel,
    pair_bins,
    pair_coef,
    currents,
    col_map,
    wave_wet,
    ocean_wet,
):
    local_bins, tile_rows, columns = spectrum.shape
    space_count = lax.axis_size("space")
    bins_count = lax.axis_size("bins")
    devices = space_count * bins_count
    bins = local_bins * bins_count
    pairs = pair_bins.shape[1]
    both = ("space", "bins")
    f32 = jnp.float32
    bf16 = jnp.bfloat16
    space_at = lax.axis_index("space")
    bins_at = lax.axis_index("bins")

    near_ids = [lax.rem(bins_at + step, bins_count) for step in (bins_count - 1, 1)]
    ids = jnp.stack([bins_at, *near_ids, space_at]).astype(jnp.int32)

    order = (4, 5, 2, 6, 3, 7, 1, 0)
    piece_shape = (CHUNKS, local_bins, LANES)
    sent = call(
        functools.partial(pack_kernel, order),
        [jax.ShapeDtypeStruct(piece_shape, bf16)]
        + [
            pltpu.HBM((CHUNKS - turn % 2, local_bins, LANES), bf16)
            for turn in range(1, bins_count)
        ],
        [in_smem(), in_hbm(), in_hbm()],
        [in_vmem()] + [in_hbm()] * (bins_count - 1),
        [
            VMEM(spectrum.shape, bf16),
            VMEM((2, local_bins * tile_rows, LANES), f32),
            VMEM(stokes_kernel.shape, bf16),
            VMEM((bins_count - 1, *piece_shape), bf16),
            pltpu.SemaphoreType.DMA((4,)),
            pltpu.SemaphoreType.DMA((bins_count, 4)),
        ],
        2_000_000,
        4_000_000,
        (
            ids,
            pltpu.with_memory_space_constraint(spectrum, pltpu.HBM),
            pltpu.with_memory_space_constraint(stokes_kernel, pltpu.HBM),
        ),
    )
    pieces = [sent[0]] * bins_count
    for turn in order[:-1]:
        partners = [(at, at ^ turn) for at in range(bins_count)]
        pieces[turn] = lax.ppermute(sent[turn], "bins", partners)

    surface = call(
        surface_kernel,
        jax.ShapeDtypeStruct((devices, LANES), f32),
        [in_smem()] + [in_vmem()] * 3,
        in_vmem(),
        [VMEM((2 * ROW_GAP, LANES), f32)],
        4_000_000,
        500_000,
        (ids, currents, ocean_wet, group_speed),
    )
    arrived = lax.all_to_all(surface, both, split_axis=0, concat_axis=0, tiled=True)
    map_row = col_map.reshape(1, -1)
    coefs, pair_rows = call(
        pairs_kernel,
        (
            pltpu.HBM((pairs, LANES), f32),
            jax.ShapeDtypeStruct((3 * pairs // LANES, LANES), jnp.int32),
        ),
        [in_vmem()] * 2,
        (in_hbm(), in_vmem()),
        [VMEM((pairs, LANES), f32), pltpu.SemaphoreType.DMA((4,))],
        1_000_000,
        2_500_000,
        (pair_coef.reshape(-1, LANES), pair_bins),
    )
    surface_rows, speed_rows = call(
        tables_kernel,
        (
            jax.ShapeDtypeStruct((32, columns), f32),
            pltpu.HBM((2, bins, LANES), f32),
        ),
        [in_vmem()] * 2,
        (in_vmem(), in_hbm()),
        [VMEM((2, bins, LANES), f32), pltpu.SemaphoreType.DMA((2,))],
        600_000_000,
        1_300_000,
        (arrived.reshape(devices, LANES), map_row),
    )

    halo_shape = (bins_count, 2, local_bins, LANES)
    stokes_shape = (bins_count // 2, local_bins, LANES)
    inner, outer, stokes = call(
        edges_kernel,
        [jax.ShapeDtypeStruct(halo_shape, bf16)] * 2 + [jax.ShapeDtypeStruct(stokes_shape, bf16)],
        [in_vmem()] * bins_count,
        [in_vmem()] * 3,
        [],
        1_000_000,
        2_400_000,
        tuple(pieces),
    )
    outward = [(at, at + 1) for at in range(1, devices - 1, 2)]
    outward += [(at + 1, at) for at, _ in outward]
    outer = lax.ppermute(outer, both, outward)
    within = [(at, at ^ 1) for at in range(devices)]
    inner = lax.ppermute(inner, both, within)
    stokes = lax.ppermute(stokes, both, within)

    routed, near, weights = call(
        functools.partial(drift_kernel, bins_count),
        (
            pltpu.HBM((devices * 8, LANES), bf16),
            jax.ShapeDtypeStruct((16, columns), f32),
            jax.ShapeDtypeStruct((32, bins), bf16),
        ),
        [in_smem()] + [in_vmem()] * (2 + bins_count),
        (in_hbm(), in_vmem(), in_vmem()),
        [
            VMEM((devices * 8, LANES), f32),
            VMEM((bins_count, local_bins, LANES), bf16),
            VMEM((devices * 8, LANES), bf16),
            pltpu.SemaphoreType.DMA((4,)),
        ],
        300_000_000,
        2_500_000,
        (ids, map_row, stokes, *pieces),
    )
    routed = lax.all_to_all(
        routed.reshape(devices, 8, LANES), both, split_axis=0, concat_axis=0, tiled=True
    )
    routed = routed.reshape(devices * 8, LANES)

    new_spectrum = wave_program(
        ids,
        pair_rows.reshape(-1),
        coefs,
        speed_rows,
        inner,
        outer,
        surface_rows,
        near,
        weights,
        wave_wet,
        *pieces,
    )
    new_currents = call(
        ocean_kernel,
        jax.ShapeDtypeStruct(currents.shape, f32),
        [in_vmem()] * 3,
        in_vmem(),
        [VMEM((devices * 8, LANES), f32), VMEM((currents.shape[1], LANES), f32)],
        4_000_000,
        1_500_000,
        (currents, routed, ocean_wet),
    )
    return (jnp.transpose(new_spectrum, (1, 0, 2)), new_currents)


def solution(mesh):
    placed = (
        P("bins", "space", None),
        P(None, "bins"),
        P("bins", None),
        P(),
        P(),
        P(("space", "bins"), None, None),
        P(),
        P("space", None),
        P(("space", "bins"), None),
    )

    return jax.shard_map(
        per_device,
        mesh=mesh,
        in_specs=placed,
        out_specs=(P(None, ("space", "bins"), None), P(("space", "bins"), None, None)),
        check_vma=False,
    )
```

```python
import functools

import jax
import jax.numpy as jnp
from jax import lax
from jax.experimental import pallas as pl
from jax.experimental.pallas import tpu as pltpu
from jax.sharding import PartitionSpec as P


DT_OCEAN = 0.5
CORIOLIS = 0.8
MIXING = 0.4
CURRENT_SCALE = 0.15
DT_SOURCE = 0.5

LANES = 128
ACCS = 3
WAVE_LIMIT = 36
CHUNKS = 7
UNROLL = 144
BLOCK = 16
PITCH = 24
ROW_GAP = 400
SPEED_LANE = 32
PIECES = 16
HIGHEST = lax.Precision.HIGHEST
VMEM = pltpu.VMEM
SMEM = pltpu.SMEM


def in_vmem():
    return pl.BlockSpec(memory_space=VMEM)


def in_smem():
    return pl.BlockSpec(memory_space=SMEM)


def anywhere():
    return pl.BlockSpec(memory_space=pl.ANY)


def in_hbm():
    return pl.BlockSpec(memory_space=pltpu.HBM)


def kept_in(space, *values):
    return [pltpu.with_memory_space_constraint(value, space) for value in values]


def call(body, out_shape, ins, outs, scratch, flops, moved, args, limit=16):
    return pl.pallas_call(
        body,
        out_shape=out_shape,
        in_specs=ins,
        out_specs=outs,
        scratch_shapes=scratch,
        compiler_params=pltpu.CompilerParams(vmem_limit_bytes=limit * 2**20),
        cost_estimate=pl.CostEstimate(flops=flops, bytes_accessed=moved, transcendentals=0),
    )(*args)


def placed(device, row):
    return row + (device & 1) * (2 - 2 * row)


def pack_kernel(order, ids_ref, spectrum_hbm, stokes_hbm, *refs):
    count = len(order)
    out_refs = refs[:count]
    narrow_ref, wide_ref, stokes_ref, piece_ref, in_sems, out_sems = refs[count:]
    local_bins, tile_rows, _ = spectrum_hbm.shape
    rows = tile_rows // count
    chunks = in_sems.shape[0] - 1
    part = local_bins // chunks
    loads = []
    for chunk in range(chunks):
        span = pl.ds(chunk * part, part)
        loads.append(
            pltpu.make_async_copy(spectrum_hbm.at[span], narrow_ref.at[span], in_sems.at[chunk])
        )
    loads.append(pltpu.make_async_copy(stokes_hbm, stokes_ref, in_sems.at[chunks]))
    for copy in loads:
        copy.start()
    own = ids_ref[0]
    stores = []
    for chunk in range(chunks):
        loads[chunk].wait()
        first = chunk * part
        span = pl.ds(first, part)
        for half in range(2):
            lanes = slice(half * LANES, (half + 1) * LANES)
            value = narrow_ref[first : first + part, :, lanes].astype(jnp.float32)
            wide_ref[half, first * tile_rows : (first + part) * tile_rows] = value.reshape(
                part * tile_rows, LANES
            )
        for turn in order:
            target = own ^ turn
            base = target * rows + first * tile_rows
            ref = piece_ref.at[turn - 1] if turn else out_refs[0]
            for row in range(rows):
                for half in range(2):
                    value = wide_ref[
                        half, pl.ds(base + placed(target, row), part, stride=tile_rows), :
                    ]
                    ref[2 * row + half, first : first + part, :] = value.astype(jnp.bfloat16)
            if turn:
                stores.append(
                    pltpu.make_async_copy(
                        piece_ref.at[turn - 1, pl.ds(0, 6), span],
                        out_refs[turn].at[pl.ds(0, 6), span],
                        out_sems.at[turn, chunk],
                    )
                )
                stores[-1].start()
        if chunk == 0:
            loads[chunks].wait()
            out_refs[0][6] = stokes_ref[...]
            for turn in range(2, count, 2):
                stores.append(
                    pltpu.make_async_copy(
                        stokes_ref, out_refs[turn].at[6], out_sems.at[turn, chunks]
                    )
                )
                stores[-1].start()
    for copy in stores:
        copy.wait()


def joined(refs, chunk):
    return jnp.concatenate([ref[chunk] for ref in refs], axis=0)


def edges_kernel(*refs):
    inner_ref, outer_ref, stokes_ref = refs[-3:]
    for turn, ref in enumerate(refs[:-3]):
        outer_ref[turn] = ref[0:2]
        inner_ref[turn] = ref[4:6]
        if turn % 2 == 0:
            stokes_ref[turn // 2] = ref[6]


def wet_columns(wet_ref):
    wet = wet_ref[...].astype(jnp.float32)
    rows = wet.shape[1]
    return jnp.concatenate([wet, jnp.zeros((6, rows), jnp.float32)], axis=0).T


def surface_kernel(ids_ref, currents_ref, wet_ref, speed_ref, out_ref, rows_ref):
    rows = currents_ref.shape[1]
    half = LANES // 2
    lane = lax.broadcasted_iota(jnp.int32, (rows, LANES), 1)
    wet = wet_columns(wet_ref)
    sign = jnp.where(lane < half, CORIOLIS, -CORIOLIS)
    kept = (lane == 0) | (lane == 1) | (lane == half)
    rows_ref[...] = jnp.zeros_like(rows_ref)
    for slot in range(2):
        x = currents_ref[slot]
        cross = sign * pltpu.roll(x, half, 1)
        below = pltpu.roll(x, LANES - 1, 1)
        column = wet[:, slot : slot + 1]
        value = column * (x + DT_OCEAN * (cross + MIXING * (below - x)))
        value = jnp.where(lane == 1, column, value)
        rows_ref[pl.ds(slot * ROW_GAP + 8, rows), :] = jnp.where(kept, value, 0.0)
    local_bins = speed_ref.shape[1]
    piece = local_bins // PIECES
    index = lax.broadcasted_iota(jnp.int32, (local_bins, LANES), 0) - ids_ref[3] * piece
    place = lax.broadcasted_iota(jnp.int32, (local_bins, LANES), 1) - SPEED_LANE
    inside = (index >= 0) & (index < piece)
    pick = inside & ((place == index) | (place == index + piece))
    split = jnp.concatenate(thirds(speed_ref[...]), axis=0)
    found = jnp.dot(
        split,
        pick.astype(jnp.float32).astype(jnp.bfloat16),
        preferred_element_type=jnp.float32,
    )
    found = found[0:2] + found[2:4] + found[4:6]
    spot = lax.broadcasted_iota(jnp.int32, (1, LANES), 1)
    speeds = jnp.where(spot < SPEED_LANE + piece, found[0:1], found[1:2])
    total = jnp.broadcast_to(speeds, (LANES, LANES))
    for slot in range(2):
        for row in range(5):
            part = rows_ref[pl.ds(slot * ROW_GAP + 7 + row, LANES, stride=3), :]
            shift = 2 * (slot * 5 + row)
            total = total + (pltpu.roll(part, shift, 1) if shift else part)
    out_ref[...] = total


def columns_of(map_ref):
    row = jnp.broadcast_to(map_ref[...].astype(jnp.float32), (LANES, LANES))
    column = row.T
    return jnp.concatenate([column, column], axis=1)


def chosen(column, slot):
    index = lax.broadcasted_iota(jnp.int32, column.shape, 1).astype(jnp.float32)
    return (2.0 * column + float(slot)) == index


def thirds(value):
    high = value.astype(jnp.bfloat16)
    rest = value - high.astype(jnp.float32)
    middle = rest.astype(jnp.bfloat16)
    low = (rest - middle.astype(jnp.float32)).astype(jnp.bfloat16)
    return [high, middle, low]


def pairs_kernel(coef_ref, pair_ref, coefs_hbm, rows_ref, coefs_ref, sems):
    blocks = coef_ref.shape[0]
    copies = []
    for block in range(blocks):
        lanes = slice(block * LANES, (block + 1) * LANES)
        for side in range(3):
            at = side * blocks + block
            rows_ref[at : at + 1, :] = pair_ref[side : side + 1, lanes] * 8
        row = DT_SOURCE * coef_ref[block : block + 1, :]
        coefs_ref[lanes, :] = jnp.broadcast_to(row, (LANES, LANES)).T
        if (block + 1) % (blocks // 4) == 0:
            span = pl.ds((block + 1 - blocks // 4) * LANES, blocks // 4 * LANES)
            copies.append(
                pltpu.make_async_copy(
                    coefs_ref.at[span], coefs_hbm.at[span], sems.at[len(copies)]
                )
            )
            copies[-1].start()
    for copy in copies:
        copy.wait()


def tables_kernel(recv_ref, map_ref, surface_ref, speeds_hbm, speeds_ref, sems):
    bf16 = jnp.bfloat16
    parts = thirds(recv_ref[...])
    copies = []
    bins = speeds_ref.shape[1]
    lane = lax.broadcasted_iota(jnp.int32, (bins, LANES), 1)
    index = lax.broadcasted_iota(jnp.int32, (bins, LANES), 0)
    first = ((lane & 7) * 16 + (lane >> 3)) * 9
    own = ((index >= first) & (index < first + 9)).astype(jnp.float32).astype(bf16)
    rows = [jnp.dot(own, part, preferred_element_type=jnp.float32) for part in parts]
    place = index - ((index * 7282) >> 16) * 9
    ones = jnp.ones((LANES, LANES), bf16)
    for part in range(2):
        mine = lane == place + (SPEED_LANE + 9 * part)
        total = jnp.zeros((bins, LANES), jnp.float32)
        for value in rows:
            kept = jnp.where(mine, value, 0.0).astype(bf16)
            total = total + jnp.dot(kept, ones, preferred_element_type=jnp.float32)
        speeds_ref[part] = total
        copies.append(
            pltpu.make_async_copy(speeds_ref.at[part], speeds_hbm.at[part], sems.at[part])
        )
        copies[-1].start()
    turned = thirds(recv_ref[...].T)
    column = columns_of(map_ref)
    found = []
    for slot in range(2):
        pick = chosen(column, slot).astype(jnp.float32).astype(bf16)
        found.append(
            sum(jnp.dot(part, pick, preferred_element_type=jnp.float32) for part in turned)
        )
    surface_ref[...] = jnp.zeros_like(surface_ref)
    surface_ref[0:10, :] = found[0][0:10] + found[1][10:20]
    surface_ref[16:26, :] = found[0][64:74] + found[1][74:84]
    for copy in copies:
        copy.wait()


def drift_kernel(count, ids_ref, map_ref, other_ref, *refs):
    piece_refs = refs[:count]
    routed_hbm, near_ref, weights_ref, rows_ref, stokes_ref, routed_ref, sems = refs[count:]
    own = ids_ref[0]
    stokes = [
        other_ref[turn // 2] if turn % 2 else ref[6] for turn, ref in enumerate(piece_refs)
    ]
    for turn, value in enumerate(stokes):
        stokes_ref[own ^ turn] = value
    in_order = stokes_ref[...].reshape(-1, LANES).T
    weights_ref[0:16, :] = in_order[0:16]
    weights_ref[16:32, :] = in_order[64:80]
    turned = jnp.concatenate(stokes, axis=0).T
    column = columns_of(map_ref)
    picks = [chosen(column, slot).astype(jnp.float32).astype(jnp.bfloat16) for slot in range(2)]
    rows_ref[...] = jnp.zeros_like(rows_ref)
    near_ref[...] = jnp.zeros_like(near_ref)
    for row in range(3):
        parts = [jnp.zeros((LANES, LANES), jnp.float32) for _ in range(2)]
        for half in range(2):
            cells = joined(piece_refs, 2 * placed(own, row) + half)
            drift = jnp.dot(turned, cells, preferred_element_type=jnp.float32)
            lanes = slice(half * LANES, (half + 1) * LANES)
            near_ref[row : row + 1, lanes] = drift[0:1]
            near_ref[8 + row : 9 + row, lanes] = drift[64:65]
            narrow = drift.astype(jnp.bfloat16)
            for slot in range(2):
                parts[slot] = parts[slot] + lax.dot_general(
                    picks[slot][:, lanes],
                    narrow,
                    (((1,), (1,)), ((), ())),
                    preferred_element_type=jnp.float32,
                )
        for slot in range(2):
            rows_ref[pl.ds(slot * 3 + row, LANES, stride=8), :] = parts[slot]
    parts = sems.shape[0]
    size = rows_ref.shape[0] // parts
    copies = []
    for part in range(parts):
        span = pl.ds(part * size, size)
        routed_ref[span, :] = rows_ref[span, :].astype(jnp.bfloat16)
        copies.append(
            pltpu.make_async_copy(routed_ref.at[span], routed_hbm.at[span], sems.at[part])
        )
        copies[-1].start()
    for copy in copies:
        copy.wait()


def wave_kernel(
    count,
    ids_ref,
    pair_hbm,
    coef_hbm,
    speeds_hbm,
    inner_hbm,
    outer_hbm,
    surface_ref,
    near_ref,
    weights_ref,
    wet_ref,
    *refs,
):
    piece_refs = refs[:count]
    (
        out_hbm,
        pair_ref,
        coef_ref,
        speeds_ref,
        halo_ref,
        out_ref,
        field_ref,
        cur_ref,
        turn_ref,
        beside_ref,
        in_sems,
        out_sems,
        *acc_refs,
    ) = refs[count:]
    local_bins = piece_refs[0].shape[1]
    bins = count * local_bins
    pairs = coef_ref.shape[0]

    core = ids_ref[0] & 1
    moves = (
        (inner_hbm, halo_ref.at[1 - core]),
        (outer_hbm, halo_ref.at[core]),
        (speeds_hbm, speeds_ref),
        (pair_hbm, pair_ref),
        (coef_hbm, coef_ref),
    )
    loads = [
        pltpu.make_async_copy(src, dst, in_sems.at[at]) for at, (src, dst) in enumerate(moves)
    ]
    for copy in loads:
        copy.start()
    own = ids_ref[0]
    turn_ref[...] = jnp.zeros_like(turn_ref)

    columns = 2 * LANES
    given = lax.broadcasted_iota(jnp.int32, (columns, 2 * columns), 0)
    taken = lax.broadcasted_iota(jnp.int32, (columns, 2 * columns), 1)
    pick = given == jnp.where(taken < columns, taken - 1, taken - columns + 1)
    pick = pick.astype(jnp.float32)
    narrow_pick = pick.astype(jnp.bfloat16)
    for row in range(3):
        cells = jnp.concatenate(
            [joined(piece_refs, 2 * row + half) for half in range(2)], axis=1
        )
        beside = jnp.dot(cells, narrow_pick, preferred_element_type=jnp.float32)
        for part in range(4):
            beside_ref[row, part] = beside[:, part * LANES : (part + 1) * LANES].astype(
                jnp.bfloat16
            )

    loads[0].wait()
    loads[1].wait()
    weights = weights_ref[...]
    for side in range(2):
        for half in range(2):
            blocks = [halo_ref[side, ids_ref[1 + side] ^ block, half] for block in range(count)]
            cells = jnp.concatenate(blocks, axis=0)
            drift = jnp.dot(weights, cells, preferred_element_type=jnp.float32)
            lanes = slice(half * LANES, (half + 1) * LANES)
            cur_ref[24 + side : 25 + side, lanes] = drift[0:1]
            cur_ref[32 + side : 33 + side, lanes] = drift[16:17]
    for row in range(5):
        if row in (0, 4):
            side = 0 if row == 0 else 1
            east = cur_ref[24 + side : 25 + side, :]
            north = cur_ref[32 + side : 33 + side, :]
        else:
            east = near_ref[row - 1 : row, :]
            north = near_ref[8 + row - 1 : 8 + row, :]
        fixed_east = surface_ref[2 * row : 2 * row + 1, :]
        wet = surface_ref[2 * row + 1 : 2 * row + 2, :]
        fixed_north = surface_ref[16 + 2 * row : 17 + 2 * row, :]
        factor = (DT_OCEAN * CORIOLIS) * wet
        cur_ref[row : row + 1, :] = CURRENT_SCALE * jnp.tanh(fixed_east + factor * north)
        cur_ref[8 + row : 9 + row, :] = CURRENT_SCALE * jnp.tanh(fixed_north - factor * east)
    for row in range(3):
        wet = wet_ref[pl.ds(own * 3 + row, 1), :]
        cur_ref[16 + row : 17 + row, :] = wet.astype(jnp.float32)

    near_cur = jnp.dot(
        cur_ref[8:16, :], pick, precision=HIGHEST, preferred_element_type=jnp.float32
    )
    cur_ref[40:48, :] = near_cur[:, :columns]
    cur_ref[48:56, :] = near_cur[:, columns:]
    loads[2].wait()

    def advect(piece_ref, turn, block, step):
        start = pl.multiple_of(step * BLOCK, BLOCK)
        first = block * local_bins + start
        span = pl.ds(start, BLOCK)
        below_at = ids_ref[1] ^ block
        above_at = ids_ref[2] ^ block
        speed_x = speeds_ref[0, pl.ds(pl.multiple_of(first, BLOCK), BLOCK), :]
        speed_y = speeds_ref[1, pl.ds(pl.multiple_of(first, BLOCK), BLOCK), :]

        def row_flux(energy, row, half):
            current = cur_ref[row : row + 1, half * LANES : (half + 1) * LANES]
            return (speed_x + current) * energy

        energy = [
            [
                piece_ref[2 * placed(own, row) + half, span, :].astype(jnp.float32)
                for half in range(2)
            ]
            for row in range(3)
        ]
        for half in range(2):
            flux = [row_flux(halo_ref[0, below_at, half, span, :].astype(jnp.float32), 0, half)]
            flux += [row_flux(energy[row][half], row + 1, half) for row in range(3)]
            flux += [row_flux(halo_ref[1, above_at, half, span, :].astype(jnp.float32), 4, half)]
            for row in range(3):
                energy[row][half] = (
                    energy[row][half],
                    energy[row][half]
                    - jnp.abs(flux[row + 1])
                    + jnp.maximum(flux[row], 0.0)
                    - jnp.minimum(flux[row + 2], 0.0),
                )
        for row in range(3):
            for half in range(2):
                old, value = energy[row][half]
                lanes = slice(half * LANES, (half + 1) * LANES)
                at_row = placed(own, row)
                spot = pl.ds(pl.multiple_of(turn * local_bins + start, BLOCK), BLOCK)

                def side(at, cells, row=row, lanes=lanes):
                    return (speed_y + cur_ref[at + 1 + row : at + 2 + row, lanes]) * cells

                left = side(40, beside_ref[at_row, half, spot, :].astype(jnp.float32))
                right = side(48, beside_ref[at_row, 2 + half, spot, :].astype(jnp.float32))
                wet = cur_ref[16 + row : 17 + row, lanes]
                moved = value - jnp.abs(side(8, old))
                result = wet * (moved + jnp.maximum(left, 0.0) - jnp.minimum(right, 0.0))
                at = (2 * row + half) * PITCH
                turn_ref[at : at + BLOCK, :] = result
        zeros = jnp.zeros((8, LANES), jnp.float32)
        for item in range(BLOCK):
            rows = pl.ds(pl.multiple_of((first + item) * 8, 8), 8)
            tile = turn_ref[pl.ds(item, 8, stride=PITCH), :]
            field_ref[rows, :] = tile
            acc_refs[0][rows, :] = tile
            for ref in acc_refs[1:]:
                ref[rows, :] = zeros

    for turn, piece_ref in enumerate(piece_refs):
        block = own ^ turn

        def one(step, carry, piece_ref=piece_ref, turn=turn, block=block):
            advect(piece_ref, turn, block, step)
            return carry

        lax.fori_loop(0, local_bins // BLOCK, one, 0)
    loads[3].wait()
    loads[4].wait()

    def interact(step, carry):
        start = pl.multiple_of(step * UNROLL, UNROLL)
        firsts = pair_ref.at[pl.ds(start, UNROLL)]
        seconds = pair_ref.at[pl.ds(pairs + start, UNROLL)]
        targets = pair_ref.at[pl.ds(2 * pairs + start, UNROLL)]
        coefs = coef_ref.at[pl.ds(start, UNROLL)]
        for item in range(UNROLL):
            first = pl.ds(pl.multiple_of(firsts[item], 8), 8)
            second = pl.ds(pl.multiple_of(seconds[item], 8), 8)
            target = pl.ds(pl.multiple_of(targets[item], 8), 8)
            ref = acc_refs[item % ACCS]
            product = coefs[item : item + 1, :] * (field_ref[first, :] * field_ref[second, :])
            ref[target, :] = ref[target, :] + product
        return carry

    lax.fori_loop(0, pairs // UNROLL, interact, 0)

    def finish(step, carry):
        first = pl.multiple_of(step * BLOCK, BLOCK)
        for row in range(3):
            for half in range(2):
                rows = pl.ds(first * 8 + (2 * row + half), BLOCK, stride=8)
                total = acc_refs[0][rows, :]
                for ref in acc_refs[1:]:
                    total = total + ref[rows, :]
                out_ref[row, pl.ds(first, BLOCK), half * LANES : (half + 1) * LANES] = (
                    total.astype(jnp.bfloat16)
                )
        return carry

    parts = 6
    out_copies = []
    for part in range(parts):
        span = pl.ds(part * (bins // parts), bins // parts)
        each = bins // BLOCK // parts
        lax.fori_loop(part * each, (part + 1) * each, finish, 0)
        for row in range(3):
            out_copies.append(
                pltpu.make_async_copy(
                    out_ref.at[row, span], out_hbm.at[row, span], out_sems.at[3 * part + row]
                )
            )
            out_copies[-1].start()
    for copy in out_copies:
        copy.wait()


def ocean_kernel(currents_ref, recv_ref, wet_ref, out_ref, wide_ref, rows_ref):
    rows = currents_ref.shape[1]
    half = LANES // 2
    lane = lax.broadcasted_iota(jnp.int32, (rows, LANES), 1)
    place = lane & (half - 1)
    sign = jnp.where(lane < half, CORIOLIS, -CORIOLIS)
    wet = wet_columns(wet_ref)
    wide_ref[...] = recv_ref[...].astype(jnp.float32)
    for slot in range(2):
        for row in range(3):
            rows_ref[pl.ds(row, LANES, stride=3), :] = wide_ref[
                pl.ds(slot * 3 + row, LANES, stride=8), :
            ]
        x = currents_ref[slot]
        upper = jnp.where(place == 0, x, pltpu.roll(x, 1, 1))
        lower = jnp.where(place == half - 1, x, pltpu.roll(x, LANES - 1, 1))
        cross = sign * pltpu.roll(x + rows_ref[...], half, 1)
        mixed = upper + lower - 2.0 * x
        out_ref[slot] = wet[:, slot : slot + 1] * (x + DT_OCEAN * (cross + MIXING * mixed))


def wave_program(ids, pair_rows, coefs, speeds, inner, outer, surface, near, weights, wet, *pieces):
    f32 = jnp.float32
    count = len(pieces)
    columns = wet.shape[1]
    rows = wet.shape[0] // count
    bins = speeds.shape[1]
    return call(
        functools.partial(wave_kernel, count),
        jax.ShapeDtypeStruct((rows, bins, columns), jnp.bfloat16),
        [in_smem(), anywhere()] + [in_hbm()] * 4 + [in_vmem()] * (4 + count),
        in_hbm(),
        [
            SMEM(pair_rows.shape, jnp.int32),
            VMEM(coefs.shape, f32),
            VMEM(speeds.shape, f32),
            VMEM((2, *inner.shape), jnp.bfloat16),
            VMEM((rows, bins, columns), jnp.bfloat16),
            VMEM((bins * 8, LANES), f32),
            VMEM((56, columns), f32),
            VMEM((8 * PITCH, LANES), f32),
            VMEM((rows, 4, bins, LANES), jnp.bfloat16),
            pltpu.SemaphoreType.DMA((5,)),
            pltpu.SemaphoreType.DMA((18,)),
        ]
        + [VMEM((bins * 8, LANES), f32)] * ACCS,
        40_000_000,
        8_000_000,
        (
            ids,
            pair_rows,
            *kept_in(pltpu.HBM, coefs, speeds, inner, outer),
            surface,
            near,
            weights,
            wet,
            *kept_in(VMEM, *pieces),
        ),
        WAVE_LIMIT,
    )


def per_device(
    spectrum,
    group_speed,
    stokes_kernel,
    pair_bins,
    pair_coef,
    currents,
    col_map,
    wave_wet,
    ocean_wet,
):
    local_bins, tile_rows, columns = spectrum.shape
    space_count = lax.axis_size("space")
    bins_count = lax.axis_size("bins")
    devices = space_count * bins_count
    bins = local_bins * bins_count
    pairs = pair_bins.shape[1]
    both = ("space", "bins")
    f32 = jnp.float32
    bf16 = jnp.bfloat16
    space_at = lax.axis_index("space")
    bins_at = lax.axis_index("bins")

    near_ids = [lax.rem(bins_at + step, bins_count) for step in (bins_count - 1, 1)]
    ids = jnp.stack([bins_at, *near_ids, space_at]).astype(jnp.int32)

    order = (4, 5, 3, 6, 2, 7, 1, 0)
    piece_shape = (CHUNKS, local_bins, LANES)
    sent = call(
        functools.partial(pack_kernel, order),
        [jax.ShapeDtypeStruct(piece_shape, bf16)]
        + [
            pltpu.HBM((CHUNKS - turn % 2, local_bins, LANES), bf16)
            for turn in range(1, bins_count)
        ],
        [in_smem(), in_hbm(), in_hbm()],
        [in_vmem()] + [in_hbm()] * (bins_count - 1),
        [
            VMEM(spectrum.shape, bf16),
            VMEM((2, local_bins * tile_rows, LANES), f32),
            VMEM(stokes_kernel.shape, bf16),
            VMEM((bins_count - 1, *piece_shape), bf16),
            pltpu.SemaphoreType.DMA((4,)),
            pltpu.SemaphoreType.DMA((bins_count, 4)),
        ],
        2_000_000,
        4_000_000,
        (
            ids,
            pltpu.with_memory_space_constraint(spectrum, pltpu.HBM),
            pltpu.with_memory_space_constraint(stokes_kernel, pltpu.HBM),
        ),
    )
    pieces = [sent[0]] * bins_count
    for turn in order[:-1]:
        partners = [(at, at ^ turn) for at in range(bins_count)]
        pieces[turn] = lax.ppermute(sent[turn], "bins", partners)

    surface = call(
        surface_kernel,
        jax.ShapeDtypeStruct((devices, LANES), f32),
        [in_smem()] + [in_vmem()] * 3,
        in_vmem(),
        [VMEM((2 * ROW_GAP, LANES), f32)],
        4_000_000,
        500_000,
        (ids, currents, ocean_wet, group_speed),
    )
    arrived = lax.all_to_all(surface, both, split_axis=0, concat_axis=0, tiled=True)
    map_row = col_map.reshape(1, -1)
    coefs, pair_rows = call(
        pairs_kernel,
        (
            pltpu.HBM((pairs, LANES), f32),
            jax.ShapeDtypeStruct((3 * pairs // LANES, LANES), jnp.int32),
        ),
        [in_vmem()] * 2,
        (in_hbm(), in_vmem()),
        [VMEM((pairs, LANES), f32), pltpu.SemaphoreType.DMA((4,))],
        1_000_000,
        2_500_000,
        (pair_coef.reshape(-1, LANES), pair_bins),
    )
    surface_rows, speed_rows = call(
        tables_kernel,
        (
            jax.ShapeDtypeStruct((32, columns), f32),
            pltpu.HBM((2, bins, LANES), f32),
        ),
        [in_vmem()] * 2,
        (in_vmem(), in_hbm()),
        [VMEM((2, bins, LANES), f32), pltpu.SemaphoreType.DMA((2,))],
        600_000_000,
        1_300_000,
        (arrived.reshape(devices, LANES), map_row),
    )

    halo_shape = (bins_count, 2, local_bins, LANES)
    stokes_shape = (bins_count // 2, local_bins, LANES)
    inner, outer, stokes = call(
        edges_kernel,
        [jax.ShapeDtypeStruct(halo_shape, bf16)] * 2 + [jax.ShapeDtypeStruct(stokes_shape, bf16)],
        [in_vmem()] * bins_count,
        [in_vmem()] * 3,
        [],
        1_000_000,
        2_400_000,
        tuple(pieces),
    )
    outward = [(at, at + 1) for at in range(1, devices - 1, 2)]
    outward += [(at + 1, at) for at, _ in outward]
    outer = lax.ppermute(outer, both, outward)
    within = [(at, at ^ 1) for at in range(devices)]
    inner = lax.ppermute(inner, both, within)
    stokes = lax.ppermute(stokes, both, within)

    routed, near, weights = call(
        functools.partial(drift_kernel, bins_count),
        (
            pltpu.HBM((devices * 8, LANES), bf16),
            jax.ShapeDtypeStruct((16, columns), f32),
            jax.ShapeDtypeStruct((32, bins), bf16),
        ),
        [in_smem()] + [in_vmem()] * (2 + bins_count),
        (in_hbm(), in_vmem(), in_vmem()),
        [
            VMEM((devices * 8, LANES), f32),
            VMEM((bins_count, local_bins, LANES), bf16),
            VMEM((devices * 8, LANES), bf16),
            pltpu.SemaphoreType.DMA((4,)),
        ],
        300_000_000,
        2_500_000,
        (ids, map_row, stokes, *pieces),
    )
    routed = lax.all_to_all(
        routed.reshape(devices, 8, LANES), both, split_axis=0, concat_axis=0, tiled=True
    )
    routed = routed.reshape(devices * 8, LANES)

    new_spectrum = wave_program(
        ids,
        pair_rows.reshape(-1),
        coefs,
        speed_rows,
        inner,
        outer,
        surface_rows,
        near,
        weights,
        wave_wet,
        *pieces,
    )
    new_currents = call(
        ocean_kernel,
        jax.ShapeDtypeStruct(currents.shape, f32),
        [in_vmem()] * 3,
        in_vmem(),
        [VMEM((devices * 8, LANES), f32), VMEM((currents.shape[1], LANES), f32)],
        4_000_000,
        1_500_000,
        (currents, routed, ocean_wet),
    )
    return (jnp.transpose(new_spectrum, (1, 0, 2)), new_currents)


def solution(mesh):
    placed = (
        P("bins", "space", None),
        P(None, "bins"),
        P("bins", None),
        P(),
        P(),
        P(("space", "bins"), None, None),
        P(),
        P("space", None),
        P(("space", "bins"), None),
    )

    return jax.shard_map(
        per_device,
        mesh=mesh,
        in_specs=placed,
        out_specs=(P(None, ("space", "bins"), None), P(("space", "bins"), None, None)),
        check_vma=False,
    )
```

```python
import functools

import jax
import jax.numpy as jnp
from jax import lax
from jax.experimental import pallas as pl
from jax.experimental.pallas import tpu as pltpu
from jax.sharding import PartitionSpec as P


DT_OCEAN = 0.5
CORIOLIS = 0.8
MIXING = 0.4
CURRENT_SCALE = 0.15
DT_SOURCE = 0.5

LANES = 128
ACCS = 3
WAVE_LIMIT = 42
CHUNKS = 7
UNROLL = 144
BLOCK = 16
PITCH = 24
ROW_GAP = 400
SPEED_LANE = 32
PIECES = 16
HIGHEST = lax.Precision.HIGHEST
VMEM = pltpu.VMEM
SMEM = pltpu.SMEM


def in_vmem():
    return pl.BlockSpec(memory_space=VMEM)


def in_smem():
    return pl.BlockSpec(memory_space=SMEM)


def anywhere():
    return pl.BlockSpec(memory_space=pl.ANY)


def in_hbm():
    return pl.BlockSpec(memory_space=pltpu.HBM)


def kept_in(space, *values):
    return [pltpu.with_memory_space_constraint(value, space) for value in values]


def call(body, out_shape, ins, outs, scratch, flops, moved, args, limit=16):
    return pl.pallas_call(
        body,
        out_shape=out_shape,
        in_specs=ins,
        out_specs=outs,
        scratch_shapes=scratch,
        compiler_params=pltpu.CompilerParams(vmem_limit_bytes=limit * 2**20),
        cost_estimate=pl.CostEstimate(flops=flops, bytes_accessed=moved, transcendentals=0),
    )(*args)


def placed(device, row):
    return row + (device & 1) * (2 - 2 * row)


def pack_kernel(order, ids_ref, spectrum_hbm, stokes_hbm, *refs):
    count = len(order)
    out_refs = refs[:count]
    narrow_ref, wide_ref, stokes_ref, piece_ref, in_sems, out_sems = refs[count:]
    local_bins, tile_rows, _ = spectrum_hbm.shape
    rows = tile_rows // count
    chunks = in_sems.shape[0] - 1
    part = local_bins // chunks
    loads = []
    for chunk in range(chunks):
        span = pl.ds(chunk * part, part)
        loads.append(
            pltpu.make_async_copy(spectrum_hbm.at[span], narrow_ref.at[span], in_sems.at[chunk])
        )
    loads.append(pltpu.make_async_copy(stokes_hbm, stokes_ref, in_sems.at[chunks]))
    for copy in loads:
        copy.start()
    own = ids_ref[0]
    stores = []
    for chunk in range(chunks):
        loads[chunk].wait()
        first = chunk * part
        span = pl.ds(first, part)
        for half in range(2):
            lanes = slice(half * LANES, (half + 1) * LANES)
            value = narrow_ref[first : first + part, :, lanes].astype(jnp.float32)
            wide_ref[half, first * tile_rows : (first + part) * tile_rows] = value.reshape(
                part * tile_rows, LANES
            )
        for turn in order:
            target = own ^ turn
            base = target * rows + first * tile_rows
            ref = piece_ref.at[turn - 1] if turn else out_refs[0]
            for row in range(rows):
                for half in range(2):
                    value = wide_ref[
                        half, pl.ds(base + placed(target, row), part, stride=tile_rows), :
                    ]
                    ref[2 * row + half, first : first + part, :] = value.astype(jnp.bfloat16)
            if turn:
                stores.append(
                    pltpu.make_async_copy(
                        piece_ref.at[turn - 1, pl.ds(0, 6), span],
                        out_refs[turn].at[pl.ds(0, 6), span],
                        out_sems.at[turn, chunk],
                    )
                )
                stores[-1].start()
        if chunk == 0:
            loads[chunks].wait()
            out_refs[0][6] = stokes_ref[...]
            for turn in range(2, count, 2):
                stores.append(
                    pltpu.make_async_copy(
                        stokes_ref, out_refs[turn].at[6], out_sems.at[turn, chunks]
                    )
                )
                stores[-1].start()
    for copy in stores:
        copy.wait()


def joined(refs, chunk):
    return jnp.concatenate([ref[chunk] for ref in refs], axis=0)


def edges_kernel(*refs):
    inner_ref, outer_ref, stokes_ref = refs[-3:]
    for turn, ref in enumerate(refs[:-3]):
        outer_ref[turn] = ref[0:2]
        inner_ref[turn] = ref[4:6]
        if turn % 2 == 0:
            stokes_ref[turn // 2] = ref[6]


def wet_columns(wet_ref):
    wet = wet_ref[...].astype(jnp.float32)
    rows = wet.shape[1]
    return jnp.concatenate([wet, jnp.zeros((6, rows), jnp.float32)], axis=0).T


def surface_kernel(ids_ref, currents_ref, wet_ref, speed_ref, out_ref, rows_ref):
    rows = currents_ref.shape[1]
    half = LANES // 2
    lane = lax.broadcasted_iota(jnp.int32, (rows, LANES), 1)
    wet = wet_columns(wet_ref)
    sign = jnp.where(lane < half, CORIOLIS, -CORIOLIS)
    kept = (lane == 0) | (lane == 1) | (lane == half)
    rows_ref[...] = jnp.zeros_like(rows_ref)
    for slot in range(2):
        x = currents_ref[slot]
        cross = sign * pltpu.roll(x, half, 1)
        below = pltpu.roll(x, LANES - 1, 1)
        column = wet[:, slot : slot + 1]
        value = column * (x + DT_OCEAN * (cross + MIXING * (below - x)))
        value = jnp.where(lane == 1, column, value)
        rows_ref[pl.ds(slot * ROW_GAP + 8, rows), :] = jnp.where(kept, value, 0.0)
    local_bins = speed_ref.shape[1]
    piece = local_bins // PIECES
    index = lax.broadcasted_iota(jnp.int32, (local_bins, LANES), 0) - ids_ref[3] * piece
    place = lax.broadcasted_iota(jnp.int32, (local_bins, LANES), 1) - SPEED_LANE
    inside = (index >= 0) & (index < piece)
    pick = inside & ((place == index) | (place == index + piece))
    split = jnp.concatenate(thirds(speed_ref[...]), axis=0)
    found = jnp.dot(
        split,
        pick.astype(jnp.float32).astype(jnp.bfloat16),
        preferred_element_type=jnp.float32,
    )
    found = found[0:2] + found[2:4] + found[4:6]
    spot = lax.broadcasted_iota(jnp.int32, (1, LANES), 1)
    speeds = jnp.where(spot < SPEED_LANE + piece, found[0:1], found[1:2])
    total = jnp.broadcast_to(speeds, (LANES, LANES))
    for slot in range(2):
        for row in range(5):
            part = rows_ref[pl.ds(slot * ROW_GAP + 7 + row, LANES, stride=3), :]
            shift = 2 * (slot * 5 + row)
            total = total + (pltpu.roll(part, shift, 1) if shift else part)
    out_ref[...] = total


def columns_of(map_ref):
    row = jnp.broadcast_to(map_ref[...].astype(jnp.float32), (LANES, LANES))
    column = row.T
    return jnp.concatenate([column, column], axis=1)


def chosen(column, slot):
    index = lax.broadcasted_iota(jnp.int32, column.shape, 1).astype(jnp.float32)
    return (2.0 * column + float(slot)) == index


def thirds(value):
    high = value.astype(jnp.bfloat16)
    rest = value - high.astype(jnp.float32)
    middle = rest.astype(jnp.bfloat16)
    low = (rest - middle.astype(jnp.float32)).astype(jnp.bfloat16)
    return [high, middle, low]


def pairs_kernel(coef_ref, pair_ref, coefs_hbm, rows_ref, coefs_ref, sems):
    blocks = coef_ref.shape[0]
    copies = []
    for block in range(blocks):
        lanes = slice(block * LANES, (block + 1) * LANES)
        for side in range(3):
            at = side * blocks + block
            rows_ref[at : at + 1, :] = pair_ref[side : side + 1, lanes] * 8
        row = DT_SOURCE * coef_ref[block : block + 1, :]
        coefs_ref[lanes, :] = jnp.broadcast_to(row, (LANES, LANES)).T
        if (block + 1) % (blocks // 4) == 0:
            span = pl.ds((block + 1 - blocks // 4) * LANES, blocks // 4 * LANES)
            copies.append(
                pltpu.make_async_copy(
                    coefs_ref.at[span], coefs_hbm.at[span], sems.at[len(copies)]
                )
            )
            copies[-1].start()
    for copy in copies:
        copy.wait()


def tables_kernel(recv_ref, map_ref, surface_ref, speeds_hbm, speeds_ref, sems):
    bf16 = jnp.bfloat16
    parts = thirds(recv_ref[...])
    copies = []
    bins = speeds_ref.shape[1]
    lane = lax.broadcasted_iota(jnp.int32, (bins, LANES), 1)
    index = lax.broadcasted_iota(jnp.int32, (bins, LANES), 0)
    first = ((lane & 7) * 16 + (lane >> 3)) * 9
    own = ((index >= first) & (index < first + 9)).astype(jnp.float32).astype(bf16)
    rows = [jnp.dot(own, part, preferred_element_type=jnp.float32) for part in parts]
    place = index - ((index * 7282) >> 16) * 9
    ones = jnp.ones((LANES, LANES), bf16)
    for part in range(2):
        mine = lane == place + (SPEED_LANE + 9 * part)
        total = jnp.zeros((bins, LANES), jnp.float32)
        for value in rows:
            kept = jnp.where(mine, value, 0.0).astype(bf16)
            total = total + jnp.dot(kept, ones, preferred_element_type=jnp.float32)
        speeds_ref[part] = total
        copies.append(
            pltpu.make_async_copy(speeds_ref.at[part], speeds_hbm.at[part], sems.at[part])
        )
        copies[-1].start()
    turned = thirds(recv_ref[...].T)
    column = columns_of(map_ref)
    found = []
    for slot in range(2):
        pick = chosen(column, slot).astype(jnp.float32).astype(bf16)
        found.append(
            sum(jnp.dot(part, pick, preferred_element_type=jnp.float32) for part in turned)
        )
    surface_ref[...] = jnp.zeros_like(surface_ref)
    surface_ref[0:10, :] = found[0][0:10] + found[1][10:20]
    surface_ref[16:26, :] = found[0][64:74] + found[1][74:84]
    for copy in copies:
        copy.wait()


def drift_kernel(count, ids_ref, map_ref, other_ref, *refs):
    piece_refs = refs[:count]
    routed_hbm, near_ref, weights_ref, rows_ref, stokes_ref, routed_ref, sems = refs[count:]
    own = ids_ref[0]
    stokes = [
        other_ref[turn // 2] if turn % 2 else ref[6] for turn, ref in enumerate(piece_refs)
    ]
    for turn, value in enumerate(stokes):
        stokes_ref[own ^ turn] = value
    in_order = stokes_ref[...].reshape(-1, LANES).T
    weights_ref[0:16, :] = in_order[0:16]
    weights_ref[16:32, :] = in_order[64:80]
    turned = jnp.concatenate(stokes, axis=0).T
    column = columns_of(map_ref)
    picks = [chosen(column, slot).astype(jnp.float32).astype(jnp.bfloat16) for slot in range(2)]
    rows_ref[...] = jnp.zeros_like(rows_ref)
    near_ref[...] = jnp.zeros_like(near_ref)
    for row in range(3):
        parts = [jnp.zeros((LANES, LANES), jnp.float32) for _ in range(2)]
        for half in range(2):
            cells = joined(piece_refs, 2 * placed(own, row) + half)
            drift = jnp.dot(turned, cells, preferred_element_type=jnp.float32)
            lanes = slice(half * LANES, (half + 1) * LANES)
            near_ref[row : row + 1, lanes] = drift[0:1]
            near_ref[8 + row : 9 + row, lanes] = drift[64:65]
            narrow = drift.astype(jnp.bfloat16)
            for slot in range(2):
                parts[slot] = parts[slot] + lax.dot_general(
                    picks[slot][:, lanes],
                    narrow,
                    (((1,), (1,)), ((), ())),
                    preferred_element_type=jnp.float32,
                )
        for slot in range(2):
            rows_ref[pl.ds(slot * 3 + row, LANES, stride=8), :] = parts[slot]
    parts = sems.shape[0]
    size = rows_ref.shape[0] // parts
    copies = []
    for part in range(parts):
        span = pl.ds(part * size, size)
        routed_ref[span, :] = rows_ref[span, :].astype(jnp.bfloat16)
        copies.append(
            pltpu.make_async_copy(routed_ref.at[span], routed_hbm.at[span], sems.at[part])
        )
        copies[-1].start()
    for copy in copies:
        copy.wait()


def wave_kernel(
    count,
    ids_ref,
    pair_hbm,
    coef_hbm,
    speeds_hbm,
    inner_hbm,
    outer_hbm,
    surface_ref,
    near_ref,
    weights_ref,
    wet_ref,
    *refs,
):
    piece_refs = refs[:count]
    (
        out_hbm,
        pair_ref,
        coef_ref,
        speeds_ref,
        halo_ref,
        out_ref,
        field_ref,
        cur_ref,
        turn_ref,
        beside_ref,
        in_sems,
        out_sems,
        *acc_refs,
    ) = refs[count:]
    local_bins = piece_refs[0].shape[1]
    bins = count * local_bins
    pairs = coef_ref.shape[0]

    core = ids_ref[0] & 1
    moves = (
        (inner_hbm, halo_ref.at[1 - core]),
        (outer_hbm, halo_ref.at[core]),
        (speeds_hbm, speeds_ref),
        (pair_hbm, pair_ref),
        (coef_hbm, coef_ref),
    )
    loads = [
        pltpu.make_async_copy(src, dst, in_sems.at[at]) for at, (src, dst) in enumerate(moves)
    ]
    for copy in loads:
        copy.start()
    own = ids_ref[0]
    turn_ref[...] = jnp.zeros_like(turn_ref)

    columns = 2 * LANES
    given = lax.broadcasted_iota(jnp.int32, (columns, 2 * columns), 0)
    taken = lax.broadcasted_iota(jnp.int32, (columns, 2 * columns), 1)
    pick = given == jnp.where(taken < columns, taken - 1, taken - columns + 1)
    pick = pick.astype(jnp.float32)
    narrow_pick = pick.astype(jnp.bfloat16)
    for row in range(3):
        cells = jnp.concatenate(
            [joined(piece_refs, 2 * row + half) for half in range(2)], axis=1
        )
        beside = jnp.dot(cells, narrow_pick, preferred_element_type=jnp.float32)
        for part in range(4):
            beside_ref[row, part] = beside[:, part * LANES : (part + 1) * LANES]

    loads[0].wait()
    loads[1].wait()
    weights = weights_ref[...]
    for side in range(2):
        for half in range(2):
            blocks = [halo_ref[side, ids_ref[1 + side] ^ block, half] for block in range(count)]
            cells = jnp.concatenate(blocks, axis=0)
            drift = jnp.dot(weights, cells, preferred_element_type=jnp.float32)
            lanes = slice(half * LANES, (half + 1) * LANES)
            cur_ref[24 + side : 25 + side, lanes] = drift[0:1]
            cur_ref[32 + side : 33 + side, lanes] = drift[16:17]
    for row in range(5):
        if row in (0, 4):
            side = 0 if row == 0 else 1
            east = cur_ref[24 + side : 25 + side, :]
            north = cur_ref[32 + side : 33 + side, :]
        else:
            east = near_ref[row - 1 : row, :]
            north = near_ref[8 + row - 1 : 8 + row, :]
        fixed_east = surface_ref[2 * row : 2 * row + 1, :]
        wet = surface_ref[2 * row + 1 : 2 * row + 2, :]
        fixed_north = surface_ref[16 + 2 * row : 17 + 2 * row, :]
        factor = (DT_OCEAN * CORIOLIS) * wet
        cur_ref[row : row + 1, :] = CURRENT_SCALE * jnp.tanh(fixed_east + factor * north)
        cur_ref[8 + row : 9 + row, :] = CURRENT_SCALE * jnp.tanh(fixed_north - factor * east)
    for row in range(3):
        wet = wet_ref[pl.ds(own * 3 + row, 1), :]
        cur_ref[16 + row : 17 + row, :] = wet.astype(jnp.float32)

    near_cur = jnp.dot(
        cur_ref[8:16, :], pick, precision=HIGHEST, preferred_element_type=jnp.float32
    )
    cur_ref[40:48, :] = near_cur[:, :columns]
    cur_ref[48:56, :] = near_cur[:, columns:]
    loads[2].wait()

    def advect(piece_ref, turn, block, step):
        start = pl.multiple_of(step * BLOCK, BLOCK)
        first = block * local_bins + start
        span = pl.ds(start, BLOCK)
        below_at = ids_ref[1] ^ block
        above_at = ids_ref[2] ^ block
        speed_x = speeds_ref[0, pl.ds(pl.multiple_of(first, BLOCK), BLOCK), :]
        speed_y = speeds_ref[1, pl.ds(pl.multiple_of(first, BLOCK), BLOCK), :]

        def row_flux(energy, row, half):
            current = cur_ref[row : row + 1, half * LANES : (half + 1) * LANES]
            return (speed_x + current) * energy

        energy = [
            [
                piece_ref[2 * placed(own, row) + half, span, :].astype(jnp.float32)
                for half in range(2)
            ]
            for row in range(3)
        ]
        for half in range(2):
            flux = [row_flux(halo_ref[0, below_at, half, span, :].astype(jnp.float32), 0, half)]
            flux += [row_flux(energy[row][half], row + 1, half) for row in range(3)]
            flux += [row_flux(halo_ref[1, above_at, half, span, :].astype(jnp.float32), 4, half)]
            for row in range(3):
                energy[row][half] = (
                    energy[row][half],
                    energy[row][half]
                    - jnp.abs(flux[row + 1])
                    + jnp.maximum(flux[row], 0.0)
                    - jnp.minimum(flux[row + 2], 0.0),
                )
        for row in range(3):
            for half in range(2):
                old, value = energy[row][half]
                lanes = slice(half * LANES, (half + 1) * LANES)
                at_row = placed(own, row)
                spot = pl.ds(pl.multiple_of(turn * local_bins + start, BLOCK), BLOCK)

                def side(at, cells, row=row, lanes=lanes):
                    return (speed_y + cur_ref[at + 1 + row : at + 2 + row, lanes]) * cells

                left = side(40, beside_ref[at_row, half, spot, :])
                right = side(48, beside_ref[at_row, 2 + half, spot, :])
                wet = cur_ref[16 + row : 17 + row, lanes]
                moved = value - jnp.abs(side(8, old))
                result = wet * (moved + jnp.maximum(left, 0.0) - jnp.minimum(right, 0.0))
                at = (2 * row + half) * PITCH
                turn_ref[at : at + BLOCK, :] = result
        zeros = jnp.zeros((8, LANES), jnp.float32)
        for item in range(BLOCK):
            rows = pl.ds(pl.multiple_of((first + item) * 8, 8), 8)
            tile = turn_ref[pl.ds(item, 8, stride=PITCH), :]
            field_ref[rows, :] = tile
            acc_refs[0][rows, :] = tile
            for ref in acc_refs[1:]:
                ref[rows, :] = zeros

    for turn, piece_ref in enumerate(piece_refs):
        block = own ^ turn

        def one(step, carry, piece_ref=piece_ref, turn=turn, block=block):
            advect(piece_ref, turn, block, step)
            return carry

        lax.fori_loop(0, local_bins // BLOCK, one, 0)
    loads[3].wait()
    loads[4].wait()

    def interact(step, carry):
        start = pl.multiple_of(step * UNROLL, UNROLL)
        firsts = pair_ref.at[pl.ds(start, UNROLL)]
        seconds = pair_ref.at[pl.ds(pairs + start, UNROLL)]
        targets = pair_ref.at[pl.ds(2 * pairs + start, UNROLL)]
        coefs = coef_ref.at[pl.ds(start, UNROLL)]
        for item in range(UNROLL):
            first = pl.ds(pl.multiple_of(firsts[item], 8), 8)
            second = pl.ds(pl.multiple_of(seconds[item], 8), 8)
            target = pl.ds(pl.multiple_of(targets[item], 8), 8)
            ref = acc_refs[item % ACCS]
            product = coefs[item : item + 1, :] * (field_ref[first, :] * field_ref[second, :])
            ref[target, :] = ref[target, :] + product
        return carry

    lax.fori_loop(0, pairs // UNROLL, interact, 0)

    def finish(step, carry):
        first = pl.multiple_of(step * BLOCK, BLOCK)
        for row in range(3):
            for half in range(2):
                rows = pl.ds(first * 8 + (2 * row + half), BLOCK, stride=8)
                total = acc_refs[0][rows, :]
                for ref in acc_refs[1:]:
                    total = total + ref[rows, :]
                out_ref[row, pl.ds(first, BLOCK), half * LANES : (half + 1) * LANES] = (
                    total.astype(jnp.bfloat16)
                )
        return carry

    parts = 6
    out_copies = []
    for part in range(parts):
        span = pl.ds(part * (bins // parts), bins // parts)
        each = bins // BLOCK // parts
        lax.fori_loop(part * each, (part + 1) * each, finish, 0)
        for row in range(3):
            out_copies.append(
                pltpu.make_async_copy(
                    out_ref.at[row, span], out_hbm.at[row, span], out_sems.at[3 * part + row]
                )
            )
            out_copies[-1].start()
    for copy in out_copies:
        copy.wait()


def ocean_kernel(currents_ref, recv_ref, wet_ref, out_ref, wide_ref, rows_ref):
    rows = currents_ref.shape[1]
    half = LANES // 2
    lane = lax.broadcasted_iota(jnp.int32, (rows, LANES), 1)
    place = lane & (half - 1)
    sign = jnp.where(lane < half, CORIOLIS, -CORIOLIS)
    wet = wet_columns(wet_ref)
    wide_ref[...] = recv_ref[...].astype(jnp.float32)
    for slot in range(2):
        for row in range(3):
            rows_ref[pl.ds(row, LANES, stride=3), :] = wide_ref[
                pl.ds(slot * 3 + row, LANES, stride=8), :
            ]
        x = currents_ref[slot]
        upper = jnp.where(place == 0, x, pltpu.roll(x, 1, 1))
        lower = jnp.where(place == half - 1, x, pltpu.roll(x, LANES - 1, 1))
        cross = sign * pltpu.roll(x + rows_ref[...], half, 1)
        mixed = upper + lower - 2.0 * x
        out_ref[slot] = wet[:, slot : slot + 1] * (x + DT_OCEAN * (cross + MIXING * mixed))


def wave_program(ids, pair_rows, coefs, speeds, inner, outer, surface, near, weights, wet, *pieces):
    f32 = jnp.float32
    count = len(pieces)
    columns = wet.shape[1]
    rows = wet.shape[0] // count
    bins = speeds.shape[1]
    return call(
        functools.partial(wave_kernel, count),
        jax.ShapeDtypeStruct((rows, bins, columns), jnp.bfloat16),
        [in_smem(), anywhere()] + [in_hbm()] * 4 + [in_vmem()] * (4 + count),
        in_hbm(),
        [
            SMEM(pair_rows.shape, jnp.int32),
            VMEM(coefs.shape, f32),
            VMEM(speeds.shape, f32),
            VMEM((2, *inner.shape), jnp.bfloat16),
            VMEM((rows, bins, columns), jnp.bfloat16),
            VMEM((bins * 8, LANES), f32),
            VMEM((56, columns), f32),
            VMEM((8 * PITCH, LANES), f32),
            VMEM((rows, 4, bins, LANES), f32),
            pltpu.SemaphoreType.DMA((5,)),
            pltpu.SemaphoreType.DMA((18,)),
        ]
        + [VMEM((bins * 8, LANES), f32)] * ACCS,
        40_000_000,
        8_000_000,
        (
            ids,
            pair_rows,
            *kept_in(pltpu.HBM, coefs, speeds, inner, outer),
            surface,
            near,
            weights,
            wet,
            *kept_in(VMEM, *pieces),
        ),
        WAVE_LIMIT,
    )


def per_device(
    spectrum,
    group_speed,
    stokes_kernel,
    pair_bins,
    pair_coef,
    currents,
    col_map,
    wave_wet,
    ocean_wet,
):
    local_bins, tile_rows, columns = spectrum.shape
    space_count = lax.axis_size("space")
    bins_count = lax.axis_size("bins")
    devices = space_count * bins_count
    bins = local_bins * bins_count
    pairs = pair_bins.shape[1]
    both = ("space", "bins")
    f32 = jnp.float32
    bf16 = jnp.bfloat16
    space_at = lax.axis_index("space")
    bins_at = lax.axis_index("bins")

    near_ids = [lax.rem(bins_at + step, bins_count) for step in (bins_count - 1, 1)]
    ids = jnp.stack([bins_at, *near_ids, space_at]).astype(jnp.int32)

    order = (4, 5, 3, 6, 2, 7, 1, 0)
    piece_shape = (CHUNKS, local_bins, LANES)
    sent = call(
        functools.partial(pack_kernel, order),
        [jax.ShapeDtypeStruct(piece_shape, bf16)]
        + [
            pltpu.HBM((CHUNKS - turn % 2, local_bins, LANES), bf16)
            for turn in range(1, bins_count)
        ],
        [in_smem(), in_hbm(), in_hbm()],
        [in_vmem()] + [in_hbm()] * (bins_count - 1),
        [
            VMEM(spectrum.shape, bf16),
            VMEM((2, local_bins * tile_rows, LANES), f32),
            VMEM(stokes_kernel.shape, bf16),
            VMEM((bins_count - 1, *piece_shape), bf16),
            pltpu.SemaphoreType.DMA((4,)),
            pltpu.SemaphoreType.DMA((bins_count, 4)),
        ],
        2_000_000,
        4_000_000,
        (
            ids,
            pltpu.with_memory_space_constraint(spectrum, pltpu.HBM),
            pltpu.with_memory_space_constraint(stokes_kernel, pltpu.HBM),
        ),
    )
    pieces = [sent[0]] * bins_count
    for turn in order[:-1]:
        partners = [(at, at ^ turn) for at in range(bins_count)]
        pieces[turn] = lax.ppermute(sent[turn], "bins", partners)

    surface = call(
        surface_kernel,
        jax.ShapeDtypeStruct((devices, LANES), f32),
        [in_smem()] + [in_vmem()] * 3,
        in_vmem(),
        [VMEM((2 * ROW_GAP, LANES), f32)],
        4_000_000,
        500_000,
        (ids, currents, ocean_wet, group_speed),
    )
    arrived = lax.all_to_all(surface, both, split_axis=0, concat_axis=0, tiled=True)
    map_row = col_map.reshape(1, -1)
    coefs, pair_rows = call(
        pairs_kernel,
        (
            pltpu.HBM((pairs, LANES), f32),
            jax.ShapeDtypeStruct((3 * pairs // LANES, LANES), jnp.int32),
        ),
        [in_vmem()] * 2,
        (in_hbm(), in_vmem()),
        [VMEM((pairs, LANES), f32), pltpu.SemaphoreType.DMA((4,))],
        1_000_000,
        2_500_000,
        (pair_coef.reshape(-1, LANES), pair_bins),
    )
    surface_rows, speed_rows = call(
        tables_kernel,
        (
            jax.ShapeDtypeStruct((32, columns), f32),
            pltpu.HBM((2, bins, LANES), f32),
        ),
        [in_vmem()] * 2,
        (in_vmem(), in_hbm()),
        [VMEM((2, bins, LANES), f32), pltpu.SemaphoreType.DMA((2,))],
        600_000_000,
        1_300_000,
        (arrived.reshape(devices, LANES), map_row),
    )

    halo_shape = (bins_count, 2, local_bins, LANES)
    stokes_shape = (bins_count // 2, local_bins, LANES)
    inner, outer, stokes = call(
        edges_kernel,
        [jax.ShapeDtypeStruct(halo_shape, bf16)] * 2 + [jax.ShapeDtypeStruct(stokes_shape, bf16)],
        [in_vmem()] * bins_count,
        [in_vmem()] * 3,
        [],
        1_000_000,
        2_400_000,
        tuple(pieces),
    )
    outward = [(at, at + 1) for at in range(1, devices - 1, 2)]
    outward += [(at + 1, at) for at, _ in outward]
    outer = lax.ppermute(outer, both, outward)
    within = [(at, at ^ 1) for at in range(devices)]
    inner = lax.ppermute(inner, both, within)
    stokes = lax.ppermute(stokes, both, within)

    routed, near, weights = call(
        functools.partial(drift_kernel, bins_count),
        (
            pltpu.HBM((devices * 8, LANES), bf16),
            jax.ShapeDtypeStruct((16, columns), f32),
            jax.ShapeDtypeStruct((32, bins), bf16),
        ),
        [in_smem()] + [in_vmem()] * (2 + bins_count),
        (in_hbm(), in_vmem(), in_vmem()),
        [
            VMEM((devices * 8, LANES), f32),
            VMEM((bins_count, local_bins, LANES), bf16),
            VMEM((devices * 8, LANES), bf16),
            pltpu.SemaphoreType.DMA((4,)),
        ],
        300_000_000,
        2_500_000,
        (ids, map_row, stokes, *pieces),
    )
    routed = lax.all_to_all(
        routed.reshape(devices, 8, LANES), both, split_axis=0, concat_axis=0, tiled=True
    )
    routed = routed.reshape(devices * 8, LANES)

    new_spectrum = wave_program(
        ids,
        pair_rows.reshape(-1),
        coefs,
        speed_rows,
        inner,
        outer,
        surface_rows,
        near,
        weights,
        wave_wet,
        *pieces,
    )
    new_currents = call(
        ocean_kernel,
        jax.ShapeDtypeStruct(currents.shape, f32),
        [in_vmem()] * 3,
        in_vmem(),
        [VMEM((devices * 8, LANES), f32), VMEM((currents.shape[1], LANES), f32)],
        4_000_000,
        1_500_000,
        (currents, routed, ocean_wet),
    )
    return (jnp.transpose(new_spectrum, (1, 0, 2)), new_currents)


def solution(mesh):
    placed = (
        P("bins", "space", None),
        P(None, "bins"),
        P("bins", None),
        P(),
        P(),
        P(("space", "bins"), None, None),
        P(),
        P("space", None),
        P(("space", "bins"), None),
    )

    return jax.shard_map(
        per_device,
        mesh=mesh,
        in_specs=placed,
        out_specs=(P(None, ("space", "bins"), None), P(("space", "bins"), None, None)),
        check_vma=False,
    )
```

```python
import functools

import jax
import jax.numpy as jnp
from jax import lax
from jax.experimental import pallas as pl
from jax.experimental.pallas import tpu as pltpu
from jax.sharding import PartitionSpec as P


DT_OCEAN = 0.5
CORIOLIS = 0.8
MIXING = 0.4
CURRENT_SCALE = 0.15
DT_SOURCE = 0.5

LANES = 128
ACCS = 3
WAVE_LIMIT = 42
CHUNKS = 7
UNROLL = 144
BLOCK = 16
PITCH = 24
ROW_GAP = 400
SPEED_LANE = 32
PIECES = 16
HIGHEST = lax.Precision.HIGHEST
VMEM = pltpu.VMEM
SMEM = pltpu.SMEM


def in_vmem():
    return pl.BlockSpec(memory_space=VMEM)


def in_smem():
    return pl.BlockSpec(memory_space=SMEM)


def anywhere():
    return pl.BlockSpec(memory_space=pl.ANY)


def in_hbm():
    return pl.BlockSpec(memory_space=pltpu.HBM)


def kept_in(space, *values):
    return [pltpu.with_memory_space_constraint(value, space) for value in values]


def call(body, out_shape, ins, outs, scratch, flops, moved, args, limit=16):
    return pl.pallas_call(
        body,
        out_shape=out_shape,
        in_specs=ins,
        out_specs=outs,
        scratch_shapes=scratch,
        compiler_params=pltpu.CompilerParams(vmem_limit_bytes=limit * 2**20),
        cost_estimate=pl.CostEstimate(flops=flops, bytes_accessed=moved, transcendentals=0),
    )(*args)


def placed(device, row):
    return row + (device & 1) * (2 - 2 * row)


def pack_kernel(order, ids_ref, spectrum_hbm, stokes_hbm, *refs):
    count = len(order)
    out_refs = refs[:count]
    narrow_ref, wide_ref, stokes_ref, piece_ref, in_sems, out_sems = refs[count:]
    local_bins, tile_rows, _ = spectrum_hbm.shape
    rows = tile_rows // count
    chunks = in_sems.shape[0] - 1
    part = local_bins // chunks
    loads = []
    for chunk in range(chunks):
        span = pl.ds(chunk * part, part)
        loads.append(
            pltpu.make_async_copy(spectrum_hbm.at[span], narrow_ref.at[span], in_sems.at[chunk])
        )
    loads.append(pltpu.make_async_copy(stokes_hbm, stokes_ref, in_sems.at[chunks]))
    for copy in loads:
        copy.start()
    own = ids_ref[0]
    stores = []
    for chunk in range(chunks):
        loads[chunk].wait()
        first = chunk * part
        span = pl.ds(first, part)
        for half in range(2):
            lanes = slice(half * LANES, (half + 1) * LANES)
            value = narrow_ref[first : first + part, :, lanes].astype(jnp.float32)
            wide_ref[half, first * tile_rows : (first + part) * tile_rows] = value.reshape(
                part * tile_rows, LANES
            )
        for turn in order:
            target = own ^ turn
            base = target * rows + first * tile_rows
            ref = piece_ref.at[turn - 1] if turn else out_refs[0]
            for row in range(rows):
                for half in range(2):
                    value = wide_ref[
                        half, pl.ds(base + placed(target, row), part, stride=tile_rows), :
                    ]
                    ref[2 * row + half, first : first + part, :] = value.astype(jnp.bfloat16)
            if turn:
                stores.append(
                    pltpu.make_async_copy(
                        piece_ref.at[turn - 1, pl.ds(0, 6), span],
                        out_refs[turn].at[pl.ds(0, 6), span],
                        out_sems.at[turn, chunk],
                    )
                )
                stores[-1].start()
        if chunk == 0:
            loads[chunks].wait()
            out_refs[0][6] = stokes_ref[...]
            for turn in range(2, count, 2):
                stores.append(
                    pltpu.make_async_copy(
                        stokes_ref, out_refs[turn].at[6], out_sems.at[turn, chunks]
                    )
                )
                stores[-1].start()
    for copy in stores:
        copy.wait()


def joined(refs, chunk):
    return jnp.concatenate([ref[chunk] for ref in refs], axis=0)


def edges_kernel(*refs):
    inner_ref, outer_ref, stokes_ref = refs[-3:]
    for turn, ref in enumerate(refs[:-3]):
        outer_ref[turn] = ref[0:2]
        inner_ref[turn] = ref[4:6]
        if turn % 2 == 0:
            stokes_ref[turn // 2] = ref[6]


def wet_columns(wet_ref):
    wet = wet_ref[...].astype(jnp.float32)
    rows = wet.shape[1]
    return jnp.concatenate([wet, jnp.zeros((6, rows), jnp.float32)], axis=0).T


def surface_kernel(ids_ref, currents_ref, wet_ref, speed_ref, out_ref, rows_ref):
    rows = currents_ref.shape[1]
    half = LANES // 2
    lane = lax.broadcasted_iota(jnp.int32, (rows, LANES), 1)
    wet = wet_columns(wet_ref)
    sign = jnp.where(lane < half, CORIOLIS, -CORIOLIS)
    kept = (lane == 0) | (lane == 1) | (lane == half)
    rows_ref[...] = jnp.zeros_like(rows_ref)
    for slot in range(2):
        x = currents_ref[slot]
        cross = sign * pltpu.roll(x, half, 1)
        below = pltpu.roll(x, LANES - 1, 1)
        column = wet[:, slot : slot + 1]
        value = column * (x + DT_OCEAN * (cross + MIXING * (below - x)))
        value = jnp.where(lane == 1, column, value)
        rows_ref[pl.ds(slot * ROW_GAP + 8, rows), :] = jnp.where(kept, value, 0.0)
    local_bins = speed_ref.shape[1]
    piece = local_bins // PIECES
    index = lax.broadcasted_iota(jnp.int32, (local_bins, LANES), 0) - ids_ref[3] * piece
    place = lax.broadcasted_iota(jnp.int32, (local_bins, LANES), 1) - SPEED_LANE
    inside = (index >= 0) & (index < piece)
    pick = inside & ((place == index) | (place == index + piece))
    split = jnp.concatenate(thirds(speed_ref[...]), axis=0)
    found = jnp.dot(
        split,
        pick.astype(jnp.float32).astype(jnp.bfloat16),
        preferred_element_type=jnp.float32,
    )
    found = found[0:2] + found[2:4] + found[4:6]
    spot = lax.broadcasted_iota(jnp.int32, (1, LANES), 1)
    speeds = jnp.where(spot < SPEED_LANE + piece, found[0:1], found[1:2])
    total = jnp.broadcast_to(speeds, (LANES, LANES))
    for slot in range(2):
        for row in range(5):
            part = rows_ref[pl.ds(slot * ROW_GAP + 7 + row, LANES, stride=3), :]
            shift = 2 * (slot * 5 + row)
            total = total + (pltpu.roll(part, shift, 1) if shift else part)
    out_ref[...] = total


def columns_of(map_ref):
    row = jnp.broadcast_to(map_ref[...].astype(jnp.float32), (LANES, LANES))
    column = row.T
    return jnp.concatenate([column, column], axis=1)


def chosen(column, slot):
    index = lax.broadcasted_iota(jnp.int32, column.shape, 1).astype(jnp.float32)
    return (2.0 * column + float(slot)) == index


def thirds(value):
    high = value.astype(jnp.bfloat16)
    rest = value - high.astype(jnp.float32)
    middle = rest.astype(jnp.bfloat16)
    low = (rest - middle.astype(jnp.float32)).astype(jnp.bfloat16)
    return [high, middle, low]


def pairs_kernel(coef_ref, pair_ref, coefs_hbm, rows_ref, coefs_ref, sems):
    blocks = coef_ref.shape[0]
    copies = []
    for block in range(blocks):
        lanes = slice(block * LANES, (block + 1) * LANES)
        for side in range(3):
            at = side * blocks + block
            rows_ref[at : at + 1, :] = pair_ref[side : side + 1, lanes] * 8
        row = DT_SOURCE * coef_ref[block : block + 1, :]
        coefs_ref[lanes, :] = jnp.broadcast_to(row, (LANES, LANES)).T
        if (block + 1) % (blocks // 4) == 0:
            span = pl.ds((block + 1 - blocks // 4) * LANES, blocks // 4 * LANES)
            copies.append(
                pltpu.make_async_copy(
                    coefs_ref.at[span], coefs_hbm.at[span], sems.at[len(copies)]
                )
            )
            copies[-1].start()
    for copy in copies:
        copy.wait()


def tables_kernel(recv_ref, map_ref, surface_ref, speeds_hbm, speeds_ref, sems):
    bf16 = jnp.bfloat16
    parts = thirds(recv_ref[...])
    copies = []
    bins = speeds_ref.shape[1]
    lane = lax.broadcasted_iota(jnp.int32, (bins, LANES), 1)
    index = lax.broadcasted_iota(jnp.int32, (bins, LANES), 0)
    first = ((lane & 7) * 16 + (lane >> 3)) * 9
    own = ((index >= first) & (index < first + 9)).astype(jnp.float32).astype(bf16)
    rows = [jnp.dot(own, part, preferred_element_type=jnp.float32) for part in parts]
    place = index - ((index * 7282) >> 16) * 9
    ones = jnp.ones((3 * LANES, LANES), bf16)
    for part in range(2):
        mine = lane == place + (SPEED_LANE + 9 * part)
        kept = [jnp.where(mine, value, 0.0).astype(bf16) for value in rows]
        speeds_ref[part] = jnp.dot(
            jnp.concatenate(kept, axis=1), ones, preferred_element_type=jnp.float32
        )
        copies.append(
            pltpu.make_async_copy(speeds_ref.at[part], speeds_hbm.at[part], sems.at[part])
        )
        copies[-1].start()
    turned = thirds(recv_ref[...].T)
    column = columns_of(map_ref)
    found = []
    for slot in range(2):
        pick = chosen(column, slot).astype(jnp.float32).astype(bf16)
        found.append(
            sum(jnp.dot(part, pick, preferred_element_type=jnp.float32) for part in turned)
        )
    surface_ref[...] = jnp.zeros_like(surface_ref)
    surface_ref[0:10, :] = found[0][0:10] + found[1][10:20]
    surface_ref[16:26, :] = found[0][64:74] + found[1][74:84]
    for copy in copies:
        copy.wait()


def drift_kernel(count, ids_ref, map_ref, other_ref, *refs):
    piece_refs = refs[:count]
    routed_hbm, near_ref, weights_ref, rows_ref, stokes_ref, routed_ref, sems = refs[count:]
    own = ids_ref[0]
    stokes = [
        other_ref[turn // 2] if turn % 2 else ref[6] for turn, ref in enumerate(piece_refs)
    ]
    for turn, value in enumerate(stokes):
        stokes_ref[own ^ turn] = value
    in_order = stokes_ref[...].reshape(-1, LANES).T
    weights_ref[0:16, :] = in_order[0:16]
    weights_ref[16:32, :] = in_order[64:80]
    turned = jnp.concatenate(stokes, axis=0).T
    column = columns_of(map_ref)
    picks = [chosen(column, slot).astype(jnp.float32).astype(jnp.bfloat16) for slot in range(2)]
    rows_ref[...] = jnp.zeros_like(rows_ref)
    near_ref[...] = jnp.zeros_like(near_ref)
    for row in range(3):
        parts = [jnp.zeros((LANES, LANES), jnp.float32) for _ in range(2)]
        for half in range(2):
            cells = joined(piece_refs, 2 * placed(own, row) + half)
            drift = jnp.dot(turned, cells, preferred_element_type=jnp.float32)
            lanes = slice(half * LANES, (half + 1) * LANES)
            near_ref[row : row + 1, lanes] = drift[0:1]
            near_ref[8 + row : 9 + row, lanes] = drift[64:65]
            narrow = drift.astype(jnp.bfloat16)
            for slot in range(2):
                parts[slot] = parts[slot] + lax.dot_general(
                    picks[slot][:, lanes],
                    narrow,
                    (((1,), (1,)), ((), ())),
                    preferred_element_type=jnp.float32,
                )
        for slot in range(2):
            rows_ref[pl.ds(slot * 3 + row, LANES, stride=8), :] = parts[slot]
    parts = sems.shape[0]
    size = rows_ref.shape[0] // parts
    copies = []
    for part in range(parts):
        span = pl.ds(part * size, size)
        routed_ref[span, :] = rows_ref[span, :].astype(jnp.bfloat16)
        copies.append(
            pltpu.make_async_copy(routed_ref.at[span], routed_hbm.at[span], sems.at[part])
        )
        copies[-1].start()
    for copy in copies:
        copy.wait()


def wave_kernel(
    count,
    ids_ref,
    pair_hbm,
    coef_hbm,
    speeds_hbm,
    inner_hbm,
    outer_hbm,
    surface_ref,
    near_ref,
    weights_ref,
    wet_ref,
    *refs,
):
    piece_refs = refs[:count]
    (
        out_hbm,
        pair_ref,
        coef_ref,
        speeds_ref,
        halo_ref,
        out_ref,
        field_ref,
        cur_ref,
        turn_ref,
        beside_ref,
        in_sems,
        out_sems,
        *acc_refs,
    ) = refs[count:]
    local_bins = piece_refs[0].shape[1]
    bins = count * local_bins
    pairs = coef_ref.shape[0]

    core = ids_ref[0] & 1
    moves = (
        (inner_hbm, halo_ref.at[1 - core]),
        (outer_hbm, halo_ref.at[core]),
        (speeds_hbm, speeds_ref),
        (pair_hbm, pair_ref),
        (coef_hbm, coef_ref),
    )
    loads = [
        pltpu.make_async_copy(src, dst, in_sems.at[at]) for at, (src, dst) in enumerate(moves)
    ]
    for copy in loads:
        copy.start()
    own = ids_ref[0]
    turn_ref[...] = jnp.zeros_like(turn_ref)

    columns = 2 * LANES
    given = lax.broadcasted_iota(jnp.int32, (columns, 2 * columns), 0)
    taken = lax.broadcasted_iota(jnp.int32, (columns, 2 * columns), 1)
    pick = given == jnp.where(taken < columns, taken - 1, taken - columns + 1)
    pick = pick.astype(jnp.float32)
    narrow_pick = pick.astype(jnp.bfloat16)
    for row in range(3):
        cells = jnp.concatenate(
            [joined(piece_refs, 2 * row + half) for half in range(2)], axis=1
        )
        beside = jnp.dot(cells, narrow_pick, preferred_element_type=jnp.float32)
        for part in range(4):
            beside_ref[row, part] = beside[:, part * LANES : (part + 1) * LANES]

    loads[0].wait()
    loads[1].wait()
    weights = weights_ref[...]
    for side in range(2):
        for half in range(2):
            blocks = [halo_ref[side, ids_ref[1 + side] ^ block, half] for block in range(count)]
            cells = jnp.concatenate(blocks, axis=0)
            drift = jnp.dot(weights, cells, preferred_element_type=jnp.float32)
            lanes = slice(half * LANES, (half + 1) * LANES)
            cur_ref[24 + side : 25 + side, lanes] = drift[0:1]
            cur_ref[32 + side : 33 + side, lanes] = drift[16:17]
    for row in range(5):
        if row in (0, 4):
            side = 0 if row == 0 else 1
            east = cur_ref[24 + side : 25 + side, :]
            north = cur_ref[32 + side : 33 + side, :]
        else:
            east = near_ref[row - 1 : row, :]
            north = near_ref[8 + row - 1 : 8 + row, :]
        fixed_east = surface_ref[2 * row : 2 * row + 1, :]
        wet = surface_ref[2 * row + 1 : 2 * row + 2, :]
        fixed_north = surface_ref[16 + 2 * row : 17 + 2 * row, :]
        factor = (DT_OCEAN * CORIOLIS) * wet
        cur_ref[row : row + 1, :] = CURRENT_SCALE * jnp.tanh(fixed_east + factor * north)
        cur_ref[8 + row : 9 + row, :] = CURRENT_SCALE * jnp.tanh(fixed_north - factor * east)
    for row in range(3):
        wet = wet_ref[pl.ds(own * 3 + row, 1), :]
        cur_ref[16 + row : 17 + row, :] = wet.astype(jnp.float32)

    near_cur = jnp.dot(
        cur_ref[8:16, :], pick, precision=HIGHEST, preferred_element_type=jnp.float32
    )
    cur_ref[40:48, :] = near_cur[:, :columns]
    cur_ref[48:56, :] = near_cur[:, columns:]
    loads[2].wait()

    def advect(piece_ref, turn, block, step):
        start = pl.multiple_of(step * BLOCK, BLOCK)
        first = block * local_bins + start
        span = pl.ds(start, BLOCK)
        below_at = ids_ref[1] ^ block
        above_at = ids_ref[2] ^ block
        speed_x = speeds_ref[0, pl.ds(pl.multiple_of(first, BLOCK), BLOCK), :]
        speed_y = speeds_ref[1, pl.ds(pl.multiple_of(first, BLOCK), BLOCK), :]

        def row_flux(energy, row, half):
            current = cur_ref[row : row + 1, half * LANES : (half + 1) * LANES]
            return (speed_x + current) * energy

        energy = [
            [
                piece_ref[2 * placed(own, row) + half, span, :].astype(jnp.float32)
                for half in range(2)
            ]
            for row in range(3)
        ]
        for half in range(2):
            flux = [row_flux(halo_ref[0, below_at, half, span, :].astype(jnp.float32), 0, half)]
            flux += [row_flux(energy[row][half], row + 1, half) for row in range(3)]
            flux += [row_flux(halo_ref[1, above_at, half, span, :].astype(jnp.float32), 4, half)]
            for row in range(3):
                energy[row][half] = (
                    energy[row][half],
                    energy[row][half]
                    - jnp.abs(flux[row + 1])
                    + jnp.maximum(flux[row], 0.0)
                    - jnp.minimum(flux[row + 2], 0.0),
                )
        for row in range(3):
            for half in range(2):
                old, value = energy[row][half]
                lanes = slice(half * LANES, (half + 1) * LANES)
                at_row = placed(own, row)
                spot = pl.ds(pl.multiple_of(turn * local_bins + start, BLOCK), BLOCK)

                def side(at, cells, row=row, lanes=lanes):
                    return (speed_y + cur_ref[at + 1 + row : at + 2 + row, lanes]) * cells

                left = side(40, beside_ref[at_row, half, spot, :])
                right = side(48, beside_ref[at_row, 2 + half, spot, :])
                wet = cur_ref[16 + row : 17 + row, lanes]
                moved = value - jnp.abs(side(8, old))
                result = wet * (moved + jnp.maximum(left, 0.0) - jnp.minimum(right, 0.0))
                at = (2 * row + half) * PITCH
                turn_ref[at : at + BLOCK, :] = result
        zeros = jnp.zeros((8, LANES), jnp.float32)
        for item in range(BLOCK):
            rows = pl.ds(pl.multiple_of((first + item) * 8, 8), 8)
            tile = turn_ref[pl.ds(item, 8, stride=PITCH), :]
            field_ref[rows, :] = tile
            acc_refs[0][rows, :] = tile
            for ref in acc_refs[1:]:
                ref[rows, :] = zeros

    for turn, piece_ref in enumerate(piece_refs):
        block = own ^ turn

        def one(step, carry, piece_ref=piece_ref, turn=turn, block=block):
            advect(piece_ref, turn, block, step)
            return carry

        lax.fori_loop(0, local_bins // BLOCK, one, 0)
    loads[3].wait()
    loads[4].wait()

    def interact(step, carry):
        start = pl.multiple_of(step * UNROLL, UNROLL)
        firsts = pair_ref.at[pl.ds(start, UNROLL)]
        seconds = pair_ref.at[pl.ds(pairs + start, UNROLL)]
        targets = pair_ref.at[pl.ds(2 * pairs + start, UNROLL)]
        coefs = coef_ref.at[pl.ds(start, UNROLL)]
        for item in range(UNROLL):
            first = pl.ds(pl.multiple_of(firsts[item], 8), 8)
            second = pl.ds(pl.multiple_of(seconds[item], 8), 8)
            target = pl.ds(pl.multiple_of(targets[item], 8), 8)
            ref = acc_refs[item % ACCS]
            product = coefs[item : item + 1, :] * (field_ref[first, :] * field_ref[second, :])
            ref[target, :] = ref[target, :] + product
        return carry

    lax.fori_loop(0, pairs // UNROLL, interact, 0)

    def finish(step, carry):
        first = pl.multiple_of(step * BLOCK, BLOCK)
        for row in range(3):
            for half in range(2):
                rows = pl.ds(first * 8 + (2 * row + half), BLOCK, stride=8)
                total = acc_refs[0][rows, :]
                for ref in acc_refs[1:]:
                    total = total + ref[rows, :]
                out_ref[row, pl.ds(first, BLOCK), half * LANES : (half + 1) * LANES] = (
                    total.astype(jnp.bfloat16)
                )
        return carry

    parts = 9
    out_copies = []
    for part in range(parts):
        span = pl.ds(part * (bins // parts), bins // parts)
        each = bins // BLOCK // parts
        lax.fori_loop(part * each, (part + 1) * each, finish, 0)
        for row in range(3):
            out_copies.append(
                pltpu.make_async_copy(
                    out_ref.at[row, span], out_hbm.at[row, span], out_sems.at[3 * part + row]
                )
            )
            out_copies[-1].start()
    for copy in out_copies:
        copy.wait()


def ocean_kernel(currents_ref, recv_ref, wet_ref, out_ref, wide_ref, rows_ref):
    rows = currents_ref.shape[1]
    half = LANES // 2
    lane = lax.broadcasted_iota(jnp.int32, (rows, LANES), 1)
    place = lane & (half - 1)
    sign = jnp.where(lane < half, CORIOLIS, -CORIOLIS)
    wet = wet_columns(wet_ref)
    wide_ref[...] = recv_ref[...].astype(jnp.float32)
    for slot in range(2):
        for row in range(3):
            rows_ref[pl.ds(row, LANES, stride=3), :] = wide_ref[
                pl.ds(slot * 3 + row, LANES, stride=8), :
            ]
        x = currents_ref[slot]
        upper = jnp.where(place == 0, x, pltpu.roll(x, 1, 1))
        lower = jnp.where(place == half - 1, x, pltpu.roll(x, LANES - 1, 1))
        cross = sign * pltpu.roll(x + rows_ref[...], half, 1)
        mixed = upper + lower - 2.0 * x
        out_ref[slot] = wet[:, slot : slot + 1] * (x + DT_OCEAN * (cross + MIXING * mixed))


def wave_program(ids, pair_rows, coefs, speeds, inner, outer, surface, near, weights, wet, *pieces):
    f32 = jnp.float32
    count = len(pieces)
    columns = wet.shape[1]
    rows = wet.shape[0] // count
    bins = speeds.shape[1]
    return call(
        functools.partial(wave_kernel, count),
        jax.ShapeDtypeStruct((rows, bins, columns), jnp.bfloat16),
        [in_smem(), anywhere()] + [in_hbm()] * 4 + [in_vmem()] * (4 + count),
        in_hbm(),
        [
            SMEM(pair_rows.shape, jnp.int32),
            VMEM(coefs.shape, f32),
            VMEM(speeds.shape, f32),
            VMEM((2, *inner.shape), jnp.bfloat16),
            VMEM((rows, bins, columns), jnp.bfloat16),
            VMEM((bins * 8, LANES), f32),
            VMEM((56, columns), f32),
            VMEM((8 * PITCH, LANES), f32),
            VMEM((rows, 4, bins, LANES), f32),
            pltpu.SemaphoreType.DMA((5,)),
            pltpu.SemaphoreType.DMA((27,)),
        ]
        + [VMEM((bins * 8, LANES), f32)] * ACCS,
        40_000_000,
        8_000_000,
        (
            ids,
            pair_rows,
            *kept_in(pltpu.HBM, coefs, speeds, inner, outer),
            surface,
            near,
            weights,
            wet,
            *kept_in(VMEM, *pieces),
        ),
        WAVE_LIMIT,
    )


def per_device(
    spectrum,
    group_speed,
    stokes_kernel,
    pair_bins,
    pair_coef,
    currents,
    col_map,
    wave_wet,
    ocean_wet,
):
    local_bins, tile_rows, columns = spectrum.shape
    space_count = lax.axis_size("space")
    bins_count = lax.axis_size("bins")
    devices = space_count * bins_count
    bins = local_bins * bins_count
    pairs = pair_bins.shape[1]
    both = ("space", "bins")
    f32 = jnp.float32
    bf16 = jnp.bfloat16
    space_at = lax.axis_index("space")
    bins_at = lax.axis_index("bins")

    near_ids = [lax.rem(bins_at + step, bins_count) for step in (bins_count - 1, 1)]
    ids = jnp.stack([bins_at, *near_ids, space_at]).astype(jnp.int32)

    order = (4, 5, 3, 6, 2, 7, 1, 0)
    piece_shape = (CHUNKS, local_bins, LANES)
    sent = call(
        functools.partial(pack_kernel, order),
        [jax.ShapeDtypeStruct(piece_shape, bf16)]
        + [
            pltpu.HBM((CHUNKS - turn % 2, local_bins, LANES), bf16)
            for turn in range(1, bins_count)
        ],
        [in_smem(), in_hbm(), in_hbm()],
        [in_vmem()] + [in_hbm()] * (bins_count - 1),
        [
            VMEM(spectrum.shape, bf16),
            VMEM((2, local_bins * tile_rows, LANES), f32),
            VMEM(stokes_kernel.shape, bf16),
            VMEM((bins_count - 1, *piece_shape), bf16),
            pltpu.SemaphoreType.DMA((4,)),
            pltpu.SemaphoreType.DMA((bins_count, 4)),
        ],
        2_000_000,
        4_000_000,
        (
            ids,
            pltpu.with_memory_space_constraint(spectrum, pltpu.HBM),
            pltpu.with_memory_space_constraint(stokes_kernel, pltpu.HBM),
        ),
    )
    pieces = [sent[0]] * bins_count
    for turn in order[:-1]:
        partners = [(at, at ^ turn) for at in range(bins_count)]
        pieces[turn] = lax.ppermute(sent[turn], "bins", partners)

    surface = call(
        surface_kernel,
        jax.ShapeDtypeStruct((devices, LANES), f32),
        [in_smem()] + [in_vmem()] * 3,
        in_vmem(),
        [VMEM((2 * ROW_GAP, LANES), f32)],
        4_000_000,
        500_000,
        (ids, currents, ocean_wet, group_speed),
    )
    arrived = lax.all_to_all(surface, both, split_axis=0, concat_axis=0, tiled=True)
    map_row = col_map.reshape(1, -1)
    coefs, pair_rows = call(
        pairs_kernel,
        (
            pltpu.HBM((pairs, LANES), f32),
            jax.ShapeDtypeStruct((3 * pairs // LANES, LANES), jnp.int32),
        ),
        [in_vmem()] * 2,
        (in_hbm(), in_vmem()),
        [VMEM((pairs, LANES), f32), pltpu.SemaphoreType.DMA((4,))],
        1_000_000,
        2_500_000,
        (pair_coef.reshape(-1, LANES), pair_bins),
    )
    surface_rows, speed_rows = call(
        tables_kernel,
        (
            jax.ShapeDtypeStruct((32, columns), f32),
            pltpu.HBM((2, bins, LANES), f32),
        ),
        [in_vmem()] * 2,
        (in_vmem(), in_hbm()),
        [VMEM((2, bins, LANES), f32), pltpu.SemaphoreType.DMA((2,))],
        600_000_000,
        1_300_000,
        (arrived.reshape(devices, LANES), map_row),
    )

    halo_shape = (bins_count, 2, local_bins, LANES)
    stokes_shape = (bins_count // 2, local_bins, LANES)
    inner, outer, stokes = call(
        edges_kernel,
        [jax.ShapeDtypeStruct(halo_shape, bf16)] * 2 + [jax.ShapeDtypeStruct(stokes_shape, bf16)],
        [in_vmem()] * bins_count,
        [in_vmem()] * 3,
        [],
        1_000_000,
        2_400_000,
        tuple(pieces),
    )
    outward = [(at, at + 1) for at in range(1, devices - 1, 2)]
    outward += [(at + 1, at) for at, _ in outward]
    outer = lax.ppermute(outer, both, outward)
    within = [(at, at ^ 1) for at in range(devices)]
    inner = lax.ppermute(inner, both, within)
    stokes = lax.ppermute(stokes, both, within)

    routed, near, weights = call(
        functools.partial(drift_kernel, bins_count),
        (
            pltpu.HBM((devices * 8, LANES), bf16),
            jax.ShapeDtypeStruct((16, columns), f32),
            jax.ShapeDtypeStruct((32, bins), bf16),
        ),
        [in_smem()] + [in_vmem()] * (2 + bins_count),
        (in_hbm(), in_vmem(), in_vmem()),
        [
            VMEM((devices * 8, LANES), f32),
            VMEM((bins_count, local_bins, LANES), bf16),
            VMEM((devices * 8, LANES), bf16),
            pltpu.SemaphoreType.DMA((4,)),
        ],
        300_000_000,
        2_500_000,
        (ids, map_row, stokes, *pieces),
    )
    routed = lax.all_to_all(
        routed.reshape(devices, 8, LANES), both, split_axis=0, concat_axis=0, tiled=True
    )
    routed = routed.reshape(devices * 8, LANES)

    new_spectrum = wave_program(
        ids,
        pair_rows.reshape(-1),
        coefs,
        speed_rows,
        inner,
        outer,
        surface_rows,
        near,
        weights,
        wave_wet,
        *pieces,
    )
    new_currents = call(
        ocean_kernel,
        jax.ShapeDtypeStruct(currents.shape, f32),
        [in_vmem()] * 3,
        in_vmem(),
        [VMEM((devices * 8, LANES), f32), VMEM((currents.shape[1], LANES), f32)],
        4_000_000,
        1_500_000,
        (currents, routed, ocean_wet),
    )
    return (jnp.transpose(new_spectrum, (1, 0, 2)), new_currents)


def solution(mesh):
    placed = (
        P("bins", "space", None),
        P(None, "bins"),
        P("bins", None),
        P(),
        P(),
        P(("space", "bins"), None, None),
        P(),
        P("space", None),
        P(("space", "bins"), None),
    )

    return jax.shard_map(
        per_device,
        mesh=mesh,
        in_specs=placed,
        out_specs=(P(None, ("space", "bins"), None), P(("space", "bins"), None, None)),
        check_vma=False,
    )
```
